32 devices in a mesh: patch: 16 (over z, x, core), rep: 2 (over y).
Axes of the slice: x: 2, y: 2, z: 4, core: 2. Of those that a mesh axis runs over, the one named last changes fastest.
Arguments:
- node_state: float32 [2, 4096, 512], P('rep', 'patch'), may hold values from -6 to 6
- noise_embed: float32 [2, 512], replicated, may hold values from -6 to 6
- w_cond: bfloat16 [512, 2048], replicated, may hold values from -0.125 to 0.125
- w_qkv: bfloat16 [512, 1536], replicated, may hold values from -0.25 to 0.25
- w_out: bfloat16 [512, 512], replicated, may hold values from -0.75 to 0.75
- w_up: bfloat16 [512, 2048], replicated, may hold values from -0.25 to 0.25
- w_down: bfloat16 [2048, 512], replicated, may hold values from -0.125 to 0.125
- neighbours: int32 [4096, 16], P('patch'), may hold values from 0 to 319, as said below
- send_rows: int32 [1024], P('patch'), may hold values from 0 to 255, as said below
- valid: int32 [4096], P('patch'), may hold values from 0 to 1, as said below
- cotangent: float32 [2, 4096, 512], P('rep', 'patch'), may hold values from -30 to 30
Outputs:
- out_state: float32 [2, 4096, 512], P('rep', 'patch')
- grad_state: float32 [2, 4096, 512], P('rep', 'patch')
- grad_noise: float32 [2, 512], replicated
- grad_cond: float32 [512, 2048], P('patch')
- grad_qkv: float32 [512, 1536], P('patch')
- grad_out: float32 [512, 512], P('patch')
- grad_up: float32 [512, 2048], P('patch')
- grad_down: float32 [2048, 512], P('patch')
The draws below stay inside these ranges and needn't reach their ends.
Inputs may be any that keep to these rules, and one draw needn't show every extreme that they name: `valid`: in each patch the real nodes fill a prefix of its 256 slots, at least three quarters of them; some patch is full. `send_rows`: entries name real slots of their own patch; the first 32 of a patch lie in the lower half of its real slots, the last 32 in the upper half. `neighbours`: entry j of a node is its own slot for j = 0; every other entry below 256 names a real slot of the patch, and entries from 256 on name the lent rows.
All inputs are finite; a program needn't handle non-finite values.
Results may differ from the reference program's by a relative error of at most 0.014.
Values may be sent and summed in bfloat16 or wider, within the bound.
A program may use at most 128 MiB of HBM per device.

```python
import functools
import math
import jax
import jax.numpy as jnp
from jax import lax

D = 512
HEADS = 4
FF = 2048
K = 16
ND = 256
HALO = 32
BATCH = 2
NODES = 4096


def patch_counts(key):
    patches = NODES // ND
    base_key = jax.random.fold_in(key, 11)
    first_key, second_key, third_key = jax.random.split(base_key, 3)
    counts = ND - jax.random.randint(first_key, (patches,), 0, ND // 4 + 1)
    full_patch = jax.random.randint(second_key, (), 0, patches)
    short_patch = (full_patch + 1 + jax.random.randint(third_key, (), 0, patches - 1)) % patches
    counts = counts.at[short_patch].set(ND - ND // 4).at[full_patch].set(ND)
    return counts.astype(jnp.int32)


def draw_valid(key, part):
    counts = patch_counts(key)
    return (jnp.arange(ND)[None, :] < counts[:, None]).astype(jnp.int32).reshape(NODES)


def draw_send_rows(key, part):
    counts = patch_counts(key)[:, None]
    patches = NODES // ND
    first_key, second_key = jax.random.split(jax.random.fold_in(key, 12))
    lower_rows = jax.random.randint(first_key, (patches, HALO), 0, counts // 2)
    upper_rows = jax.random.randint(second_key, (patches, HALO), counts // 2, counts)
    upper_rows = upper_rows.at[:, HALO - 1].set(counts[:, 0] - 1)
    joined = jnp.concatenate([lower_rows, upper_rows], axis=1).astype(jnp.int32)
    return joined.reshape(2 * HALO * patches)


def draw_neighbours(key, part):
    counts = patch_counts(key)[:, None, None]
    patches = NODES // ND
    first_key, second_key, third_key = jax.random.split(jax.random.fold_in(key, 13), 3)
    local_ids = jax.random.randint(first_key, (patches, ND, K), 0, counts)
    halo_ids = ND + jax.random.randint(second_key, (patches, ND, K), 0, 2 * HALO)
    use_halo = jax.random.randint(third_key, (patches, ND, K), 0, 4) == 0
    chosen = jnp.where(use_halo, halo_ids, local_ids).astype(jnp.int32)
    row_ids = jnp.arange(ND).astype(jnp.int32)
    chosen = chosen.at[:, :, 0].set(row_ids[None, :])
    chosen = chosen.at[:, :, 1].set(ND + row_ids[None, :] % (2 * HALO))
    return chosen.astype(jnp.int32).reshape(NODES, K)


def draw_cotangent(key, part):
    patches = NODES // ND
    first_key = jax.random.fold_in(jax.random.fold_in(key, 14), 0)
    rising = 1.0 + 2.0 * (jnp.arange(NODES) // ND).astype(jnp.float32) / max(patches - 1, 1)
    noise = jax.random.normal(first_key, (BATCH, NODES, D), jnp.float32)
    return noise * rising[None, :, None]


def block_levels(stream_key, dims, pieces, least, top_value):
    def one(axis_at, parts):
        steps = jax.random.uniform(jax.random.fold_in(jax.random.fold_in(stream_key, 6), axis_at), (parts,), jnp.float32, least / len(pieces), top_value / len(pieces))
        return jnp.repeat(jnp.exp(steps), dims[axis_at] // parts).reshape((-1,) + (1,) * (len(dims) - axis_at - 1))

    factor_of = one(*pieces[0])
    for cut in pieces[1:]:
        factor_of = factor_of * one(*cut)
    return factor_of


def gaussian(key, shape, scale, most, shards=(), held_as=jnp.bfloat16):
    level = block_levels(key, shape, shards, -0.22, 0.18) if shards else 1.0
    array = jax.random.normal(key, shape, jnp.float32) * scale * level
    return jnp.minimum(jnp.maximum(array, -most), most).astype(held_as)


def setup_inputs(seed: int = 0) -> dict:
    streams_of = jax.random.split(jax.random.key(seed), 12)
    return {
        "node_state": gaussian(streams_of[0], (BATCH, NODES, D), 1.0, 6.0, ((0, 2), (1, 16)), jnp.float32),
        "noise_embed": gaussian(streams_of[1], (BATCH, D), 1.0, 6.0, (), jnp.float32),
        "w_cond": gaussian(streams_of[2], (D, 4 * D), (4 * D) ** -0.5, 0.125),
        "w_qkv": gaussian(streams_of[3], (D, 3 * D), D ** -0.5, 0.25),
        "w_out": gaussian(streams_of[4], (D, D), (D // 8) ** -0.5, 0.75),
        "w_up": gaussian(streams_of[5], (D, FF), D ** -0.5, 0.25),
        "w_down": gaussian(streams_of[6], (FF, D), FF ** -0.5, 0.125),
        "neighbours": draw_neighbours(jax.random.fold_in(streams_of[11], 71), 0),
        "send_rows": draw_send_rows(jax.random.fold_in(streams_of[11], 71), 0),
        "valid": draw_valid(jax.random.fold_in(streams_of[11], 71), 0),
        "cotangent": draw_cotangent(jax.random.fold_in(streams_of[11], 71), 0),
    }


highest = lax.Precision.HIGHEST

@jax.custom_vjp
def low(v):
    return lax.optimization_barrier(v.astype(jnp.bfloat16)).astype(jnp.float32)

@jax.custom_vjp
def low_back(v):
    return v

def low_keep(v):
    return (low(v), None)

def low_pass(kept, grad):
    return (grad,)

def back_keep(v):
    return (v, None)

def back_low(kept, grad):
    return (low(grad),)
low.defvjp(low_keep, low_pass)
low_back.defvjp(back_keep, back_low)

def layer_norm(values):
    centred = values - lax.optimization_barrier(jnp.mean(values, axis=-1, keepdims=True))
    return centred * lax.rsqrt(lax.optimization_barrier(jnp.mean(centred * centred, axis=-1, keepdims=True)) + 1e-05)

def global_index(neighbours, send_rows):
    patches = NODES // ND
    send_table = send_rows.reshape(patches, 2 * HALO)
    starts = (jnp.arange(patches) * ND).astype(jnp.int32)[:, None]
    own_rows = starts + jnp.arange(ND).astype(jnp.int32)[None, :]
    prev_rows = jnp.roll(send_table, 1, axis=0)[:, HALO:] + jnp.roll(starts, 1, axis=0)
    next_rows = jnp.roll(send_table, -1, axis=0)[:, :HALO] + jnp.roll(starts, -1, axis=0)
    ext_table = jnp.concatenate([own_rows, prev_rows, next_rows], axis=1).astype(jnp.int32)
    local_ids = neighbours.reshape(patches, ND * K).astype(jnp.int32)
    return jnp.take_along_axis(ext_table, local_ids, axis=1).reshape(NODES, K).astype(jnp.int32)

def attend_block(queries, neighbour_ids, key_table, value_table):
    row_count = queries.shape[0]
    head_size = queries.shape[1] // HEADS
    key_rows = key_table[neighbour_ids].reshape(row_count, K, HEADS, head_size)
    value_rows = value_table[neighbour_ids].reshape(row_count, K, HEADS, head_size)
    query_heads = queries.reshape(row_count, HEADS, head_size)
    scores = jnp.einsum('rhd,rkhd->rhk', query_heads, key_rows, precision=highest) * head_size ** (-0.5)
    scores = low_back(scores)
    attn_weights = jax.nn.softmax(scores, axis=-1)
    mixture = jnp.einsum('rhk,rkhd->rhd', low(attn_weights), value_rows, precision=highest)
    return mixture.reshape(row_count, HEADS * head_size)

def sample_forward(states, condition, w_cond, w_qkv, w_out, w_up, w_down, neighbour_index=None, valid_mask=None):
    model_width = states.shape[-1]
    modulation = jnp.dot(condition[None, :], w_cond, precision=highest)[0]
    scale1, shift1, scale2, shift2 = jnp.split(modulation, 4)
    hidden1 = low(layer_norm(states) * (1.0 + scale1) + shift1)
    qkv_rows = low(low_back(jnp.dot(hidden1, low(w_qkv), precision=highest)))
    queries = qkv_rows[:, :model_width]
    key_table = qkv_rows[:, model_width:2 * model_width]
    value_table = qkv_rows[:, 2 * model_width:]
    block_rows = math.gcd(NODES, 4096)
    num_blocks = NODES // block_rows
    checked = jax.checkpoint(attend_block)

    def one_block(block_item):
        return checked(block_item[0], block_item[1], key_table, value_table)
    mixture = lax.map(one_block, (queries.reshape(num_blocks, block_rows, model_width), neighbour_index.reshape(num_blocks, block_rows, K)))
    mixture = low(low_back(mixture.reshape(NODES, model_width)))
    attended = low_back(jnp.dot(mixture, low(w_out), precision=highest))
    middle = states + valid_mask * attended
    hidden2 = low(layer_norm(middle) * (1.0 + scale2) + shift2)
    up_proj = low_back(jnp.dot(hidden2, low(w_up), precision=highest))
    activation = low(jax.nn.silu(up_proj))
    branch = low_back(jnp.dot(activation, low(w_down), precision=highest))
    return middle + valid_mask * branch

def reference(node_state, noise_embed, w_cond, w_qkv, w_out, w_up, w_down, neighbours, send_rows, valid, cotangent):
    neighbour_index = global_index(neighbours, send_rows)
    valid_mask = valid.astype(jnp.float32)[:, None]
    weights = [matrix.astype(jnp.float32) for matrix in (w_cond, w_qkv, w_out, w_up, w_down)]
    forward = functools.partial(sample_forward, neighbour_index=neighbour_index, valid_mask=valid_mask)
    outputs = []
    state_grads = []
    noise_grads = []
    totals = []
    for sample in range(BATCH):
        result, pullback = jax.vjp(forward, node_state[sample], noise_embed[sample], weights[0], weights[1], weights[2], weights[3], weights[4])
        gradients = pullback(cotangent[sample])
        outputs.append(result)
        state_grads.append(gradients[0])
        noise_grads.append(gradients[1])
        if sample == 0:
            totals = list(gradients[2:])
        else:
            totals = [before + after for before, after in zip(totals, gradients[2:])]
    return (jnp.stack(outputs), jnp.stack(state_grads), jnp.stack(noise_grads), totals[0], totals[1], totals[2], totals[3], totals[4])
```

```python
import functools

import jax
import jax.numpy as jnp
from jax import lax
from jax.experimental import pallas as pl
from jax.experimental.pallas import tpu as pltpu
from jax.sharding import PartitionSpec as P

HEADS = 4
GROUP = 16
MESH = pl.DeviceIdType.MESH
F32 = jnp.float32
BF16 = jnp.bfloat16


def dot(a, b):
    return lax.dot_general(a, b, (((1,), (0,)), ((), ())), preferred_element_type=F32)


def dot_nt(a, b):
    return lax.dot_general(a, b, (((1,), (1,)), ((), ())), preferred_element_type=F32)


def dot_tn(a, b):
    return lax.dot_general(a, b, (((0,), (0,)), ((), ())), preferred_element_type=F32)


def split3(v):
    high = v.astype(BF16)
    rest = v - high.astype(F32)
    mid = rest.astype(BF16)
    low = (rest - mid.astype(F32)).astype(BF16)
    return high.astype(F32), mid.astype(F32), low.astype(F32)


def layer_norm(values):
    centred = values - jnp.mean(values, axis=-1, keepdims=True)
    inv_std = lax.rsqrt(jnp.mean(centred * centred, axis=-1, keepdims=True) + 1e-05)
    return centred * inv_std, inv_std


def norm_back(gradient, normed, inv_std):
    first = jnp.mean(gradient, axis=-1, keepdims=True)
    second = jnp.mean(gradient * normed, axis=-1, keepdims=True)
    return (gradient - first - normed * second) * inv_std


class Names:
    pass


def kernel(fold, patches, names, *refs):
    v = Names()
    for name, ref in zip(names, refs):
        setattr(v, name, ref)
    p = lax.axis_index("patch")
    r = lax.axis_index("rep")
    member = p // fold
    lane = lax.rem(p, fold)
    c = lax.rem(member, 2)
    x = lax.rem(member // 2, 2)
    z = member // 4
    finish = fold == 1

    def device(index, rep=r):
        return (index * fold + lane, rep)

    before = (lax.rem(p + patches - 1, patches), r)
    after = (lax.rem(p + 1, patches), r)
    core_peer = device(member + 1 - 2 * c)
    x_peer = device(member + 2 - 4 * x)
    y_peer = (p, 1 - r)

    nodes, width = v.states_hbm.shape[1:]
    tiles = v.w_up_v.shape[0]
    head = width // HEADS
    factor = head ** (-0.5)
    table = v.k_v.shape[0]
    lent = table - nodes

    barrier = pltpu.get_barrier_semaphore()
    others = [device(lax.rem(member + d, GROUP)) for d in range(1, GROUP)] + [y_peer]
    if fold > 1:
        others += [before, after]
    for other in others:
        pl.semaphore_signal(barrier, inc=1, device_id=other, device_id_type=MESH)

    loads = {}

    def load(key, pairs):
        copies = []
        for number, (src, dst) in enumerate(pairs):
            copy = pltpu.make_async_copy(src, dst, v.load_sem.at[len(loads), number])
            copy.start()
            copies.append(copy)
        loads[key] = copies

    def arrive(key):
        for copy in loads[key]:
            copy.wait()

    load("states", [(v.states_hbm.at[0], v.states_v)])
    load("cond1", [(v.w_cond_hbm.at[:, 0 : 2 * width], v.w_cond_v.at[0])])
    load("qkv", [(v.w_qkv_hbm.at[:, t * width : (t + 1) * width], v.w_qkv_v.at[t]) for t in range(3)])
    load("cond2", [(v.w_cond_hbm.at[:, 2 * width : 4 * width], v.w_cond_v.at[1])])
    load("out", [(v.w_out_hbm, v.w_out_v)])
    load("cot", [(v.cot_hbm.at[0], v.cot_v)])
    load("up", [(v.w_up_hbm.at[:, t * width : (t + 1) * width], v.w_up_v.at[t]) for t in range(tiles)])
    load("down", [(v.w_down_hbm.at[t * width : (t + 1) * width, :], v.w_down_v.at[t]) for t in range(tiles)])

    sent = []

    def send(src, dst, target):
        number = len(sent)
        copy = pltpu.make_async_remote_copy(
            src_ref=src,
            dst_ref=dst,
            send_sem=v.send_sem.at[number],
            recv_sem=v.recv_sem.at[number],
            device_id=target,
            device_id_type=MESH,
        )
        copy.start()
        sent.append(copy)
        return copy

    condition = v.noise_v[pl.ds(r, 1), :]
    row = lax.broadcasted_iota(jnp.int32, (16, width), 0)
    high, mid, low = split3(condition)
    stacked = jnp.where(row == 0, high, jnp.where(row == 1, mid, jnp.where(row == 2, low, 0.0))).astype(BF16)
    arrive("states")
    arrive("cond1")
    mod1 = jnp.sum(dot(stacked, v.w_cond_v[0]), axis=0, keepdims=True)
    scale1, shift1 = mod1[:, :width], mod1[:, width:]

    states = v.states_v[...]
    normed1, inv1 = layer_norm(states)
    v.normed1_v[...] = normed1
    hidden1 = (normed1 * (1.0 + scale1) + shift1).astype(BF16)
    v.table_v[0:nodes, :] = hidden1

    pick = (v.send_v[...] == lax.broadcasted_iota(jnp.int32, (lent, nodes), 1)).astype(BF16)
    v.lend_v[...] = dot(pick, hidden1).astype(BF16)
    pl.semaphore_wait(barrier, len(others))
    half = lent // 2
    halo = [
        send(v.lend_v.at[0:half], v.halo_v.at[half:lent], before),
        send(v.lend_v.at[half:lent], v.halo_v.at[0:half], after),
    ]

    arrive("qkv")
    v.q_v[...] = dot(hidden1, v.w_qkv_v[0]).astype(BF16)
    v.k_v[0:nodes, :] = dot(hidden1, v.w_qkv_v[1]).astype(BF16)
    v.v_v[0:nodes, :] = dot(hidden1, v.w_qkv_v[2]).astype(BF16)

    ids = v.neighbours_v[...]
    column = lax.broadcasted_iota(jnp.int32, (nodes, table), 1)
    count = jnp.zeros((nodes, table), F32)
    for j in range(ids.shape[1]):
        count = count + (ids[:, j : j + 1] == column).astype(F32)
    v.count_v[...] = count

    arrive("cond2")
    mod2 = jnp.sum(dot(stacked, v.w_cond_v[1]), axis=0, keepdims=True)
    scale2, shift2 = mod2[:, :width], mod2[:, width:]
    arrive("cot")
    mask = v.valid_v[...]
    d_branch = (mask * v.cot_v[...]).astype(BF16)
    v.d_branch_v[...] = d_branch

    for copy in halo:
        copy.wait()
    rows = v.halo_v[...]
    v.table_v[nodes:table, :] = rows
    v.k_v[nodes:table, :] = dot(rows, v.w_qkv_v[1]).astype(BF16)
    v.v_v[nodes:table, :] = dot(rows, v.w_qkv_v[2]).astype(BF16)

    for h in range(HEADS):
        cols = slice(h * head, (h + 1) * head)
        scores = dot_nt(v.q_v[:, cols], v.k_v[:, cols]) * factor
        times = v.count_v[...]
        scores = jnp.where(times > 0.0, scores, -1e30)
        exponent = times * jnp.exp(scores - jnp.max(scores, axis=-1, keepdims=True))
        attn = exponent / jnp.sum(exponent, axis=-1, keepdims=True)
        v.attn_v[h] = attn
        v.mix_v[:, cols] = dot(attn.astype(BF16), v.v_v[:, cols]).astype(BF16)

    arrive("out")
    middle = v.states_v[...] + mask * dot(v.mix_v[...], v.w_out_v[...])
    v.middle_v[...] = middle
    normed2, inv2 = layer_norm(middle)
    v.normed2_v[...] = normed2
    v.hidden2_v[...] = (normed2 * (1.0 + scale2) + shift2).astype(BF16)

    arrive("up")
    arrive("down")
    core = [[], [], []]

    def core_send(w, zs, ts):
        core[w].append(
            (zs, ts, send(v.grad_v.at[w, zs, :, 1 - c, ts], v.core_v.at[w, zs, :, ts], core_peer))
        )

    every = slice(0, 4)
    for t in range(tiles):
        up = dot(v.hidden2_v[...], v.w_up_v[t])
        sigmoid = 1.0 / (1.0 + jnp.exp(-up))
        activation = (up * sigmoid).astype(BF16)
        d_act = dot_nt(v.d_branch_v[...], v.w_down_v[t])
        d_up = (d_act * sigmoid * (1.0 + up * (1.0 - sigmoid))).astype(BF16)
        v.grad_v[0, t] = dot_tn(activation, v.d_branch_v[...]).astype(BF16).reshape(v.grad_v.shape[2:])
        core_send(0, slice(t, t + 1), every)
        v.grad_v[1, :, :, :, t] = dot_tn(v.hidden2_v[...], d_up).astype(BF16).reshape(4, 2, 2, 32, width)
        core_send(1, every, slice(t, t + 1))
        branch = dot(activation, v.w_down_v[t])
        back = dot_nt(d_up, v.w_up_v[t])
        if t == 0:
            v.out_v[...] = branch
            v.d_hidden2_v[...] = back
        else:
            v.out_v[...] += branch
            v.d_hidden2_v[...] += back

    stores = []

    def store(src, dst):
        copy = pltpu.make_async_copy(src, dst, v.store_sem.at[len(stores)])
        copy.start()
        stores.append(copy)

    v.out_v[...] = v.middle_v[...] + mask * v.out_v[...]
    store(v.out_v, v.out_hbm.at[0])

    d_hidden2 = v.d_hidden2_v[...]
    normed2 = v.normed2_v[...]
    v.mod_v[:, 2 * width : 3 * width] = jnp.sum(d_hidden2 * normed2, axis=0, keepdims=True)
    v.mod_v[:, 3 * width : 4 * width] = jnp.sum(d_hidden2, axis=0, keepdims=True)
    d_middle = v.cot_v[...] + norm_back(d_hidden2 * (1.0 + scale2), normed2, inv2)
    v.middle_v[...] = d_middle
    d_attended = (mask * d_middle).astype(BF16)
    v.grad_v[2, :, :, :, 0] = dot_tn(v.mix_v[...], d_attended).astype(BF16).reshape(4, 2, 2, 32, width)
    core_send(2, every, slice(0, 1))
    v.d_mix_v[...] = dot_nt(d_attended, v.w_out_v[...]).astype(BF16)

    for h in range(HEADS):
        cols = slice(h * head, (h + 1) * head)
        attn = v.attn_v[h]
        d_attn = dot_nt(v.d_mix_v[:, cols], v.v_v[:, cols])
        inner = jnp.sum(attn * d_attn, axis=-1, keepdims=True)
        d_scores = (attn * (d_attn - inner)).astype(BF16)
        v.d_q_v[:, cols] = (dot(d_scores, v.k_v[:, cols]) * factor).astype(BF16)
        v.d_k_v[:, cols] = (dot_tn(d_scores, v.q_v[:, cols]) * factor).astype(BF16)
        v.d_v_v[:, cols] = dot_tn(attn.astype(BF16), v.d_mix_v[:, cols]).astype(BF16)

    parts = [
        (v.table_v[0:nodes, :], v.d_q_v[...]),
        (v.table_v[...], v.d_k_v[...]),
        (v.table_v[...], v.d_v_v[...]),
    ]
    for t, (left, right) in enumerate(parts):
        v.grad_v[2, :, :, :, t + 1] = dot_tn(left, right).astype(BF16).reshape(4, 2, 2, 32, width)
        core_send(2, every, slice(t + 1, t + 2))

    d_table = dot_nt(v.d_k_v[...], v.w_qkv_v[1]) + dot_nt(v.d_v_v[...], v.w_qkv_v[2])
    v.lend_v[...] = d_table[nodes:table, :].astype(BF16)
    back = [
        send(v.lend_v.at[0:half], v.returned_v.at[half:lent], before),
        send(v.lend_v.at[half:lent], v.returned_v.at[0:half], after),
    ]
    v.d_hidden2_v[...] = d_table[0:nodes, :] + dot_nt(v.d_q_v[...], v.w_qkv_v[0])
    for copy in back:
        copy.wait()
    d_hidden1 = v.d_hidden2_v[...] + dot_tn(pick, v.returned_v[...])
    normed1 = v.normed1_v[...]
    v.mod_v[:, 0:width] = jnp.sum(d_hidden1 * normed1, axis=0, keepdims=True)
    v.mod_v[:, width : 2 * width] = jnp.sum(d_hidden1, axis=0, keepdims=True)
    v.d_states_v[...] = v.middle_v[...] + norm_back(d_hidden1 * (1.0 + scale1), normed1, inv1)
    store(v.d_states_v, v.d_states_hbm.at[0])

    v.mods_v[member] = v.mod_v[...]
    mods = [
        send(v.mod_v, v.mods_v.at[member], device(lax.rem(member + d, GROUP))) for d in range(1, GROUP)
    ]

    def core_add(w, zs, ts, copy):
        copy.wait()
        total = v.grad_v[w, zs, :, c, ts] + v.core_v[w, zs, :, ts]
        v.first_v[w, zs, :, ts] = total[..., 0:16, :]
        second = total[..., 16:32, :]
        v.second_v[w, zs, :, ts, 0] = second[..., 0 : width // 2]
        v.second_v[w, zs, :, ts, 1] = second[..., width // 2 :]
        return (
            zs,
            ts,
            send(v.first_v.at[w, zs, 1 - x, ts], v.first_x_v.at[w, zs, ts], x_peer),
            send(v.second_v.at[w, zs, :, ts, 1 - r], v.second_y_v.at[w, zs, :, ts], y_peer),
        )

    def second_x(w, zs, ts, copy):
        copy.wait()
        v.second_y_v[w, zs, :, ts] = v.second_v[w, zs, :, ts, r] + v.second_y_v[w, zs, :, ts]
        return zs, ts, send(v.second_y_v.at[w, zs, 1 - x, ts], v.second_x_v.at[w, zs, ts], x_peer)

    def first_sum(w, zs, ts, copy):
        copy.wait()
        v.first_x_v[w, zs, ts] = v.first_v[w, zs, x, ts] + v.first_x_v[w, zs, ts]

    def second_sum(w, zs, ts, copy):
        copy.wait()
        v.second_x_v[w, zs, ts] = v.second_y_v[w, zs, x, ts] + v.second_x_v[w, zs, ts]

    def along_z(buffer, landing, w, ts):
        copies = []
        for d in range(1, 4):
            there = lax.rem(z + d, 4)
            copies.append(
                send(buffer.at[w, there, ts], landing.at[w, d - 1, ts], device(there * 4 + x * 2 + c))
            )
        return copies

    def z_sum(buffer, landing, w, ts, copies):
        for copy in copies:
            copy.wait()
        total = buffer[w, z, ts].astype(F32)
        for d in range(3):
            total = total + landing[w, d, ts].astype(F32)
        return total.astype(BF16)

    units = {0: [every], 1: [slice(0, 2), slice(2, 4)], 2: [slice(0, 2), slice(2, 4)]}
    started = {w: [core_add(w, *job) for job in core[w]] for w in range(3)}
    middle_jobs = {w: [second_x(w, zs, ts, cy) for zs, ts, _, cy in started[w]] for w in range(3)}
    for w in range(3):
        for zs, ts, cx, _ in started[w]:
            first_sum(w, zs, ts, cx)
    first_z = {w: [(ts, along_z(v.first_x_v, v.first_z_v, w, ts)) for ts in units[w]] for w in range(3)}
    for w in range(3):
        for zs, ts, copy in middle_jobs[w]:
            second_sum(w, zs, ts, copy)
    second_z = {w: [(ts, along_z(v.second_x_v, v.second_z_v, w, ts)) for ts in units[w]] for w in range(3)}
    last_first = {0: [], 1: [], 2: []}
    last_second = {0: [], 1: [], 2: []}
    for w in range(3):
        for ts, copies in first_z[w]:
            v.first_s_v[w, ts] = z_sum(v.first_x_v, v.first_z_v, w, ts, copies)
            last_first[w].append(send(v.first_s_v.at[w, ts], v.first_r_v.at[w, ts], y_peer))
    for w in range(3):
        for ts, copies in second_z[w]:
            v.second_s_v[w, ts] = z_sum(v.second_x_v, v.second_z_v, w, ts, copies)
            last_second[w].append(send(v.second_s_v.at[w, ts], v.second_r_v.at[w, ts], y_peer))

    for copy in mods:
        copy.wait()
    total = v.mods_v[0]
    for d in range(1, GROUP):
        total = total + v.mods_v[d]
    v.rows_v[r] = total
    swap = send(v.rows_v.at[r], v.rows_v.at[r], y_peer)
    swap.wait()
    if finish:
        first_row, second_row = v.rows_v[0], v.rows_v[1]
        row = lax.broadcasted_iota(jnp.int32, (16, 4 * width), 0)
        stacked = jnp.zeros((16, 4 * width), F32)
        for number, piece in enumerate(split3(first_row) + split3(second_row)):
            stacked = jnp.where(row == number, piece, stacked)
        stacked = stacked.astype(BF16)
        noise = dot_nt(stacked[:, 0 : 2 * width], v.w_cond_v[0]) + dot_nt(
            stacked[:, 2 * width :], v.w_cond_v[1]
        )
        v.noise_out[0:1, :] = jnp.sum(noise[0:3], axis=0, keepdims=True)
        v.noise_out[1:2, :] = jnp.sum(noise[3:6], axis=0, keepdims=True)
        v.cond_out[...] = v.cond_cols_v[:, 0:1] * first_row + v.cond_cols_v[:, 1:2] * second_row
    else:
        v.rows_out[0:1, :] = v.rows_v[0]
        v.rows_out[1:2, :] = v.rows_v[1]

    def finals(w):
        for copy in last_first[w] + last_second[w]:
            copy.wait()
        top = v.first_s_v[w].astype(F32) + v.first_r_v[w].astype(F32)
        mine = v.second_s_v[w].astype(F32)
        theirs = v.second_r_v[w].astype(F32)
        left = jnp.where(r == 0, mine, theirs)
        right = jnp.where(r == 0, theirs, mine)
        return top, left, right

    top, left, right = finals(0)
    for t in range(4):
        v.down_out[t * 32 : t * 32 + 16, :] = top[t]
        v.down_out[t * 32 + 16 : t * 32 + 32, 0 : width // 2] = left[t]
        v.down_out[t * 32 + 16 : t * 32 + 32, width // 2 :] = right[t]
    top, left, right = finals(1)
    for t in range(4):
        v.up_out[0:16, t * width : (t + 1) * width] = top[t]
        v.up_out[16:32, t * width : t * width + width // 2] = left[t]
        v.up_out[16:32, t * width + width // 2 : (t + 1) * width] = right[t]
    top, left, right = finals(2)
    for t in range(4):
        ref, base = (v.o_out, 0) if t == 0 else (v.qkv_out, (t - 1) * width)
        ref[0:16, base : base + width] = top[t]
        ref[16:32, base : base + width // 2] = left[t]
        ref[16:32, base + width // 2 : base + width] = right[t]

    for copy in stores:
        copy.wait()


def body(
    node_state,
    noise_embed,
    w_cond,
    w_qkv,
    w_out,
    w_up,
    w_down,
    neighbours,
    send_rows,
    valid,
    cotangent,
):
    nodes, width = node_state.shape[1:]
    hidden = w_up.shape[1]
    lent = send_rows.shape[0]
    table = nodes + lent
    patches = lax.axis_size("patch")
    fold = patches // GROUP
    rows_each = width // patches
    first_row = lax.axis_index("patch") * rows_each
    cond_cols = lax.dynamic_slice_in_dim(noise_embed, first_row, rows_each, 1).T
    block = width // GROUP
    half = width // 2

    hbm = pl.BlockSpec(memory_space=pl.ANY)
    vmem = pl.BlockSpec(memory_space=pltpu.VMEM)
    inputs = [
        ("states_hbm", node_state, hbm),
        ("noise_v", noise_embed, vmem),
        ("w_cond_hbm", w_cond, hbm),
        ("w_qkv_hbm", w_qkv, hbm),
        ("w_out_hbm", w_out, hbm),
        ("w_up_hbm", w_up, hbm),
        ("w_down_hbm", w_down, hbm),
        ("neighbours_v", neighbours, vmem),
        ("send_v", send_rows[:, None], vmem),
        ("valid_v", valid.astype(F32)[:, None], vmem),
        ("cot_hbm", cotangent, hbm),
        ("cond_cols_v", cond_cols, vmem),
    ]
    outputs = [
        ("out_hbm", node_state.shape, hbm),
        ("d_states_hbm", node_state.shape, hbm),
        ("down_out", (hidden // GROUP, width), vmem),
        ("up_out", (block, hidden), vmem),
        ("o_out", (block, width), vmem),
        ("qkv_out", (block, 3 * width), vmem),
    ]
    if fold == 1:
        outputs += [("noise_out", noise_embed.shape, vmem), ("cond_out", (rows_each, 4 * width), vmem)]
    else:
        outputs += [("rows_out", (noise_embed.shape[0], 4 * width), vmem)]
    tiles = hidden // width
    remote = 128
    scratch = [
        ("states_v", (nodes, width), F32),
        ("cot_v", (nodes, width), F32),
        ("w_cond_v", (2, width, 2 * width), BF16),
        ("w_qkv_v", (3, width, width), BF16),
        ("w_out_v", (width, width), BF16),
        ("w_up_v", (tiles, width, width), BF16),
        ("w_down_v", (tiles, width, width), BF16),
        ("normed1_v", (nodes, width), F32),
        ("table_v", (table, width), BF16),
        ("lend_v", (lent, width), BF16),
        ("halo_v", (lent, width), BF16),
        ("returned_v", (lent, width), BF16),
        ("q_v", (nodes, width), BF16),
        ("k_v", (table, width), BF16),
        ("v_v", (table, width), BF16),
        ("count_v", (nodes, table), F32),
        ("attn_v", (HEADS, nodes, table), F32),
        ("mix_v", (nodes, width), BF16),
        ("middle_v", (nodes, width), F32),
        ("normed2_v", (nodes, width), F32),
        ("hidden2_v", (nodes, width), BF16),
        ("d_branch_v", (nodes, width), BF16),
        ("out_v", (nodes, width), F32),
        ("d_hidden2_v", (nodes, width), F32),
        ("d_mix_v", (nodes, width), BF16),
        ("d_q_v", (nodes, width), BF16),
        ("d_k_v", (table, width), BF16),
        ("d_v_v", (table, width), BF16),
        ("d_states_v", (nodes, width), F32),
        ("mod_v", (1, 4 * width), F32),
        ("mods_v", (GROUP, 1, 4 * width), F32),
        ("rows_v", (2, 1, 4 * width), F32),
        ("grad_v", (3, 4, 2, 2, 4, 32, width), BF16),
        ("core_v", (3, 4, 2, 4, 32, width), BF16),
        ("first_v", (3, 4, 2, 4, 16, width), BF16),
        ("second_v", (3, 4, 2, 4, 2, 16, half), BF16),
        ("first_x_v", (3, 4, 4, 16, width), BF16),
        ("second_y_v", (3, 4, 2, 4, 16, half), BF16),
        ("second_x_v", (3, 4, 4, 16, half), BF16),
        ("first_z_v", (3, 3, 4, 16, width), BF16),
        ("second_z_v", (3, 3, 4, 16, half), BF16),
        ("first_s_v", (3, 4, 16, width), BF16),
        ("first_r_v", (3, 4, 16, width), BF16),
        ("second_s_v", (3, 4, 16, half), BF16),
        ("second_r_v", (3, 4, 16, half), BF16),
    ]
    semaphores = [
        ("load_sem", pltpu.SemaphoreType.DMA((8, 4))),
        ("store_sem", pltpu.SemaphoreType.DMA((2,))),
        ("send_sem", pltpu.SemaphoreType.DMA((remote,))),
        ("recv_sem", pltpu.SemaphoreType.DMA((remote,))),
    ]
    names = [n for group in (inputs, outputs, scratch, semaphores) for n in [e[0] for e in group]]
    results = pl.pallas_call(
        functools.partial(kernel, fold, patches, names),
        out_shape=[jax.ShapeDtypeStruct(shape, F32) for _, shape, _ in outputs],
        in_specs=[spec for _, _, spec in inputs],
        out_specs=[spec for _, _, spec in outputs],
        scratch_shapes=[pltpu.VMEM(shape, dtype) for _, shape, dtype in scratch]
        + [sem for _, sem in semaphores],
        compiler_params=pltpu.CompilerParams(
            collective_id=0, has_side_effects=True, vmem_limit_bytes=56 * 1024 * 1024
        ),
    )(*[array for _, array, _ in inputs])
    output, d_state, g_down, g_up, g_out, g_qkv = results[:6]
    if fold == 1:
        grad_noise, grad_cond = results[6:]
    else:
        groups = [[m * fold + i for i in range(fold)] for m in range(GROUP)]

        def rest(array):
            return lax.psum_scatter(
                array, "patch", scatter_dimension=0, axis_index_groups=groups, tiled=True
            )

        g_down, g_up, g_out, g_qkv = rest(g_down), rest(g_up), rest(g_out), rest(g_qkv)
        mods = lax.psum(results[6], "patch") / GROUP
        highest = lax.Precision.HIGHEST
        grad_noise = jnp.dot(mods, w_cond.astype(F32).T, precision=highest)
        grad_cond = jnp.dot(cond_cols, mods, precision=highest)
    return output, d_state, grad_noise, grad_cond, g_qkv, g_out, g_up, g_down


def solution(mesh):
    in_specs = (
        P("rep", "patch", None),
        P(),
        P(),
        P(),
        P(),
        P(),
        P(),
        P("patch", None),
        P("patch"),
        P("patch"),
        P("rep", "patch", None),
    )
    out_specs = (
        P("rep", "patch", None),
        P("rep", "patch", None),
        P(),
        P("patch", None),
        P("patch", None),
        P("patch", None),
        P("patch", None),
        P("patch", None),
    )
    return jax.shard_map(body, mesh=mesh, in_specs=in_specs, out_specs=out_specs, check_vma=False)
```

```python
import functools

import jax
import jax.numpy as jnp
from jax import lax
from jax.experimental import pallas as pl
from jax.experimental.pallas import tpu as pltpu
from jax.sharding import PartitionSpec as P

HEADS = 4
GROUP = 16
FLOWS = ("Bd", "A", "C", "C", "A", "B", "Cd", "A", "C", "Cd", "Cd", "A")
ORDER = (
    "up", ("gd", 0), ("gd", 1), ("gu", 0), ("gu", 1), ("gu", 2), ("gu", 3), 0, "out", 1, 2, 3, 4, 5,
    "mid", 6, 7, "go", ("attn", 0), ("attn", 1), 1, 2, ("attn", 2), 8, ("attn", 3), ("gq", 0),
    ("gq", 1), 4, 0, 3, ("gq", 2), "table", 9, 10, 7, 11, 6, 5, "state", 2, 0, 1, 8, 3, 4, 9, 11, 5,
    7, 6, 2, "mods", 1, 10, 3, 8, 0, 4, 9, 11, 5, "cond", 7, 1, 2, 10, 3, 4, 6, 8, 5, 7, 11, 2, 3,
    9, 6, 8, 10, 11, 9, 8, 10,
)
MESH = pl.DeviceIdType.MESH
F32 = jnp.float32
BF16 = jnp.bfloat16


def dot(a, b):
    return lax.dot_general(a, b, (((1,), (0,)), ((), ())), preferred_element_type=F32)


def dot_nt(a, b):
    return lax.dot_general(a, b, (((1,), (1,)), ((), ())), preferred_element_type=F32)


def dot_tn(a, b):
    return lax.dot_general(a, b, (((0,), (0,)), ((), ())), preferred_element_type=F32)


def split3(v):
    high = v.astype(BF16)
    rest = v - high.astype(F32)
    mid = rest.astype(BF16)
    low = (rest - mid.astype(F32)).astype(BF16)
    return high.astype(F32), mid.astype(F32), low.astype(F32)


def layer_norm(values):
    centred = values - jnp.mean(values, axis=-1, keepdims=True)
    inv_std = lax.rsqrt(jnp.mean(centred * centred, axis=-1, keepdims=True) + 1e-05)
    return centred * inv_std, inv_std


def norm_back(gradient, normed, inv_std):
    first = jnp.mean(gradient, axis=-1, keepdims=True)
    second = jnp.mean(gradient * normed, axis=-1, keepdims=True)
    return (gradient - first - normed * second) * inv_std


class Names:
    pass


class Message:
    def __init__(self, v, number, src, dst, target, receive=None):
        self.parts = dict(
            src_ref=src,
            dst_ref=dst,
            send_sem=v.send_sem.at[number],
            recv_sem=v.recv_sem.at[number if receive is None else receive],
            device_id=target,
            device_id_type=MESH,
        )

    def start(self):
        pltpu.make_async_remote_copy(**self.parts).start()

    def arrive(self):
        pltpu.make_async_remote_copy(**self.parts).wait_recv()

    def leave(self):
        pltpu.make_async_remote_copy(**self.parts).wait_send()


def kernel(fold, patches, names, *refs):
    v = Names()
    for name, ref in zip(names, refs):
        setattr(v, name, ref)
    p = lax.axis_index("patch")
    r = lax.axis_index("rep")
    member = p // fold
    lane = lax.rem(p, fold)
    c = lax.rem(member, 2)
    x = lax.rem(member // 2, 2)
    z = member // 4
    finish = fold == 1

    def device(index, rep=r):
        return (index * fold + lane, rep)

    before = (lax.rem(p + patches - 1, patches), r)
    after = (lax.rem(p + 1, patches), r)
    core_peer = device(member + 1 - 2 * c)
    x_peer = device(member + 2 - 4 * x)
    y_peer = (p, 1 - r)

    def z_peer(there):
        return device(there * 4 + x * 2 + c)

    nodes, width = v.states_hbm.shape[1:]
    tiles = v.w_up_v.shape[0]
    head = width // HEADS
    factor = head ** (-0.5)
    table = v.k_v.shape[0]
    lent = table - nodes
    half = lent // 2

    barrier = pltpu.get_barrier_semaphore()
    others = [device(lax.rem(member + d, GROUP)) for d in range(1, GROUP)] + [y_peer]
    if fold > 1:
        others += [before, after]
    for other in others:
        pl.semaphore_signal(barrier, inc=1, device_id=other, device_id_type=MESH)

    stores = []

    def store(src, dst):
        copy = pltpu.make_async_copy(src, dst, v.store_sem.at[len(stores)])
        copy.start()
        stores.append(copy)

    loads = {}

    def load(key, pairs):
        copies = []
        for number, (src, dst) in enumerate(pairs):
            copy = pltpu.make_async_copy(src, dst, v.load_sem.at[len(loads), number])
            copy.start()
            copies.append(copy)
        loads[key] = copies

    def arrive(key):
        for copy in loads[key]:
            copy.wait()

    def columns(ref, t):
        return ref.at[:, t * width : (t + 1) * width]

    load("states", [(v.states_hbm.at[0], v.states_v), (v.noise_hbm, v.noise_v), (v.send_hbm, v.pick_v)])
    load("cond1", [(v.w_cond_hbm.at[:, 0 : 2 * width], v.w_cond_v.at[0])])
    load("qkv", [(columns(v.w_qkv_hbm, t), v.w_qkv_v.at[t]) for t in range(3)])
    load("index", [(v.neighbours_hbm, v.neighbours_v), (v.valid_hbm, v.valid_v)])
    load("cond2", [(v.w_cond_hbm.at[:, 2 * width : 4 * width], v.w_cond_v.at[1])])
    load("cot", [(v.cot_hbm.at[0], v.cot_v)])
    load("down", [(v.w_down_hbm.at[t * width : (t + 1) * width, :], v.w_down_v.at[t]) for t in range(tiles)])
    load("out", [(v.w_out_hbm, v.w_out_v)])
    load("up", [(columns(v.w_up_hbm, t), v.w_up_v.at[t]) for t in range(tiles)])

    numbers = []
    leaving = []

    def message(src, dst, target, receive=None):
        numbers.append(None)
        return Message(v, len(numbers) - 1, src, dst, target, receive)

    def send(src, dst, target):
        copy = message(src, dst, target)
        copy.start()
        leaving.append(copy)
        return copy

    arrive("states")
    condition = v.noise_v[pl.ds(r, 1), :]
    row = lax.broadcasted_iota(jnp.int32, (16, width), 0)
    high, mid, low = split3(condition)
    stacked = jnp.where(row == 0, high, jnp.where(row == 1, mid, jnp.where(row == 2, low, 0.0))).astype(BF16)
    arrive("cond1")
    mod1 = jnp.sum(dot(stacked, v.w_cond_v[0]), axis=0, keepdims=True)
    scale1, shift1 = mod1[:, :width], mod1[:, width:]

    states = v.states_v[...]
    normed1, inv1 = layer_norm(states)
    v.normed1_v[...] = normed1
    hidden1 = (normed1 * (1.0 + scale1) + shift1).astype(BF16)
    v.table_v[0:nodes, :] = hidden1

    pick = (v.pick_v[...] == lax.broadcasted_iota(jnp.int32, (nodes, lent), 0)).astype(BF16)
    v.lend_v[...] = dot_tn(pick, hidden1).astype(BF16)
    pl.semaphore_wait(barrier, len(others))
    halo = [
        send(v.lend_v.at[0:half], v.halo_v.at[half:lent], before),
        send(v.lend_v.at[half:lent], v.halo_v.at[0:half], after),
    ]

    arrive("qkv")
    v.k_v[0:nodes, :] = dot(hidden1, v.w_qkv_v[1]).astype(BF16)
    v.v_v[0:nodes, :] = dot(hidden1, v.w_qkv_v[2]).astype(BF16)
    v.q_v[...] = dot(hidden1, v.w_qkv_v[0]).astype(BF16)

    arrive("index")
    entry = lax.broadcasted_iota(jnp.int32, (table, nodes), 0)
    count = jnp.zeros((table, nodes), F32)
    for j in range(v.neighbours_v.shape[0]):
        count = count + (v.neighbours_v[j : j + 1, :] == entry).astype(F32)
    v.count_v[...] = count

    arrive("cond2")
    mod2 = jnp.sum(dot(stacked, v.w_cond_v[1]), axis=0, keepdims=True)
    scale2, shift2 = mod2[:, :width], mod2[:, width:]
    arrive("cot")
    real = jnp.sum(v.valid_v[...], axis=1, keepdims=True)
    mask = (lax.broadcasted_iota(jnp.int32, (nodes, 1), 0) < real).astype(F32)
    v.d_branch_v[...] = (mask * v.cot_v[...]).astype(BF16)
    arrive("down")
    for t in range(tiles):
        v.d_act_v[t] = dot_nt(v.d_branch_v[...], v.w_down_v[t])

    for copy in halo:
        copy.arrive()
    rows = v.halo_v[...]
    v.table_v[nodes:table, :] = rows
    v.k_v[nodes:table, :] = dot(rows, v.w_qkv_v[1]).astype(BF16)
    v.v_v[nodes:table, :] = dot(rows, v.w_qkv_v[2]).astype(BF16)

    for h in range(HEADS):
        cols = slice(h * head, (h + 1) * head)
        scores = dot_nt(v.k_v[:, cols], v.q_v[:, cols]) * factor
        times = v.count_v[...]
        scores = jnp.where(times > 0.0, scores, -1e30)
        exponent = times * jnp.exp(scores - jnp.max(scores, axis=0, keepdims=True))
        attn = exponent * (1.0 / jnp.sum(exponent, axis=0, keepdims=True))
        v.attn_v[h] = attn
        v.mix_v[:, cols] = dot_tn(attn.astype(BF16), v.v_v[:, cols]).astype(BF16)

    arrive("out")
    middle = v.states_v[...] + mask * dot(v.mix_v[...], v.w_out_v[...])
    v.middle_v[...] = middle
    normed2, inv2 = layer_norm(middle)
    v.normed2_v[...] = normed2
    v.hidden2_v[...] = (normed2 * (1.0 + scale2) + shift2).astype(BF16)

    def exchange_z(own, name):
        triple, single, middle_in, comb = (
            getattr(v, name + "_triple"),
            getattr(v, name + "_single"),
            getattr(v, name + "_middle"),
            getattr(v, name + "_comb"),
        )
        outer = (z == 0) | (z == 3)
        outer_z = jnp.where(z < 2, 0, 3)
        other_inner = jnp.where(z < 2, 2, 1)
        other_outer = 3 - outer_z
        near_inner = jnp.where(z < 2, 1, 2)
        first = jnp.where(z == 0, 1, 0)
        offset = jnp.where(z == 1, 1, 0)
        to_inner = message(own.at[pl.ds(first, 3)], triple, z_peer(near_inner))
        to_outer = message(own.at[outer_z], single, z_peer(outer_z))
        across = message(comb.at[0], middle_in, z_peer(other_inner))
        beyond = message(comb.at[1], middle_in, z_peer(other_outer), len(numbers) - 1)

        def begin():
            @pl.when(outer)
            def _():
                to_inner.start()

            @pl.when(jnp.logical_not(outer))
            def _():
                to_outer.start()

        def combine():
            @pl.when(jnp.logical_not(outer))
            def _():
                to_inner.arrive()
                comb[1] = own[other_outer] + triple[other_outer - offset]
                beyond.start()
                comb[0] = own[other_inner] + triple[other_inner - offset]
                across.start()

        def finish_sum(result):
            across.arrive()

            @pl.when(outer)
            def _():
                to_outer.arrive()
                total = own[z].astype(F32) + single[...].astype(F32) + middle_in[...].astype(F32)
                result[...] = total.astype(BF16)

            @pl.when(jnp.logical_not(outer))
            def _():
                total = own[z].astype(F32) + triple[z - offset].astype(F32) + middle_in[...].astype(F32)
                result[...] = total.astype(BF16)

        def leave():
            @pl.when(outer)
            def _():
                to_inner.leave()

            @pl.when(jnp.logical_not(outer))
            def _():
                to_outer.leave()
                across.leave()
                beyond.leave()

        endings.append(leave)
        return begin, combine, finish_sum

    def direct_z(own, name):
        landing = getattr(v, name + "_landing")
        copies = []

        def begin():
            for d in range(1, 4):
                there = lax.rem(z + d, 4)
                copies.append(send(own.at[there], landing.at[d - 1], z_peer(there)))

        def finish_sum(result):
            for copy in copies:
                copy.arrive()
            total = own[z].astype(F32)
            for d in range(3):
                total = total + landing[d].astype(F32)
            result[...] = total.astype(BF16)

        return begin, finish_sum

    endings = []
    queue = {}
    core_copies = {}

    def place(n, value, part=None):
        w, t = n // 4, n % 4
        rows = value.shape[0]
        first = 0 if part is None else pl.multiple_of(part * rows, rows)
        if w == 0:
            for b in range(4):
                start = b * 32 if part is None else pl.multiple_of(b * 32 + part * rows, rows)
                v.down_s[pl.ds(start, rows), t * 128 : (t + 1) * 128] = value[:, b * 128 : (b + 1) * 128]
        else:
            ref = v.up_s if w == 1 else v.last_s
            ref[pl.ds(first, rows), t * width : (t + 1) * width] = value

    def unit_steps(n):
        name, flow = "u%d" % n, FLOWS[n]
        grad, landed, mine = v.grad_v.at[n], v.core_v.at[n], getattr(v, name + "_mine")
        result, received = getattr(v, name + "_result"), getattr(v, name + "_received")
        direct = flow[1:] == "d"
        copies = {}

        def core_sum():
            core_copies[n].arrive()
            total = grad[:, :, c] + landed[...]
            mine[...] = total.reshape(mine.shape)

        def y_exchange():
            copies["last"] = send(result, received, y_peer)

        def ending():
            copies["last"].arrive()
            if flow[0] == "C":
                place(n, result[...].astype(F32), r)
                place(n, received[...].astype(F32), 1 - r)
            else:
                place(n, result[...].astype(F32) + received[...].astype(F32))

        def reduce_z(own, then):
            if direct:
                begin, finish_sum = direct_z(own, name)
                middle_steps = []
            else:
                begin, combine, finish_sum = exchange_z(own, name)
                middle_steps = [combine]

            def last():
                finish_sum(then[0])
                then[1]()

            return begin, middle_steps + [last]

        if flow[0] == "A":
            from_x = getattr(v, name + "_x")
            begin, rest = reduce_z(from_x, (result, y_exchange))

            def start():
                core_sum()
                copies["x"] = send(mine.at[:, 1 - x], from_x, x_peer)

            def second():
                copies["x"].arrive()
                from_x[...] = mine[:, x] + from_x[...]
                begin()

            return [start, second] + rest + [ending]
        if flow[0] == "C":
            from_y, from_x = getattr(v, name + "_y"), getattr(v, name + "_x")
            begin, rest = reduce_z(from_x, (result, y_exchange))

            def start():
                core_sum()
                copies["y"] = send(mine.at[:, :, 1 - r], from_y, y_peer)

            def second():
                copies["y"].arrive()
                from_y[...] = mine[:, :, r] + from_y[...]
                copies["x"] = send(from_y.at[:, 1 - x], from_x, x_peer)

            def third():
                copies["x"].arrive()
                from_x[...] = from_y[:, x] + from_x[...]
                begin()

            return [start, second, third] + rest + [ending]
        pair, from_x = getattr(v, name + "_pair"), getattr(v, name + "_x")

        def x_exchange():
            copies["x"] = send(pair.at[1 - x], from_x, x_peer)

        begin, rest = reduce_z(mine, (pair, x_exchange))

        def start():
            core_sum()
            begin()

        def after_x():
            copies["x"].arrive()
            result[...] = pair[x] + from_x[...]
            y_exchange()

        return [start] + rest + [after_x, ending]

    def produce(n, value):
        v.grad_v[n] = value.reshape(v.grad_v.shape[1:])
        core_copies[n] = send(v.grad_v.at[n, :, :, 1 - c], v.core_v.at[n], core_peer)
        queue[n] = unit_steps(n)

    def section_up():
        arrive("up")
        for t in range(tiles):
            cols = slice(t * width, (t + 1) * width)
            up = dot(v.hidden2_v[...], v.w_up_v[t])
            sigmoid = 1.0 / (1.0 + jnp.exp(-up))
            v.activation_v[:, cols] = (up * sigmoid).astype(BF16)
            v.d_up_v[:, cols] = (v.d_act_v[t] * sigmoid * (1.0 + up * (1.0 - sigmoid))).astype(BF16)

    def section_gd(h):
        value = dot_tn(v.activation_v[...], v.d_branch_v[:, h * 256 : (h + 1) * 256]).astype(BF16)
        value = value.reshape(GROUP, 4, 32, 256)
        for k in range(2):
            blocks = [value[:, b, :, k * 128 : (k + 1) * 128] for b in range(4)]
            produce(2 * h + k, jnp.concatenate(blocks, axis=-1))

    def section_gu(t):
        produce(4 + t, dot_tn(v.hidden2_v[...], v.d_up_v[:, t * width : (t + 1) * width]).astype(BF16))

    def section_out():
        branch = dot(v.activation_v[:, 0:width], v.w_down_v[0])
        for t in range(1, tiles):
            branch = branch + dot(v.activation_v[:, t * width : (t + 1) * width], v.w_down_v[t])
        v.out_v[...] = v.middle_v[...] + mask * branch
        store(v.out_v, v.out_hbm.at[0])

    def section_mid():
        d_hidden2 = dot_nt(v.d_up_v[:, 0:width], v.w_up_v[0])
        for t in range(1, tiles):
            d_hidden2 = d_hidden2 + dot_nt(v.d_up_v[:, t * width : (t + 1) * width], v.w_up_v[t])
        normed2 = v.normed2_v[...]
        v.mod_v[:, 2 * width : 3 * width] = jnp.sum(d_hidden2 * normed2, axis=0, keepdims=True)
        v.mod_v[:, 3 * width : 4 * width] = jnp.sum(d_hidden2, axis=0, keepdims=True)
        d_middle = v.cot_v[...] + norm_back(d_hidden2 * (1.0 + scale2), normed2, inv2)
        v.d_middle_v[...] = d_middle
        v.d_attended_v[...] = (mask * d_middle).astype(BF16)
        v.d_mix_v[...] = dot_nt(v.d_attended_v[...], v.w_out_v[...]).astype(BF16)

    def section_go():
        produce(8, dot_tn(v.mix_v[...], v.d_attended_v[...]).astype(BF16))

    def section_attn(h):
        cols = slice(h * head, (h + 1) * head)
        attn = v.attn_v[h]
        d_attn = dot_nt(v.v_v[:, cols], v.d_mix_v[:, cols])
        inner = jnp.sum(attn * d_attn, axis=0, keepdims=True)
        d_scores = (attn * (d_attn - inner)).astype(BF16)
        v.d_q_v[:, cols] = (dot_tn(d_scores, v.k_v[:, cols]) * factor).astype(BF16)
        v.d_k_v[:, cols] = (dot(d_scores, v.q_v[:, cols]) * factor).astype(BF16)
        v.d_v_v[:, cols] = dot(attn.astype(BF16), v.d_mix_v[:, cols]).astype(BF16)

    def section_gq(t):
        left = v.table_v[0:nodes, :] if t == 0 else v.table_v[...]
        right = (v.d_q_v, v.d_k_v, v.d_v_v)[t][...]
        produce(9 + t, dot_tn(left, right).astype(BF16))

    back = []
    mods = []
    swap = []

    def section_table():
        d_table = dot_nt(v.d_k_v[...], v.w_qkv_v[1]) + dot_nt(v.d_v_v[...], v.w_qkv_v[2])
        v.lend_back_v[...] = d_table[nodes:table, :].astype(BF16)
        back.append(send(v.lend_back_v.at[0:half], v.returned_v.at[half:lent], before))
        back.append(send(v.lend_back_v.at[half:lent], v.returned_v.at[0:half], after))
        v.d_hidden1_v[...] = d_table[0:nodes, :] + dot_nt(v.d_q_v[...], v.w_qkv_v[0])

    def section_state():
        for copy in back:
            copy.arrive()
        d_hidden1 = v.d_hidden1_v[...] + dot(pick, v.returned_v[...])
        normed1 = v.normed1_v[...]
        v.mod_v[:, 0:width] = jnp.sum(d_hidden1 * normed1, axis=0, keepdims=True)
        v.mod_v[:, width : 2 * width] = jnp.sum(d_hidden1, axis=0, keepdims=True)
        v.mods_v[member] = v.mod_v[...]
        for d in range(1, GROUP):
            mods.append(send(v.mod_v, v.mods_v.at[member], device(lax.rem(member + d, GROUP))))
        v.d_states_v[...] = v.d_middle_v[...] + norm_back(d_hidden1 * (1.0 + scale1), normed1, inv1)
        store(v.d_states_v, v.d_states_hbm.at[0])

    def section_mods():
        for copy in mods:
            copy.arrive()
        total = v.mods_v[0]
        for d in range(1, GROUP):
            total = total + v.mods_v[d]
        v.rows_v[r] = total
        swap.append(send(v.rows_v.at[r], v.rows_v.at[r], y_peer))

    def section_cond():
        swap[0].arrive()
        if finish:
            first_row, second_row = v.rows_v[0], v.rows_v[1]
            row = lax.broadcasted_iota(jnp.int32, (16, 4 * width), 0)
            stacked = jnp.zeros((16, 4 * width), F32)
            for number, piece in enumerate(split3(first_row) + split3(second_row)):
                stacked = jnp.where(row == number, piece, stacked)
            stacked = stacked.astype(BF16)
            noise = dot_nt(stacked[:, 0 : 2 * width], v.w_cond_v[0]) + dot_nt(
                stacked[:, 2 * width :], v.w_cond_v[1]
            )
            v.noise_s[0:1, :] = jnp.sum(noise[0:3], axis=0, keepdims=True)
            v.noise_s[1:2, :] = jnp.sum(noise[3:6], axis=0, keepdims=True)
            store(v.noise_s, v.noise_out)
            shape = (v.cond_s.shape[0], width)
            here = lax.broadcasted_iota(jnp.int32, shape, 1) == (
                lax.broadcasted_iota(jnp.int32, shape, 0) + p * shape[0]
            )
            picked = [
                jnp.sum(jnp.where(here, v.noise_v[b : b + 1, :], 0.0), axis=1, keepdims=True)
                for b in range(2)
            ]
            v.cond_s[...] = picked[0] * first_row + picked[1] * second_row
            store(v.cond_s, v.cond_out)
        else:
            v.noise_s[0:1, :] = v.rows_v[0]
            v.noise_s[1:2, :] = v.rows_v[1]
            store(v.noise_s, v.noise_out)

    sections = {
        "up": section_up,
        "gd": section_gd,
        "gu": section_gu,
        "out": section_out,
        "mid": section_mid,
        "go": section_go,
        "attn": section_attn,
        "gq": section_gq,
        "table": section_table,
        "state": section_state,
        "mods": section_mods,
        "cond": section_cond,
    }
    for entry in ORDER:
        if isinstance(entry, int):
            queue[entry].pop(0)()
        elif isinstance(entry, tuple):
            sections[entry[0]](entry[1])
        else:
            sections[entry]()
    for n in range(12):
        for step in queue[n]:
            step()

    store(v.down_s, v.down_out)
    store(v.up_s, v.up_out)
    store(v.last_s.at[:, 0:width], v.o_out)
    store(v.last_s.at[:, width : 4 * width], v.qkv_out)
    for copy in leaving:
        copy.leave()
    for ending in endings:
        ending()
    for copy in stores:
        copy.wait()


def copy_out(count, *refs):
    copies = [
        pltpu.make_async_copy(refs[n], refs[count + n], refs[-1].at[n]) for n in range(count)
    ]
    for copy in copies:
        copy.start()
    for copy in copies:
        copy.wait()


def body(
    node_state,
    noise_embed,
    w_cond,
    w_qkv,
    w_out,
    w_up,
    w_down,
    neighbours,
    send_rows,
    valid,
    cotangent,
):
    nodes, width = node_state.shape[1:]
    hidden = w_up.shape[1]
    lent = send_rows.shape[0]
    table = nodes + lent
    patches = lax.axis_size("patch")
    fold = patches // GROUP
    rows_each = width // patches
    block = width // GROUP
    half = width // 2

    hbm = pl.BlockSpec(memory_space=pl.ANY)
    inputs = [
        ("states_hbm", node_state, hbm),
        ("noise_hbm", noise_embed, hbm),
        ("w_cond_hbm", w_cond, hbm),
        ("w_qkv_hbm", w_qkv, hbm),
        ("w_out_hbm", w_out, hbm),
        ("w_up_hbm", w_up, hbm),
        ("w_down_hbm", w_down, hbm),
        ("neighbours_hbm", neighbours.T, hbm),
        ("send_hbm", send_rows[None, :], hbm),
        ("valid_hbm", valid[None, :], hbm),
        ("cot_hbm", cotangent, hbm),
    ]
    outputs = [
        ("out_hbm", node_state.shape, hbm),
        ("d_states_hbm", node_state.shape, hbm),
        ("down_out", (hidden // GROUP, width), hbm),
        ("up_out", (block, hidden), hbm),
        ("o_out", (block, width), hbm),
        ("qkv_out", (block, 3 * width), hbm),
    ]
    if fold == 1:
        outputs += [("noise_out", noise_embed.shape, hbm), ("cond_out", (rows_each, 4 * width), hbm)]
    else:
        outputs += [("noise_out", (noise_embed.shape[0], 4 * width), hbm)]
    tiles = hidden // width
    remote = 160
    scratch = [
        ("noise_v", noise_embed.shape, F32),
        ("neighbours_v", neighbours.shape[::-1], jnp.int32),
        ("pick_v", (1, lent), jnp.int32),
        ("valid_v", (1, nodes), jnp.int32),
        ("states_v", (nodes, width), F32),
        ("cot_v", (nodes, width), F32),
        ("w_cond_v", (2, width, 2 * width), BF16),
        ("w_qkv_v", (3, width, width), BF16),
        ("w_out_v", (width, width), BF16),
        ("w_up_v", (tiles, width, width), BF16),
        ("w_down_v", (tiles, width, width), BF16),
        ("normed1_v", (nodes, width), F32),
        ("table_v", (table, width), BF16),
        ("lend_v", (lent, width), BF16),
        ("halo_v", (lent, width), BF16),
        ("returned_v", (lent, width), BF16),
        ("q_v", (nodes, width), BF16),
        ("k_v", (table, width), BF16),
        ("v_v", (table, width), BF16),
        ("count_v", (table, nodes), F32),
        ("attn_v", (HEADS, table, nodes), F32),
        ("mix_v", (nodes, width), BF16),
        ("middle_v", (nodes, width), F32),
        ("normed2_v", (nodes, width), F32),
        ("hidden2_v", (nodes, width), BF16),
        ("d_branch_v", (nodes, width), BF16),
        ("out_v", (nodes, width), F32),
        ("d_mix_v", (nodes, width), BF16),
        ("d_q_v", (nodes, width), BF16),
        ("d_k_v", (table, width), BF16),
        ("d_v_v", (table, width), BF16),
        ("d_states_v", (nodes, width), F32),
        ("down_s", (hidden // GROUP, width), F32),
        ("up_s", (block, hidden), F32),
        ("last_s", (block, 4 * width), F32),
        ("noise_s", outputs[6][1], F32),
        ("cond_s", (rows_each, 4 * width), F32),
        ("mod_v", (1, 4 * width), F32),
        ("mods_v", (GROUP, 1, 4 * width), F32),
        ("rows_v", (2, 1, 4 * width), F32),
        ("d_act_v", (tiles, nodes, width), F32),
        ("activation_v", (nodes, hidden), BF16),
        ("d_up_v", (nodes, hidden), BF16),
        ("d_middle_v", (nodes, width), F32),
        ("d_attended_v", (nodes, width), BF16),
        ("d_hidden1_v", (nodes, width), F32),
        ("lend_back_v", (lent, width), BF16),
        ("grad_v", (12, 4, 2, 2, 32, width), BF16),
        ("core_v", (12, 4, 2, 32, width), BF16),
    ]
    for n, flow in enumerate(FLOWS):
        name = "u%d" % n
        rows = 16 if flow[0] == "C" else 32
        part = (2, 32, width) if flow[0] == "B" else (rows, width)
        buffers = [("_mine", (4, 2, 2, 16, width) if flow[0] == "C" else (4, 2, 32, width))]
        buffers += [("_result", (rows, width)), ("_received", (rows, width))]
        buffers += [("_x", (rows, width) if flow[0] == "B" else (4, rows, width))]
        if flow[0] == "C":
            buffers += [("_y", (4, 2, 16, width))]
        if flow[0] == "B":
            buffers += [("_pair", part)]
        if flow[1:] == "d":
            buffers += [("_landing", (3, *part))]
        else:
            buffers += [("_triple", (3, *part)), ("_single", part), ("_middle", part), ("_comb", (2, *part))]
        scratch += [(name + suffix, shape, BF16) for suffix, shape in buffers]
    semaphores = [
        ("load_sem", pltpu.SemaphoreType.DMA((9, 4))),
        ("store_sem", pltpu.SemaphoreType.DMA((8,))),
        ("send_sem", pltpu.SemaphoreType.DMA((remote,))),
        ("recv_sem", pltpu.SemaphoreType.DMA((remote,))),
    ]
    names = [n for group in (inputs, outputs, scratch, semaphores) for n in [e[0] for e in group]]
    results = pl.pallas_call(
        functools.partial(kernel, fold, patches, names),
        out_shape=[pltpu.VMEM(shape, F32) for _, shape, _ in outputs],
        in_specs=[spec for _, _, spec in inputs],
        out_specs=[spec for _, _, spec in outputs],
        scratch_shapes=[pltpu.VMEM(shape, dtype) for _, shape, dtype in scratch]
        + [sem for _, sem in semaphores],
        compiler_params=pltpu.CompilerParams(
            collective_id=0, has_side_effects=True, vmem_limit_bytes=44 * 1024 * 1024
        ),
    )(
        *[pltpu.with_memory_space_constraint(array, pltpu.HBM) for _, array, _ in inputs]
    )
    if fold == 1:
        results = pl.pallas_call(
            functools.partial(copy_out, len(results)),
            out_shape=[jax.ShapeDtypeStruct(a.shape, a.dtype) for a in results],
            in_specs=[hbm] * len(results),
            out_specs=[hbm] * len(results),
            scratch_shapes=[pltpu.SemaphoreType.DMA((len(results),))],
            compiler_params=pltpu.CompilerParams(vmem_limit_bytes=1024 * 1024),
        )(*results)
    output, d_state, g_down, g_up, g_out, g_qkv = results[:6]
    if fold == 1:
        grad_noise, grad_cond = results[6:]
    else:
        groups = [[m * fold + i for i in range(fold)] for m in range(GROUP)]

        def rest(array):
            return lax.psum_scatter(
                array, "patch", scatter_dimension=0, axis_index_groups=groups, tiled=True
            )

        g_down, g_up, g_out, g_qkv = rest(g_down), rest(g_up), rest(g_out), rest(g_qkv)
        mods = lax.psum(results[6], "patch") / GROUP
        highest = lax.Precision.HIGHEST
        grad_noise = jnp.dot(mods, w_cond.astype(F32).T, precision=highest)
        first_row = lax.axis_index("patch") * rows_each
        cond_cols = lax.dynamic_slice_in_dim(noise_embed, first_row, rows_each, 1)
        grad_cond = jnp.dot(cond_cols.T, mods, precision=highest)
    return output, d_state, grad_noise, grad_cond, g_qkv, g_out, g_up, g_down


def solution(mesh):
    in_specs = (
        P("rep", "patch", None),
        P(),
        P(),
        P(),
        P(),
        P(),
        P(),
        P("patch", None),
        P("patch"),
        P("patch"),
        P("rep", "patch", None),
    )
    out_specs = (
        P("rep", "patch", None),
        P("rep", "patch", None),
        P(),
        P("patch", None),
        P("patch", None),
        P("patch", None),
        P("patch", None),
        P("patch", None),
    )
    return jax.shard_map(body, mesh=mesh, in_specs=in_specs, out_specs=out_specs, check_vma=False)
```

```python
import functools

import jax
import jax.numpy as jnp
from jax import lax
from jax.experimental import pallas as pl
from jax.experimental.pallas import tpu as pltpu
from jax.sharding import PartitionSpec as P

HEADS = 4
GROUP = 16
SEND_SLOTS = 28
RECEIVERS = {"A": 5, "Ad": 6, "B": 5, "Bd": 6, "C": 6, "Cd": 7, "G": 3}
UNITS = (
    ("d", 0, 0, 256, "B"), ("d", 0, 256, 256, "C"), ("d", 2, 0, 512, "Bd"), ("d", 3, 0, 512, "C"),
    ("u", 0, 0, 256, "Cd"), ("u", 0, 256, 256, "A"), ("u", 2, 0, 512, "C"), ("o", 0, 0, 512, "Cd"),
    ("h", 3, 0, 128, "Cd"), ("h", 3, 128, 256, "C"), ("h", 1, 0, 128, "A"),
    ("h", 1, 128, 256, "Ad"), ("u", 3, 0, 512, "Cd"), ("h", 2, 0, 128, "B"),
    ("h", 2, 128, 256, "Cd"), ("d", 1, 0, 512, "A"), ("u", 1, 0, 512, "A"), ("h", 0, 0, 384, "C"),
)
ORDER = (
    "mask", ("up", 0), ("up", 3), ("dup", 0), ("gu", 0), ("up", 1), ("up", 2), ("gd", 0),
    ("dup", 1), 4, 5, ("gd", 1), ("gu", 1), 0, 1, ("dup", 3), 15, ("gu", 3), 2, ("dup", 2), 3,
    "mid", 16, 5, 12, 4, ("attn", 2), "m1", 0, 1, ("gu", 2), ("attn", 1), ("attn", 0), ("attn", 3),
    15, "out", 6, 3, "go", "table", ("gq", 0), ("gq", 3), 16, ("gq", 1), 7, "m0", 4, 17, 12, 1, 5,
    10, 11, 2, "m1", ("gq", 2), 3, 0, 9, 15, 6, 13, 14, "state", 12, 8, 10, 5, 16, 7, 11, "m0", 1,
    15, 2, 4, 0, 17, "m1", 3, 6, 13, 9, 16, 7, 14, 10, 12, 8, 17, 5, "m0", 9, 1, 15, 11, 6, 3, 2, 4,
    14, 0, 13, 8, 16, 17, 12, 1, 9, 11, 10, 7, 3, 6, 13, 14, 8, 17, 10, 9, 7, 6, 13, 14, 8, 17, 9,
)
MESH = pl.DeviceIdType.MESH
F32 = jnp.float32
BF16 = jnp.bfloat16


def dot(a, b):
    return lax.dot_general(a, b, (((1,), (0,)), ((), ())), preferred_element_type=F32)


def dot_nt(a, b):
    return lax.dot_general(a, b, (((1,), (1,)), ((), ())), preferred_element_type=F32)


def dot_tn(a, b):
    return lax.dot_general(a, b, (((0,), (0,)), ((), ())), preferred_element_type=F32)


def split3(v):
    high = v.astype(BF16)
    rest = v - high.astype(F32)
    mid = rest.astype(BF16)
    low = (rest - mid.astype(F32)).astype(BF16)
    return high.astype(F32), mid.astype(F32), low.astype(F32)


def layer_norm(values):
    centred = values - jnp.mean(values, axis=-1, keepdims=True)
    inv_std = lax.rsqrt(jnp.mean(centred * centred, axis=-1, keepdims=True) + 1e-05)
    return centred * inv_std, inv_std


def norm_back(gradient, normed, inv_std):
    first = jnp.mean(gradient, axis=-1, keepdims=True)
    second = jnp.mean(gradient * normed, axis=-1, keepdims=True)
    return (gradient - first - normed * second) * inv_std


class Names:
    pass


class Message:
    def __init__(self, v, receive, src, dst, target):
        self.v = v
        self.receive = receive
        self.ends = dict(src_ref=src, dst_ref=dst, device_id=target, device_id_type=MESH)
        self.slot = 0

    def copy(self):
        return pltpu.make_async_remote_copy(
            send_sem=self.v.send_sem.at[self.slot], recv_sem=self.v.recv_sem.at[self.receive], **self.ends
        )

    def start(self, slot):
        self.slot = slot
        self.copy().start()

    def arrive(self):
        self.copy().wait_recv()

    def leave(self):
        self.copy().wait_send()


def kernel(fold, patches, names, *refs):
    v = Names()
    for name, ref in zip(names, refs):
        setattr(v, name, ref)
    p = lax.axis_index("patch")
    r = lax.axis_index("rep")
    member = p // fold
    lane = lax.rem(p, fold)
    c = lax.rem(member, 2)
    x = lax.rem(member // 2, 2)
    z = member // 4
    finish = fold == 1

    def device(index, rep=r):
        return (index * fold + lane, rep)

    before = (lax.rem(p + patches - 1, patches), r)
    after = (lax.rem(p + 1, patches), r)
    core_peer = device(member + 1 - 2 * c)
    x_peer = device(member + 2 - 4 * x)
    y_peer = (p, 1 - r)

    def z_peer(there):
        return device(there * 4 + x * 2 + c)

    def z_x_peer(there):
        return device(there * 4 + (1 - x) * 2 + c)

    nodes, width = v.states_hbm.shape[1:]
    tiles = v.w_up_hbm.shape[1] // width
    head = width // HEADS
    factor = head ** (-0.5)
    table = v.k_v.shape[0]
    lent = table - nodes
    half = lent // 2

    loads = {}
    loaded = [0]

    def load(key, *pairs):
        copies = []
        for src, dst in pairs:
            copy = pltpu.make_async_copy(src, dst, v.load_sem.at[loaded[0]])
            loaded[0] += 1
            copy.start()
            copies.append(copy)
        loads[key] = copies

    def arrive(key):
        for copy in loads[key]:
            copy.wait()

    quarter = nodes // 4
    load(
        "states",
        (v.send_hbm, v.pick_v),
        *[
            (v.states_hbm.at[0, k * quarter : (k + 1) * quarter], v.states_v.at[k * quarter : (k + 1) * quarter])
            for k in range(4)
        ],
    )

    barrier = pltpu.get_barrier_semaphore()
    others = [before, after, core_peer, x_peer, y_peer] + [z_peer(lax.rem(z + d, 4)) for d in range(1, 4)]
    others += [z_x_peer(lax.rem(z + d, 4)) for d in range(1, 4)]
    for other in others:
        pl.semaphore_signal(barrier, inc=1, device_id=other, device_id_type=MESH)

    load("cond1", (v.noise_hbm, v.noise_v), (v.w_cond_hbm.at[:, 0 : 2 * width], v.w_cond_v.at[0]))
    load("qkv", (v.w_qkv_hbm, v.w_qkv_v))

    def tile(ref, t):
        return ref[:, t * width : (t + 1) * width]

    received = [0]
    slots = {}
    taken = [0]

    def receiver():
        received[0] += 1
        return received[0] - 1

    def take_slot(leave):
        slot = taken[0] % SEND_SLOTS
        taken[0] += 1
        if slot in slots:
            slots[slot]()
        slots[slot] = leave
        return slot

    def send(src, dst, target, receive=None):
        copy = Message(v, receiver() if receive is None else receive, src, dst, target)
        copy.start(take_slot(copy.leave))
        return copy

    arrive("states")
    normed1, inv1 = layer_norm(v.states_v[...])
    v.normed1_v[...] = normed1
    pick = (v.pick_v[...] == lax.broadcasted_iota(jnp.int32, (nodes, lent), 0)).astype(BF16)
    v.lend_v[...] = dot_tn(pick, normed1.astype(BF16)).astype(BF16)
    pl.semaphore_wait(barrier, len(others))
    halo = [
        send(v.lend_v.at[0:half], v.halo_v.at[half:lent], before),
        send(v.lend_v.at[half:lent], v.halo_v.at[0:half], after),
    ]

    load("index", (v.neighbours_hbm, v.neighbours_v), (v.valid_hbm, v.valid_v))
    load("cond2", (v.w_cond_hbm.at[:, 2 * width : 4 * width], v.w_cond_v.at[1]))
    load("out", (v.w_out_hbm, v.w_out_v))
    load("up", (v.w_up_hbm, v.w_up_v))
    load("down", (v.cot_hbm.at[0], v.cot_v), (v.w_down_hbm, v.w_down_v))

    arrive("cond1")
    condition = v.noise_v[pl.ds(r, 1), :]
    row = lax.broadcasted_iota(jnp.int32, (16, width), 0)
    high, mid, low = split3(condition)
    stacked = jnp.where(row == 0, high, jnp.where(row == 1, mid, jnp.where(row == 2, low, 0.0))).astype(BF16)
    mod1 = jnp.sum(dot(stacked, v.w_cond_v[0]), axis=0, keepdims=True)
    scale1, shift1 = mod1[:, :width], mod1[:, width:]
    hidden1 = (v.normed1_v[...] * (1.0 + scale1) + shift1).astype(BF16)
    v.table_v[0:nodes, :] = hidden1

    arrive("qkv")
    v.k_v[0:nodes, :] = dot(hidden1, tile(v.w_qkv_v, 1)).astype(BF16)
    v.v_v[0:nodes, :] = dot(hidden1, tile(v.w_qkv_v, 2)).astype(BF16)
    v.q_v[...] = dot(hidden1, tile(v.w_qkv_v, 0)).astype(BF16)

    arrive("index")
    entry = lax.broadcasted_iota(jnp.int32, (table, nodes), 0)
    count = jnp.zeros((table, nodes), F32)
    for j in range(v.neighbours_v.shape[0]):
        count = count + (v.neighbours_v[j : j + 1, :] == entry).astype(F32)
    v.count_v[...] = count

    arrive("cond2")
    mod2 = jnp.sum(dot(stacked, v.w_cond_v[1]), axis=0, keepdims=True)
    scale2, shift2 = mod2[:, :width], mod2[:, width:]
    real = jnp.sum(v.valid_v[...], axis=1, keepdims=True)
    mask = (lax.broadcasted_iota(jnp.int32, (nodes, 1), 0) < real).astype(F32)

    for copy in halo:
        copy.arrive()
    rows = (v.halo_v[...].astype(F32) * (1.0 + scale1) + shift1).astype(BF16)
    v.table_v[nodes:table, :] = rows
    v.k_v[nodes:table, :] = dot(rows, tile(v.w_qkv_v, 1)).astype(BF16)
    v.v_v[nodes:table, :] = dot(rows, tile(v.w_qkv_v, 2)).astype(BF16)

    for h in range(HEADS):
        cols = slice(h * head, (h + 1) * head)
        scores = dot_nt(v.k_v[:, cols], v.q_v[:, cols]) * factor
        times = v.count_v[...]
        scores = jnp.where(times > 0.0, scores, -1e30)
        exponent = times * jnp.exp(scores - jnp.max(scores, axis=0, keepdims=True))
        attn = exponent * (1.0 / jnp.sum(exponent, axis=0, keepdims=True))
        v.attn_v[h] = attn
        v.mix_v[:, cols] = dot_tn(attn.astype(BF16), v.v_v[:, cols]).astype(BF16)

    arrive("out")
    middle = v.states_v[...] + mask * dot(v.mix_v[...], v.w_out_v[...])
    v.middle_v[...] = middle
    normed2, inv2 = layer_norm(middle)
    v.normed2_v[...] = normed2
    v.hidden2_v[...] = (normed2 * (1.0 + scale2) + shift2).astype(BF16)

    def exchange_z(own, name):
        triple, single, middle_in, comb = (
            getattr(v, name + "_triple"),
            getattr(v, name + "_single"),
            getattr(v, name + "_middle"),
            getattr(v, name + "_comb"),
        )
        outer = (z == 0) | (z == 3)
        outer_z = jnp.where(z < 2, 0, 3)
        other_inner = jnp.where(z < 2, 2, 1)
        other_outer = 3 - outer_z
        near_inner = jnp.where(z < 2, 1, 2)
        first = jnp.where(z == 0, 1, 0)
        offset = jnp.where(z == 1, 1, 0)
        first_number, middle_number = receiver(), receiver()
        to_inner = Message(v, first_number, own.at[pl.ds(first, 3)], triple, z_peer(near_inner))
        to_outer = Message(v, first_number, own.at[outer_z], single, z_peer(outer_z))
        across = Message(v, middle_number, comb.at[0], middle_in, z_peer(other_inner))
        beyond = Message(v, middle_number, comb.at[1], middle_in, z_peer(other_outer))

        def first_left():
            @pl.when(outer)
            def _():
                to_inner.leave()

            @pl.when(jnp.logical_not(outer))
            def _():
                to_outer.leave()

        def inner_left(copy):
            def left():
                @pl.when(jnp.logical_not(outer))
                def _():
                    copy.leave()

            return left

        def begin():
            slot = take_slot(first_left)

            @pl.when(outer)
            def _():
                to_inner.start(slot)

            @pl.when(jnp.logical_not(outer))
            def _():
                to_outer.start(slot)

        def combine():
            beyond_slot, across_slot = take_slot(inner_left(beyond)), take_slot(inner_left(across))

            @pl.when(jnp.logical_not(outer))
            def _():
                to_inner.arrive()
                comb[1] = own[other_outer] + triple[other_outer - offset]
                beyond.start(beyond_slot)
                comb[0] = own[other_inner] + triple[other_inner - offset]
                across.start(across_slot)

        def finish_sum(result):
            across.arrive()

            @pl.when(outer)
            def _():
                to_outer.arrive()
                total = own[z].astype(F32) + single[...].astype(F32) + middle_in[...].astype(F32)
                result[...] = total.astype(BF16)

            @pl.when(jnp.logical_not(outer))
            def _():
                total = own[z].astype(F32) + triple[z - offset].astype(F32) + middle_in[...].astype(F32)
                result[...] = total.astype(BF16)

        return begin, combine, finish_sum

    def direct_z(own, name):
        landing = getattr(v, name + "_landing")
        copies = []

        def begin():
            for d in range(1, 4):
                there = lax.rem(z + d, 4)
                copies.append(send(own.at[there], landing.at[d - 1], z_peer(there)))

        def finish_sum(result):
            for copy in copies:
                copy.arrive()
            total = own[z].astype(F32)
            for d in range(3):
                total = total + landing[d].astype(F32)
            result[...] = total.astype(BF16)

        return begin, finish_sum

    queue = {}
    core_copies = {}

    def place(n, value, part=None):
        kind, where, start, wide, _ = UNITS[n]
        rows = value.shape[0]

        def at(first):
            return pl.ds(first if part is None else pl.multiple_of(first + part * rows, rows), rows)

        if kind == "d":
            for b in range(wide // 128):
                block = value[:, b * 128 : (b + 1) * 128]
                v.down_v[at((start // 128 + b) * 32), where * 128 : (where + 1) * 128] = block
        elif kind == "u":
            first = where * width + start
            v.up_v[at(0), first : first + wide] = value
        elif kind == "o":
            v.o_v[at(0), start : start + wide] = value
        else:
            for b in range(wide // 128):
                first = (start // 128 + b) * width + where * 128
                v.qkv_v[at(0), first : first + 128] = value[:, b * 128 : (b + 1) * 128]

    def unit_steps(n):
        name, flow = "u%d" % n, UNITS[n][4]
        grad, landed, mine = (getattr(v, name + suffix) for suffix in ("_grad", "_core", "_mine"))
        result, received = getattr(v, name + "_result"), getattr(v, name + "_received")
        direct = flow[1:] == "d"
        copies = {}

        def core_sum():
            core_copies[n].arrive()
            total = grad[:, :, c] + landed[...]
            mine[...] = total.reshape(mine.shape)

        def y_exchange():
            copies["last"] = send(result, received, y_peer)

        def ending():
            copies["last"].arrive()
            if flow[0] == "C":
                place(n, result[...].astype(F32), r)
                place(n, received[...].astype(F32), 1 - r)
            else:
                place(n, result[...].astype(F32) + received[...].astype(F32))

        def reduce_z(own, then):
            if direct:
                begin, finish_sum = direct_z(own, name)
                middle_steps = []
            else:
                begin, combine, finish_sum = exchange_z(own, name)
                middle_steps = [combine]

            def last():
                finish_sum(then[0])
                then[1]()

            return begin, middle_steps + [last]

        if flow[0] == "G":
            plane = getattr(v, name + "_plane")

            def start():
                core_sum()
                number = receiver()
                for d in range(1, 8):
                    there = lax.rem(z + d // 2, 4)
                    target = z_peer(there) if d % 2 == 0 else z_x_peer(there)
                    send(mine.at[there, x if d % 2 == 0 else 1 - x], plane.at[d - 1], target, number)
                copies["plane"] = Message(v, number, plane, plane, x_peer)

            def second():
                copies["plane"].arrive()
                total = mine[z, x].astype(F32)
                for d in range(7):
                    total = total + plane[d].astype(F32)
                result[...] = total.astype(BF16)
                y_exchange()

            return [start, second, ending]
        if flow[0] == "A":
            from_x = getattr(v, name + "_x")
            begin, rest = reduce_z(from_x, (result, y_exchange))

            def start():
                core_sum()
                copies["x"] = send(mine.at[:, 1 - x], from_x, x_peer)

            def second():
                copies["x"].arrive()
                from_x[...] = mine[:, x] + from_x[...]
                begin()

            return [start, second] + rest + [ending]
        if flow[0] == "C":
            from_y, from_x = getattr(v, name + "_y"), getattr(v, name + "_x")
            begin, rest = reduce_z(from_x, (result, y_exchange))

            def start():
                core_sum()
                copies["y"] = send(mine.at[:, :, 1 - r], from_y, y_peer)

            def second():
                copies["y"].arrive()
                from_y[...] = mine[:, :, r] + from_y[...]
                copies["x"] = send(from_y.at[:, 1 - x], from_x, x_peer)

            def third():
                copies["x"].arrive()
                from_x[...] = from_y[:, x] + from_x[...]
                begin()

            return [start, second, third] + rest + [ending]
        pair, from_x = getattr(v, name + "_pair"), getattr(v, name + "_x")

        def x_exchange():
            copies["x"] = send(pair.at[1 - x], from_x, x_peer)

        begin, rest = reduce_z(mine, (pair, x_exchange))

        def start():
            core_sum()
            begin()

        def after_x():
            copies["x"].arrive()
            result[...] = pair[x] + from_x[...]
            y_exchange()

        return [start] + rest + [after_x, ending]

    def produce(kind, where, piece):
        for n, (its_kind, its_where, start, wide, _) in enumerate(UNITS):
            if (its_kind, its_where) == (kind, where):
                grad = getattr(v, "u%d_grad" % n)
                for b in range(0, wide, 128):
                    grad[..., b : b + 128] = piece(start + b).reshape(4, 2, 2, 32, 128)
                core_copies[n] = send(grad.at[:, :, 1 - c], getattr(v, "u%d_core" % n), core_peer)
                queue[n] = unit_steps(n)

    def section_up(t):
        if t == 0:
            arrive("up")
        cols = slice(t * width, (t + 1) * width)
        up = dot(v.hidden2_v[...], v.w_up_v[:, cols])
        v.up_proj_v[:, cols] = up
        v.activation_v[:, cols] = (up * (1.0 / (1.0 + jnp.exp(-up)))).astype(BF16)

    def section_mask():
        arrive("down")
        v.d_branch_v[...] = (mask * v.cot_v[...]).astype(BF16)

    def section_dup(t):
        cols = slice(t * width, (t + 1) * width)
        up = v.up_proj_v[:, cols]
        sigmoid = 1.0 / (1.0 + jnp.exp(-up))
        d_act = dot_nt(v.d_branch_v[...], v.w_down_v[t * width : (t + 1) * width, :])
        v.d_up_v[:, cols] = (d_act * sigmoid * (1.0 + up * (1.0 - sigmoid))).astype(BF16)

    def section_gd(h):
        value = dot_tn(v.activation_v[...], v.d_branch_v[:, h * 256 : (h + 1) * 256]).astype(BF16)
        value = value.reshape(GROUP, 4, 32, 256)
        for k in range(2):
            produce("d", 2 * h + k, lambda start: value[:, start // 128, :, k * 128 : (k + 1) * 128])

    def section_gu(t):
        value = dot_tn(v.hidden2_v[...], v.d_up_v[:, t * width : (t + 1) * width]).astype(BF16)
        produce("u", t, lambda start: value[:, start : start + 128])

    def section_out():
        branch = dot(v.activation_v[:, 0:width], v.w_down_v[0:width, :])
        for t in range(1, tiles):
            branch = branch + dot(v.activation_v[:, t * width : (t + 1) * width], v.w_down_v[t * width : (t + 1) * width, :])
        v.out_v[0] = v.middle_v[...] + mask * branch

    def section_mid():
        d_hidden2 = dot_nt(v.d_up_v[:, 0:width], tile(v.w_up_v, 0))
        for t in range(1, tiles):
            d_hidden2 = d_hidden2 + dot_nt(v.d_up_v[:, t * width : (t + 1) * width], tile(v.w_up_v, t))
        normed2 = v.normed2_v[...]
        v.mod_v[1, :, 0:width] = jnp.sum(d_hidden2 * normed2, axis=0, keepdims=True)
        v.mod_v[1, :, width : 2 * width] = jnp.sum(d_hidden2, axis=0, keepdims=True)
        queue["m1"] = mod_steps(1)
        d_middle = v.cot_v[...] + norm_back(d_hidden2 * (1.0 + scale2), normed2, inv2)
        v.d_middle_v[...] = d_middle
        v.d_attended_v[...] = (mask * d_middle).astype(BF16)
        v.d_mix_v[...] = dot_nt(v.d_attended_v[...], v.w_out_v[...]).astype(BF16)

    def section_go():
        value = dot_tn(v.mix_v[...], v.d_attended_v[...]).astype(BF16)
        produce("o", 0, lambda start: value[:, start : start + 128])

    def section_attn(h):
        cols = slice(h * head, (h + 1) * head)
        attn = v.attn_v[h]
        d_attn = dot_nt(v.v_v[:, cols], v.d_mix_v[:, cols])
        inner = jnp.sum(attn * d_attn, axis=0, keepdims=True)
        d_scores = (attn * (d_attn - inner)).astype(BF16)
        v.d_q_v[:, cols] = (dot_tn(d_scores, v.k_v[:, cols]) * factor).astype(BF16)
        v.d_k_v[:, cols] = (dot(d_scores, v.q_v[:, cols]) * factor).astype(BF16)
        v.d_v_v[:, cols] = dot(attn.astype(BF16), v.d_mix_v[:, cols]).astype(BF16)

    def section_gq(h):
        cols = slice(h * head, (h + 1) * head)
        values = [
            dot_tn(v.table_v[0:nodes, :], v.d_q_v[:, cols]).astype(BF16),
            dot_tn(v.table_v[...], v.d_k_v[:, cols]).astype(BF16),
            dot_tn(v.table_v[...], v.d_v_v[:, cols]).astype(BF16),
        ]
        produce("h", h, lambda start: values[start // 128])

    back = []

    def section_table():
        d_table = dot_nt(v.d_k_v[...], tile(v.w_qkv_v, 1)) + dot_nt(v.d_v_v[...], tile(v.w_qkv_v, 2))
        v.lend_back_v[...] = d_table[nodes:table, :].astype(BF16)
        back.append(send(v.lend_back_v.at[0:half], v.returned_v.at[half:lent], before))
        back.append(send(v.lend_back_v.at[half:lent], v.returned_v.at[0:half], after))
        d_hidden1 = d_table[0:nodes, :] + dot_nt(v.d_q_v[...], tile(v.w_qkv_v, 0))
        v.d_hidden1_v[...] = d_hidden1
        d_lent = d_table[nodes:table, :]
        v.mod_v[0, :, 0:width] = jnp.sum(d_hidden1 * v.normed1_v[...], axis=0, keepdims=True) + jnp.sum(
            d_lent * v.halo_v[...].astype(F32), axis=0, keepdims=True
        )
        v.mod_v[0, :, width : 2 * width] = jnp.sum(d_hidden1, axis=0, keepdims=True) + jnp.sum(
            d_lent, axis=0, keepdims=True
        )
        queue["m0"] = mod_steps(0)

    def section_state():
        for copy in back:
            copy.arrive()
        d_hidden1 = v.d_hidden1_v[...] + dot(pick, v.returned_v[...])
        normed1 = v.normed1_v[...]
        v.d_states_v[0] = v.d_middle_v[...] + norm_back(d_hidden1 * (1.0 + scale1), normed1, inv1)

    def mod_steps(part):
        own, from_core, plane, rows = v.mod_v.at[part], v.mod_core_v.at[part], v.mods_v.at[part], v.rows_v.at[part]
        copies = [send(own, from_core, core_peer)]

        def spread():
            copies.pop().arrive()
            plane[0] = own[...] + from_core[...]
            number = receiver()
            for d in range(1, 8):
                there = lax.rem(z + d // 2, 4)
                target = z_peer(there) if d % 2 == 0 else z_x_peer(there)
                send(plane.at[0], plane.at[d], target, number)
            copies.append(Message(v, number, plane.at[pl.ds(1, 7)], plane.at[pl.ds(1, 7)], x_peer))

        def swap():
            copies.pop().arrive()
            total = jnp.zeros(own.shape, F32)
            for there in range(4):
                for side in range(2):
                    total = total + plane[lax.rem(z + 4 - there, 4) * 2 + lax.rem(x + side, 2)]
            rows[r] = total
            copies.append(send(rows.at[r], rows.at[r], y_peer))

        def spend():
            copies.pop().arrive()
            first_row, second_row = rows[0], rows[1]
            here = slice(part * 2 * width, (part + 1) * 2 * width)
            if not finish:
                v.d_noise_v[0:1, here] = first_row
                v.d_noise_v[1:2, here] = second_row
                return
            row = lax.broadcasted_iota(jnp.int32, (16, 2 * width), 0)
            stacked = jnp.zeros((16, 2 * width), F32)
            for number, piece in enumerate(split3(first_row) + split3(second_row)):
                stacked = jnp.where(row == number, piece, stacked)
            noise = dot_nt(stacked.astype(BF16), v.w_cond_v[part])
            first_noise = jnp.sum(noise[0:3], axis=0, keepdims=True)
            second_noise = jnp.sum(noise[3:6], axis=0, keepdims=True)
            if part == 1:
                v.noise_part_v[0:1, :] = first_noise
                v.noise_part_v[1:2, :] = second_noise
            else:
                v.d_noise_v[0:1, :] = first_noise + v.noise_part_v[0:1, :]
                v.d_noise_v[1:2, :] = second_noise + v.noise_part_v[1:2, :]
            shape = (v.d_cond_v.shape[0], width)
            mine = lax.broadcasted_iota(jnp.int32, shape, 1) == (
                lax.broadcasted_iota(jnp.int32, shape, 0) + p * shape[0]
            )
            picked = [
                jnp.sum(jnp.where(mine, v.noise_v[b : b + 1, :], 0.0), axis=1, keepdims=True)
                for b in range(2)
            ]
            v.d_cond_v[:, here] = picked[0] * first_row + picked[1] * second_row

        return [spread, swap, spend]

    sections = {
        "up": section_up,
        "mask": section_mask,
        "dup": section_dup,
        "gd": section_gd,
        "gu": section_gu,
        "out": section_out,
        "mid": section_mid,
        "go": section_go,
        "attn": section_attn,
        "gq": section_gq,
        "table": section_table,
        "state": section_state,
    }
    for entry in ORDER:
        if entry in queue:
            queue[entry].pop(0)()
        elif isinstance(entry, tuple):
            sections[entry[0]](entry[1])
        else:
            sections[entry]()
    for steps in queue.values():
        for step in steps:
            step()
    assert received[0] == v.recv_sem.shape[0]

    for leave in slots.values():
        leave()


def copy_out(count, *refs):
    for n in range(count):
        src, dst = refs[n], refs[count + n]
        rows = src.shape[-2]
        pieces = 4 if rows % 64 == 0 else 1
        for k in range(pieces):
            at = (*[slice(None)] * (len(src.shape) - 2), slice(k * rows // pieces, (k + 1) * rows // pieces))
            pltpu.make_async_copy(src.at[at], dst.at[at], refs[-1].at[n]).start()
    for n in range(count):
        pltpu.make_async_copy(refs[n], refs[count + n], refs[-1].at[n]).wait()


def body(
    node_state,
    noise_embed,
    w_cond,
    w_qkv,
    w_out,
    w_up,
    w_down,
    neighbours,
    send_rows,
    valid,
    cotangent,
):
    nodes, width = node_state.shape[1:]
    hidden = w_up.shape[1]
    lent = send_rows.shape[0]
    table = nodes + lent
    patches = lax.axis_size("patch")
    fold = patches // GROUP
    rows_each = width // patches
    block = width // GROUP
    half = width // 2

    hbm = pl.BlockSpec(memory_space=pl.ANY)
    vmem = pl.BlockSpec(memory_space=pltpu.VMEM)
    inputs = [
        ("states_hbm", node_state, hbm),
        ("noise_hbm", noise_embed, hbm),
        ("w_cond_hbm", w_cond, hbm),
        ("w_qkv_hbm", w_qkv, hbm),
        ("w_out_hbm", w_out, hbm),
        ("w_up_hbm", w_up, hbm),
        ("w_down_hbm", w_down, hbm),
        ("neighbours_hbm", neighbours.T, hbm),
        ("send_hbm", send_rows[None, :], hbm),
        ("valid_hbm", valid[None, :], hbm),
        ("cot_hbm", cotangent, hbm),
    ]
    outputs = [
        ("out_v", node_state.shape, vmem),
        ("d_states_v", node_state.shape, vmem),
        ("down_v", (hidden // GROUP, width), vmem),
        ("up_v", (block, hidden), vmem),
        ("o_v", (block, width), vmem),
        ("qkv_v", (block, 3 * width), vmem),
    ]
    if fold == 1:
        outputs += [("d_noise_v", noise_embed.shape, vmem), ("d_cond_v", (rows_each, 4 * width), vmem)]
    else:
        outputs += [("d_noise_v", (noise_embed.shape[0], 4 * width), vmem)]
    tiles = hidden // width
    receivers = 10 + sum(RECEIVERS[unit[4]] for unit in UNITS)
    scratch = [
        ("noise_v", noise_embed.shape, F32),
        ("neighbours_v", neighbours.shape[::-1], jnp.int32),
        ("pick_v", (1, lent), jnp.int32),
        ("valid_v", (1, nodes), jnp.int32),
        ("states_v", (nodes, width), F32),
        ("cot_v", (nodes, width), F32),
        ("w_cond_v", (2, width, 2 * width), BF16),
        ("w_qkv_v", w_qkv.shape, BF16),
        ("w_out_v", (width, width), BF16),
        ("w_up_v", w_up.shape, BF16),
        ("w_down_v", w_down.shape, BF16),
        ("normed1_v", (nodes, width), F32),
        ("table_v", (table, width), BF16),
        ("lend_v", (lent, width), BF16),
        ("halo_v", (lent, width), BF16),
        ("returned_v", (lent, width), BF16),
        ("q_v", (nodes, width), BF16),
        ("k_v", (table, width), BF16),
        ("v_v", (table, width), BF16),
        ("count_v", (table, nodes), F32),
        ("attn_v", (HEADS, table, nodes), F32),
        ("mix_v", (nodes, width), BF16),
        ("middle_v", (nodes, width), F32),
        ("normed2_v", (nodes, width), F32),
        ("hidden2_v", (nodes, width), BF16),
        ("d_branch_v", (nodes, width), BF16),
        ("d_mix_v", (nodes, width), BF16),
        ("d_q_v", (nodes, width), BF16),
        ("d_k_v", (table, width), BF16),
        ("d_v_v", (table, width), BF16),
        ("mod_v", (2, 1, 2 * width), F32),
        ("mod_core_v", (2, 1, 2 * width), F32),
        ("mods_v", (2, 8, 1, 2 * width), F32),
        ("rows_v", (2, 2, 1, 2 * width), F32),
        ("noise_part_v", noise_embed.shape, F32),
        ("up_proj_v", (nodes, hidden), F32),
        ("activation_v", (nodes, hidden), BF16),
        ("d_up_v", (nodes, hidden), BF16),
        ("d_middle_v", (nodes, width), F32),
        ("d_attended_v", (nodes, width), BF16),
        ("d_hidden1_v", (nodes, width), F32),
        ("lend_back_v", (lent, width), BF16),
    ]
    for n, (_, _, _, wide, flow) in enumerate(UNITS):
        name = "u%d" % n
        rows = 16 if flow[0] == "C" else 32
        part = (2, 32, wide) if flow[0] == "B" else (rows, wide)
        buffers = [("_grad", (4, 2, 2, 32, wide)), ("_core", (4, 2, 32, wide))]
        buffers += [("_mine", (4, 2, 2, 16, wide) if flow[0] == "C" else (4, 2, 32, wide))]
        buffers += [("_result", (rows, wide)), ("_received", (rows, wide))]
        if flow[0] == "G":
            buffers += [("_plane", (7, rows, wide))]
        else:
            buffers += [("_x", (rows, wide) if flow[0] == "B" else (4, rows, wide))]
            if flow[0] == "C":
                buffers += [("_y", (4, 2, 16, wide))]
            if flow[0] == "B":
                buffers += [("_pair", part)]
            if flow[1:] == "d":
                buffers += [("_landing", (3, *part))]
            else:
                buffers += [("_triple", (3, *part)), ("_single", part), ("_middle", part), ("_comb", (2, *part))]
        scratch += [(name + suffix, shape, BF16) for suffix, shape in buffers]
    semaphores = [
        ("load_sem", pltpu.SemaphoreType.DMA((15,))),
        ("send_sem", pltpu.SemaphoreType.DMA((SEND_SLOTS,))),
        ("recv_sem", pltpu.SemaphoreType.DMA((receivers,))),
    ]
    names = [n for group in (inputs, outputs, scratch, semaphores) for n in [e[0] for e in group]]
    results = pl.pallas_call(
        functools.partial(kernel, fold, patches, names),
        out_shape=[pltpu.VMEM(shape, F32) for _, shape, _ in outputs],
        in_specs=[spec for _, _, spec in inputs],
        out_specs=[spec for _, _, spec in outputs],
        scratch_shapes=[pltpu.VMEM(shape, dtype) for _, shape, dtype in scratch]
        + [sem for _, sem in semaphores],
        compiler_params=pltpu.CompilerParams(
            collective_id=0, has_side_effects=True, vmem_limit_bytes=44 * 1024 * 1024
        ),
    )(
        *[pltpu.with_memory_space_constraint(array, pltpu.HBM) for _, array, _ in inputs]
    )
    if fold == 1:
        results = pl.pallas_call(
            functools.partial(copy_out, len(results)),
            out_shape=[jax.ShapeDtypeStruct(a.shape, a.dtype) for a in results],
            in_specs=[hbm] * len(results),
            out_specs=[hbm] * len(results),
            scratch_shapes=[pltpu.SemaphoreType.DMA((len(results),))],
            compiler_params=pltpu.CompilerParams(vmem_limit_bytes=1024 * 1024),
        )(*results)
    output, d_state, g_down, g_up, g_out, g_qkv = results[:6]
    if fold == 1:
        grad_noise, grad_cond = results[6:]
    else:
        groups = [[m * fold + i for i in range(fold)] for m in range(GROUP)]

        def rest(array):
            return lax.psum_scatter(
                array, "patch", scatter_dimension=0, axis_index_groups=groups, tiled=True
            )

        g_down, g_up, g_out, g_qkv = rest(g_down), rest(g_up), rest(g_out), rest(g_qkv)
        mods = lax.psum(results[6], "patch") / GROUP
        highest = lax.Precision.HIGHEST
        grad_noise = jnp.dot(mods, w_cond.astype(F32).T, precision=highest)
        first_row = lax.axis_index("patch") * rows_each
        cond_cols = lax.dynamic_slice_in_dim(noise_embed, first_row, rows_each, 1)
        grad_cond = jnp.dot(cond_cols.T, mods, precision=highest)
    return output, d_state, grad_noise, grad_cond, g_qkv, g_out, g_up, g_down


def solution(mesh):
    in_specs = (
        P("rep", "patch", None),
        P(),
        P(),
        P(),
        P(),
        P(),
        P(),
        P("patch", None),
        P("patch"),
        P("patch"),
        P("rep", "patch", None),
    )
    out_specs = (
        P("rep", "patch", None),
        P("rep", "patch", None),
        P(),
        P("patch", None),
        P("patch", None),
        P("patch", None),
        P("patch", None),
        P("patch", None),
    )
    return jax.shard_map(body, mesh=mesh, in_specs=in_specs, out_specs=out_specs, check_vma=False)
```

```python
import functools

import jax
import jax.numpy as jnp
from jax import lax
from jax.experimental import pallas as pl
from jax.experimental.pallas import tpu as pltpu
from jax.sharding import PartitionSpec as P

HEADS = 4
GROUP = 16
UNITS = (
    ("d", 0, 0, 256, "C"), ("d", 0, 256, 256, "A"), ("d", 1, 0, 512, "B"), ("d", 2, 0, 256, "Cd"),
    ("d", 2, 256, 256, "Bd"), ("d", 3, 0, 512, "A"), ("u", 0, 0, 512, "A"), ("u", 1, 0, 256, "Bd"),
    ("u", 1, 256, 256, "A"), ("u", 2, 0, 512, "C"), ("u", 3, 0, 512, "C"), ("o", 0, 0, 512, "Cd"),
    ("h", 0, 0, 128, "Ad"), ("h", 0, 128, 256, "Cd"), ("h", 1, 0, 128, "Ad"),
    ("h", 1, 128, 256, "C"), ("h", 2, 0, 384, "C"), ("h", 3, 0, 128, "Cd"),
    ("h", 3, 128, 256, "Cd"),
)
ORDER = (
    "mask", ("up", 1), ("dup", 1), ("gu", 1), ("up", 0), ("up", 3), ("up", 2), ("gd", 0), 7,
    ("gd", 1), 8, ("dup", 3), ("gu", 3), 0, 1, ("dup", 2), 2, 3, 4, ("dup", 0), 5, ("gu", 2),
    ("gu", 0), 10, "mid", 8, 0, 9, "go", 1, 6, 7, "m1", 3, ("attn", 1), ("attn", 0), 11,
    ("attn", 2), "out", 5, 2, 0, 10, ("attn", 3), ("gq", 2), "table", ("gq", 1), ("gq", 3),
    ("gq", 0), 16, 8, 6, 14, 9, 15, 1, 18, 12, 13, 3, "m0", "m1", 17, 11, 2, 7, 4, 10, 5, 14, 0, 8,
    1, 16, 9, "state", 12, 15, 6, 18, 5, 11, 3, 2, "m0", 4, 13, 10, "m1", 0, 17, 16, 7, 14, 9, 8,
    15, 1, 6, 18, 5, 3, 12, 13, 2, "m0", 17, 4, 11, 16, 14, 10, 15, 0, 9, 6, 12, 18, 11, 13, 10, 17,
    16, 9, 15, 18, 13, 17, 16, 15,
)
MESH = pl.DeviceIdType.MESH
F32 = jnp.float32
BF16 = jnp.bfloat16


def dot(a, b):
    return lax.dot_general(a, b, (((1,), (0,)), ((), ())), preferred_element_type=F32)


def dot_nt(a, b):
    return lax.dot_general(a, b, (((1,), (1,)), ((), ())), preferred_element_type=F32)


def dot_tn(a, b):
    return lax.dot_general(a, b, (((0,), (0,)), ((), ())), preferred_element_type=F32)


def split3(v):
    high = v.astype(BF16)
    rest = v - high.astype(F32)
    mid = rest.astype(BF16)
    low = (rest - mid.astype(F32)).astype(BF16)
    return high.astype(F32), mid.astype(F32), low.astype(F32)


def layer_norm(values):
    centred = values - jnp.mean(values, axis=-1, keepdims=True)
    inv_std = lax.rsqrt(jnp.mean(centred * centred, axis=-1, keepdims=True) + 1e-05)
    return centred * inv_std, inv_std


def norm_back(gradient, normed, inv_std):
    first = jnp.mean(gradient, axis=-1, keepdims=True)
    second = jnp.mean(gradient * normed, axis=-1, keepdims=True)
    return (gradient - first - normed * second) * inv_std


ROUTES = {
    "A": (("core", -1, 0), ("x", 0, 1), ("first", 1, 3), ("middle", 2, 3), ("y", 3, 4)),
    "Ad": (("core", -1, 0), ("x", 0, 1), ("z", 1, 2), ("y", 2, 3)),
    "B": (("core", -1, 0), ("first", 0, 2), ("middle", 1, 2), ("x", 2, 3), ("y", 3, 4)),
    "Bd": (("core", -1, 0), ("z", 0, 1), ("x", 1, 2), ("y", 2, 3)),
    "C": (("core", -1, 0), ("early y", 0, 1), ("x", 1, 2), ("first", 2, 4), ("middle", 3, 4), ("y", 4, 5)),
    "Cd": (("core", -1, 0), ("early y", 0, 1), ("x", 1, 2), ("z", 2, 3), ("y", 3, 4)),
    "G": (("core", -1, 0), ("plane", 0, 1), ("y", 1, 2)),
    "M": (("core", -1, 0), ("plane", 0, 1), ("y", 1, 2)),
}
SOURCE = {"d": lambda w: ("gd", w // 2), "u": lambda w: ("gu", w), "o": lambda w: "go", "h": lambda w: ("gq", w)}


def receive_plan():
    steps = {}
    for position, entry in enumerate(ORDER):
        steps.setdefault(entry, []).append(position)
    copies = []
    for n, (kind, where, _, _, route) in enumerate(UNITS):
        copies += [(n, steps[SOURCE[kind](where)][0], *copy) for copy in ROUTES[route]]
    for name, source in (("m1", "mid"), ("m0", "table")):
        copies += [(name, steps[source][0], *copy) for copy in ROUTES["M"]]
    timed = []
    for n, start, what, sender, waiter in copies:
        timed.append((start if sender < 0 else steps[n][sender], steps[n][waiter], what, n))
    timed.sort(key=lambda copy: copy[0])
    kinds = {"early y": "y", "middle": "first"}

    def answered(send, kind, waited):
        return any(
            kinds.get(what, what) == kind and what != "middle" and waited <= sent and got <= send
            for sent, got, what, _ in timed
        )

    numbers, free = {}, [(-1, 0), (-1, 1)]
    count = 4
    for send, got, what, n in timed:
        kind = kinds.get(what, what)
        fit = [entry for entry in free if answered(send, kind, entry[0])]
        if fit:
            entry = max(fit)
            free.remove(entry)
            number = entry[1]
        else:
            number, count = count, count + 1
        numbers[n, what] = number
        free.append((got, number))
    return numbers, count


class Names:
    pass


class Message:
    def __init__(self, v, outgoing, receive, src, dst, target):
        self.parts = dict(
            src_ref=src,
            dst_ref=dst,
            send_sem=v.send_sem.at[outgoing],
            recv_sem=v.recv_sem.at[receive],
            device_id=target,
            device_id_type=MESH,
        )

    def start(self):
        pltpu.make_async_remote_copy(**self.parts).start()

    def arrive(self):
        pltpu.make_async_remote_copy(**self.parts).wait_recv()

    def leave(self):
        pltpu.make_async_remote_copy(**self.parts).wait_send()


def kernel(fold, patches, names, *refs):
    v = Names()
    for name, ref in zip(names, refs):
        setattr(v, name, ref)
    p = lax.axis_index("patch")
    r = lax.axis_index("rep")
    member = p // fold
    lane = lax.rem(p, fold)
    c = lax.rem(member, 2)
    x = lax.rem(member // 2, 2)
    z = member // 4
    finish = fold == 1

    def device(index, rep=r):
        return (index * fold + lane, rep)

    before = (lax.rem(p + patches - 1, patches), r)
    after = (lax.rem(p + 1, patches), r)
    core_peer = device(member + 1 - 2 * c)
    x_peer = device(member + 2 - 4 * x)
    y_peer = (p, 1 - r)

    def z_peer(there):
        return device(there * 4 + x * 2 + c)

    def z_x_peer(there):
        return device(there * 4 + (1 - x) * 2 + c)

    nodes, width = v.states_hbm.shape[1:]
    tiles = v.w_up_hbm.shape[1] // width
    head = width // HEADS
    factor = head ** (-0.5)
    table = v.k_v.shape[0]
    lent = table - nodes
    half = lent // 2

    loads = {}
    loaded = [0]

    def load(key, *pairs):
        copies = []
        for src, dst in pairs:
            copy = pltpu.make_async_copy(src, dst, v.load_sem.at[loaded[0]])
            loaded[0] += 1
            copy.start()
            copies.append(copy)
        loads[key] = copies

    def arrive(key):
        for copy in loads.pop(key, ()):
            copy.wait()

    load("states", (v.states_hbm.at[0], v.states_v), (v.send_hbm, v.pick_v))

    barrier = pltpu.get_barrier_semaphore()
    others = [before, after, core_peer, x_peer, y_peer] + [z_peer(lax.rem(z + d, 4)) for d in range(1, 4)]
    others += [z_x_peer(lax.rem(z + d, 4)) for d in range(1, 4)]
    for other in others:
        pl.semaphore_signal(barrier, inc=1, device_id=other, device_id_type=MESH)

    load("cond1", (v.noise_hbm, v.noise_v), (v.w_cond_hbm.at[:, 0 : 2 * width], v.w_cond_v.at[0]))
    load("qkv", (v.w_qkv_hbm, v.w_qkv_v))

    def tile(ref, t):
        return ref[:, t * width : (t + 1) * width]

    numbers, _ = receive_plan()
    outgoing = {n: n for n in range(len(UNITS))}
    for name in ("m0", "m1", "halo", "back"):
        outgoing[name] = len(outgoing)

    def message(n, src, dst, target, receive):
        return Message(v, outgoing[n], numbers.get((n, receive), receive), src, dst, target)

    def send(n, src, dst, target, receive):
        copy = message(n, src, dst, target, receive)
        copy.start()
        return copy

    def all_left(n, ref):
        message(n, ref, ref, x_peer, 0).leave()

    arrive("states")
    normed1, inv1 = layer_norm(v.states_v[...])
    v.normed1_v[...] = normed1
    pick = (v.pick_v[...] == lax.broadcasted_iota(jnp.int32, (nodes, lent), 0)).astype(BF16)
    v.lend_v[...] = dot_tn(pick, normed1.astype(BF16)).astype(BF16)
    pl.semaphore_wait(barrier, len(others))
    halo = [
        send("halo", v.lend_v.at[0:half], v.halo_v.at[half:lent], before, 0),
        send("halo", v.lend_v.at[half:lent], v.halo_v.at[0:half], after, 1),
    ]

    load("index", (v.neighbours_hbm, v.neighbours_v), (v.valid_hbm, v.valid_v))
    load("cond2", (v.w_cond_hbm.at[:, 2 * width : 4 * width], v.w_cond_v.at[1]))
    load("out", (v.w_out_hbm, v.w_out_v))
    load("up", (v.w_up_hbm, v.w_up_v))
    load("down", (v.cot_hbm.at[0], v.cot_v), (v.w_down_hbm, v.w_down_v))

    arrive("cond1")
    condition = v.noise_v[pl.ds(r, 1), :]
    row = lax.broadcasted_iota(jnp.int32, (16, width), 0)
    high, mid, low = split3(condition)
    stacked = jnp.where(row == 0, high, jnp.where(row == 1, mid, jnp.where(row == 2, low, 0.0))).astype(BF16)
    mod1 = jnp.sum(dot(stacked, v.w_cond_v[0]), axis=0, keepdims=True)
    scale1, shift1 = mod1[:, :width], mod1[:, width:]
    hidden1 = (v.normed1_v[...] * (1.0 + scale1) + shift1).astype(BF16)
    v.table_v[0:nodes, :] = hidden1

    arrive("qkv")
    v.k_v[0:nodes, :] = dot(hidden1, tile(v.w_qkv_v, 1)).astype(BF16)
    v.v_v[0:nodes, :] = dot(hidden1, tile(v.w_qkv_v, 2)).astype(BF16)
    v.q_v[...] = dot(hidden1, tile(v.w_qkv_v, 0)).astype(BF16)

    arrive("index")
    entry = lax.broadcasted_iota(jnp.int32, (table, nodes), 0)
    count = jnp.zeros((table, nodes), F32)
    for j in range(v.neighbours_v.shape[0]):
        count = count + (v.neighbours_v[j : j + 1, :] == entry).astype(F32)
    v.count_v[...] = count

    arrive("cond2")
    mod2 = jnp.sum(dot(stacked, v.w_cond_v[1]), axis=0, keepdims=True)
    scale2, shift2 = mod2[:, :width], mod2[:, width:]
    real = jnp.sum(v.valid_v[...], axis=1, keepdims=True)
    mask = (lax.broadcasted_iota(jnp.int32, (nodes, 1), 0) < real).astype(F32)

    for copy in halo:
        copy.arrive()
    rows = (v.halo_v[...].astype(F32) * (1.0 + scale1) + shift1).astype(BF16)
    v.table_v[nodes:table, :] = rows
    v.k_v[nodes:table, :] = dot(rows, tile(v.w_qkv_v, 1)).astype(BF16)
    v.v_v[nodes:table, :] = dot(rows, tile(v.w_qkv_v, 2)).astype(BF16)

    for h in range(HEADS):
        cols = slice(h * head, (h + 1) * head)
        scores = dot_nt(v.k_v[:, cols], v.q_v[:, cols]) * factor
        times = v.count_v[...]
        scores = jnp.where(times > 0.0, scores, -1e30)
        exponent = times * jnp.exp(scores - jnp.max(scores, axis=0, keepdims=True))
        attn = exponent * (1.0 / jnp.sum(exponent, axis=0, keepdims=True))
        v.attn_v[h] = attn
        v.mix_v[:, cols] = dot_tn(attn.astype(BF16), v.v_v[:, cols]).astype(BF16)

    arrive("out")
    middle = v.states_v[...] + mask * dot(v.mix_v[...], v.w_out_v[...])
    v.middle_v[...] = middle
    normed2, inv2 = layer_norm(middle)
    v.normed2_v[...] = normed2
    v.hidden2_v[...] = (normed2 * (1.0 + scale2) + shift2).astype(BF16)

    def exchange_z(own, name, n):
        triple, single, middle_in, comb = (
            getattr(v, name + "_triple"),
            getattr(v, name + "_single"),
            getattr(v, name + "_middle"),
            getattr(v, name + "_comb"),
        )
        outer = (z == 0) | (z == 3)
        outer_z = jnp.where(z < 2, 0, 3)
        other_inner = jnp.where(z < 2, 2, 1)
        other_outer = 3 - outer_z
        near_inner = jnp.where(z < 2, 1, 2)
        first = jnp.where(z == 0, 1, 0)
        offset = jnp.where(z == 1, 1, 0)
        to_inner = message(n, own.at[pl.ds(first, 3)], triple, z_peer(near_inner), "first")
        to_outer = message(n, own.at[outer_z], single, z_peer(outer_z), "first")
        across = message(n, comb.at[0], middle_in, z_peer(other_inner), "middle")
        beyond = message(n, comb.at[1], middle_in, z_peer(other_outer), "middle")

        def begin():
            @pl.when(outer)
            def _():
                to_inner.start()

            @pl.when(jnp.logical_not(outer))
            def _():
                to_outer.start()

        def combine():
            @pl.when(jnp.logical_not(outer))
            def _():
                to_inner.arrive()
                comb[1] = own[other_outer] + triple[other_outer - offset]
                beyond.start()
                comb[0] = own[other_inner] + triple[other_inner - offset]
                across.start()

        def finish_sum(result):
            across.arrive()

            @pl.when(outer)
            def _():
                to_outer.arrive()
                total = own[z].astype(F32) + single[...].astype(F32) + middle_in[...].astype(F32)
                result[...] = total.astype(BF16)

            @pl.when(jnp.logical_not(outer))
            def _():
                total = own[z].astype(F32) + triple[z - offset].astype(F32) + middle_in[...].astype(F32)
                result[...] = total.astype(BF16)

        return begin, combine, finish_sum

    def direct_z(own, name, n):
        landing = getattr(v, name + "_landing")

        def begin():
            for d in range(1, 4):
                there = lax.rem(z + d, 4)
                send(n, own.at[there], landing.at[d - 1], z_peer(there), "z")

        def finish_sum(result):
            message(n, landing, landing, x_peer, "z").arrive()
            total = own[z].astype(F32)
            for d in range(3):
                total = total + landing[d].astype(F32)
            result[...] = total.astype(BF16)

        return begin, finish_sum

    queue = {}
    core_copies = {}

    def place(n, value, part=None):
        kind, where, start, wide, _ = UNITS[n]
        rows = value.shape[0]

        def at(first):
            return pl.ds(first if part is None else pl.multiple_of(first + part * rows, rows), rows)

        if kind == "d":
            for b in range(wide // 128):
                block = value[:, b * 128 : (b + 1) * 128]
                v.down_v[at((start // 128 + b) * 32), where * 128 : (where + 1) * 128] = block
        elif kind == "u":
            first = where * width + start
            v.up_v[at(0), first : first + wide] = value
        elif kind == "o":
            v.o_v[at(0), start : start + wide] = value
        else:
            for b in range(wide // 128):
                first = (start // 128 + b) * width + where * 128
                v.qkv_v[at(0), first : first + 128] = value[:, b * 128 : (b + 1) * 128]

    def unit_steps(n):
        name, flow = "u%d" % n, UNITS[n][4]
        grad, landed, mine = (getattr(v, name + suffix) for suffix in ("_grad", "_core", "_mine"))
        result, received = getattr(v, name + "_result"), getattr(v, name + "_received")
        direct = flow[1:] == "d"
        copies = {}

        def core_sum():
            core_copies[n].arrive()
            total = grad[:, :, c] + landed[...]
            mine[...] = total.reshape(mine.shape)

        def y_exchange():
            copies["last"] = send(n, result, received, y_peer, "y")

        def ending():
            copies["last"].arrive()
            if flow[0] == "C":
                place(n, result[...].astype(F32), r)
                place(n, received[...].astype(F32), 1 - r)
            else:
                place(n, result[...].astype(F32) + received[...].astype(F32))

        def reduce_z(own, then):
            if direct:
                begin, finish_sum = direct_z(own, name, n)
                middle_steps = []
            else:
                begin, combine, finish_sum = exchange_z(own, name, n)
                middle_steps = [combine]

            def last():
                finish_sum(then[0])
                then[1]()

            return begin, middle_steps + [last]

        if flow[0] == "G":
            plane = getattr(v, name + "_plane")

            def start():
                core_sum()
                for d in range(1, 8):
                    there = lax.rem(z + d // 2, 4)
                    target = z_peer(there) if d % 2 == 0 else z_x_peer(there)
                    send(n, mine.at[there, x if d % 2 == 0 else 1 - x], plane.at[d - 1], target, "plane")
                copies["plane"] = message(n, plane, plane, x_peer, "plane")

            def second():
                copies["plane"].arrive()
                total = mine[z, x].astype(F32)
                for d in range(7):
                    total = total + plane[d].astype(F32)
                result[...] = total.astype(BF16)
                y_exchange()

            return [start, second, ending]
        if flow[0] == "A":
            from_x = getattr(v, name + "_x")
            begin, rest = reduce_z(from_x, (result, y_exchange))

            def start():
                core_sum()
                copies["x"] = send(n, mine.at[:, 1 - x], from_x, x_peer, "x")

            def second():
                copies["x"].arrive()
                from_x[...] = mine[:, x] + from_x[...]
                begin()

            return [start, second] + rest + [ending]
        if flow[0] == "C":
            from_y, from_x = getattr(v, name + "_y"), getattr(v, name + "_x")
            begin, rest = reduce_z(from_x, (result, y_exchange))

            def start():
                core_sum()
                copies["y"] = send(n, mine.at[:, :, 1 - r], from_y, y_peer, "early y")

            def second():
                copies["y"].arrive()
                from_y[...] = mine[:, :, r] + from_y[...]
                copies["x"] = send(n, from_y.at[:, 1 - x], from_x, x_peer, "x")

            def third():
                copies["x"].arrive()
                from_x[...] = from_y[:, x] + from_x[...]
                begin()

            return [start, second, third] + rest + [ending]
        pair, from_x = getattr(v, name + "_pair"), getattr(v, name + "_x")

        def x_exchange():
            copies["x"] = send(n, pair.at[1 - x], from_x, x_peer, "x")

        begin, rest = reduce_z(mine, (pair, x_exchange))

        def start():
            core_sum()
            begin()

        def after_x():
            copies["x"].arrive()
            result[...] = pair[x] + from_x[...]
            y_exchange()

        return [start] + rest + [after_x, ending]

    def produce(kind, where, piece):
        for n, (its_kind, its_where, start, wide, _) in enumerate(UNITS):
            if (its_kind, its_where) == (kind, where):
                grad = getattr(v, "u%d_grad" % n)
                for b in range(0, wide, 128):
                    grad[..., b : b + 128] = piece(start + b).reshape(4, 2, 2, 32, 128)
                landed = getattr(v, "u%d_core" % n)
                core_copies[n] = send(n, grad.at[:, :, 1 - c], landed, core_peer, "core")
                queue[n] = unit_steps(n)

    def section_up(t):
        arrive("up")
        cols = slice(t * width, (t + 1) * width)
        up = dot(v.hidden2_v[...], v.w_up_v[:, cols])
        v.up_proj_v[:, cols] = up
        v.activation_v[:, cols] = (up * (1.0 / (1.0 + jnp.exp(-up)))).astype(BF16)

    def section_mask():
        arrive("down")
        v.d_branch_v[...] = (mask * v.cot_v[...]).astype(BF16)

    def section_dup(t):
        cols = slice(t * width, (t + 1) * width)
        up = v.up_proj_v[:, cols]
        sigmoid = 1.0 / (1.0 + jnp.exp(-up))
        d_act = dot_nt(v.d_branch_v[...], v.w_down_v[t * width : (t + 1) * width, :])
        v.d_up_v[:, cols] = (d_act * sigmoid * (1.0 + up * (1.0 - sigmoid))).astype(BF16)

    def section_gd(h):
        value = dot_tn(v.activation_v[...], v.d_branch_v[:, h * 256 : (h + 1) * 256]).astype(BF16)
        value = value.reshape(GROUP, 4, 32, 256)
        for k in range(2):
            produce("d", 2 * h + k, lambda start: value[:, start // 128, :, k * 128 : (k + 1) * 128])

    def section_gu(t):
        value = dot_tn(v.hidden2_v[...], v.d_up_v[:, t * width : (t + 1) * width]).astype(BF16)
        produce("u", t, lambda start: value[:, start : start + 128])

    def section_out():
        branch = dot(v.activation_v[:, 0:width], v.w_down_v[0:width, :])
        for t in range(1, tiles):
            branch = branch + dot(v.activation_v[:, t * width : (t + 1) * width], v.w_down_v[t * width : (t + 1) * width, :])
        v.out_v[0] = v.middle_v[...] + mask * branch

    def section_mid():
        d_hidden2 = dot_nt(v.d_up_v[:, 0:width], tile(v.w_up_v, 0))
        for t in range(1, tiles):
            d_hidden2 = d_hidden2 + dot_nt(v.d_up_v[:, t * width : (t + 1) * width], tile(v.w_up_v, t))
        normed2 = v.normed2_v[...]
        v.mod_v[1, :, 0:width] = jnp.sum(d_hidden2 * normed2, axis=0, keepdims=True)
        v.mod_v[1, :, width : 2 * width] = jnp.sum(d_hidden2, axis=0, keepdims=True)
        queue["m1"] = mod_steps(1)
        d_middle = v.cot_v[...] + norm_back(d_hidden2 * (1.0 + scale2), normed2, inv2)
        v.d_middle_v[...] = d_middle
        v.d_attended_v[...] = (mask * d_middle).astype(BF16)
        v.d_mix_v[...] = dot_nt(v.d_attended_v[...], v.w_out_v[...]).astype(BF16)

    def section_go():
        value = dot_tn(v.mix_v[...], v.d_attended_v[...]).astype(BF16)
        produce("o", 0, lambda start: value[:, start : start + 128])

    def section_attn(h):
        cols = slice(h * head, (h + 1) * head)
        attn = v.attn_v[h]
        d_attn = dot_nt(v.v_v[:, cols], v.d_mix_v[:, cols])
        inner = jnp.sum(attn * d_attn, axis=0, keepdims=True)
        d_scores = (attn * (d_attn - inner)).astype(BF16)
        v.d_q_v[:, cols] = (dot_tn(d_scores, v.k_v[:, cols]) * factor).astype(BF16)
        v.d_k_v[:, cols] = (dot(d_scores, v.q_v[:, cols]) * factor).astype(BF16)
        v.d_v_v[:, cols] = dot(attn.astype(BF16), v.d_mix_v[:, cols]).astype(BF16)

    def section_gq(h):
        cols = slice(h * head, (h + 1) * head)
        values = [
            dot_tn(v.table_v[0:nodes, :], v.d_q_v[:, cols]).astype(BF16),
            dot_tn(v.table_v[...], v.d_k_v[:, cols]).astype(BF16),
            dot_tn(v.table_v[...], v.d_v_v[:, cols]).astype(BF16),
        ]
        produce("h", h, lambda start: values[start // 128])

    back = []

    def section_table():
        d_table = dot_nt(v.d_k_v[...], tile(v.w_qkv_v, 1)) + dot_nt(v.d_v_v[...], tile(v.w_qkv_v, 2))
        v.lend_back_v[...] = d_table[nodes:table, :].astype(BF16)
        back.append(send("back", v.lend_back_v.at[0:half], v.returned_v.at[half:lent], before, 2))
        back.append(send("back", v.lend_back_v.at[half:lent], v.returned_v.at[0:half], after, 3))
        d_hidden1 = d_table[0:nodes, :] + dot_nt(v.d_q_v[...], tile(v.w_qkv_v, 0))
        v.d_hidden1_v[...] = d_hidden1
        d_lent = d_table[nodes:table, :]
        v.mod_v[0, :, 0:width] = jnp.sum(d_hidden1 * v.normed1_v[...], axis=0, keepdims=True) + jnp.sum(
            d_lent * v.halo_v[...].astype(F32), axis=0, keepdims=True
        )
        v.mod_v[0, :, width : 2 * width] = jnp.sum(d_hidden1, axis=0, keepdims=True) + jnp.sum(
            d_lent, axis=0, keepdims=True
        )
        queue["m0"] = mod_steps(0)

    def section_state():
        for copy in back:
            copy.arrive()
        d_hidden1 = v.d_hidden1_v[...] + dot(pick, v.returned_v[...])
        normed1 = v.normed1_v[...]
        v.d_states_v[0] = v.d_middle_v[...] + norm_back(d_hidden1 * (1.0 + scale1), normed1, inv1)

    def mod_steps(part):
        own, from_core, plane, rows = v.mod_v.at[part], v.mod_core_v.at[part], v.mods_v.at[part], v.rows_v.at[part]
        name = "m%d" % part
        copies = [send(name, own, from_core, core_peer, "core")]

        def spread():
            copies.pop().arrive()
            plane[0] = own[...] + from_core[...]
            for d in range(1, 8):
                there = lax.rem(z + d // 2, 4)
                target = z_peer(there) if d % 2 == 0 else z_x_peer(there)
                send(name, plane.at[0], plane.at[d], target, "plane")
            copies.append(message(name, plane.at[pl.ds(1, 7)], plane.at[pl.ds(1, 7)], x_peer, "plane"))

        def swap():
            copies.pop().arrive()
            total = jnp.zeros(own.shape, F32)
            for there in range(4):
                for side in range(2):
                    total = total + plane[lax.rem(z + 4 - there, 4) * 2 + lax.rem(x + side, 2)]
            rows[r] = total
            copies.append(send(name, rows.at[r], rows.at[r], y_peer, "y"))

        def spend():
            copies.pop().arrive()
            first_row, second_row = rows[0], rows[1]
            here = slice(part * 2 * width, (part + 1) * 2 * width)
            if not finish:
                v.d_noise_v[0:1, here] = first_row
                v.d_noise_v[1:2, here] = second_row
                return
            row = lax.broadcasted_iota(jnp.int32, (16, 2 * width), 0)
            stacked = jnp.zeros((16, 2 * width), F32)
            for number, piece in enumerate(split3(first_row) + split3(second_row)):
                stacked = jnp.where(row == number, piece, stacked)
            noise = dot_nt(stacked.astype(BF16), v.w_cond_v[part])
            first_noise = jnp.sum(noise[0:3], axis=0, keepdims=True)
            second_noise = jnp.sum(noise[3:6], axis=0, keepdims=True)
            if part == 1:
                v.noise_part_v[0:1, :] = first_noise
                v.noise_part_v[1:2, :] = second_noise
            else:
                v.d_noise_v[0:1, :] = first_noise + v.noise_part_v[0:1, :]
                v.d_noise_v[1:2, :] = second_noise + v.noise_part_v[1:2, :]
            shape = (v.d_cond_v.shape[0], width)
            mine = lax.broadcasted_iota(jnp.int32, shape, 1) == (
                lax.broadcasted_iota(jnp.int32, shape, 0) + p * shape[0]
            )
            picked = [
                jnp.sum(jnp.where(mine, v.noise_v[b : b + 1, :], 0.0), axis=1, keepdims=True)
                for b in range(2)
            ]
            v.d_cond_v[:, here] = picked[0] * first_row + picked[1] * second_row

        return [spread, swap, spend]

    sections = {
        "up": section_up,
        "mask": section_mask,
        "dup": section_dup,
        "gd": section_gd,
        "gu": section_gu,
        "out": section_out,
        "mid": section_mid,
        "go": section_go,
        "attn": section_attn,
        "gq": section_gq,
        "table": section_table,
        "state": section_state,
    }
    for entry in ORDER:
        if entry in queue:
            queue[entry].pop(0)()
        elif isinstance(entry, tuple):
            sections[entry[0]](entry[1])
        else:
            sections[entry]()
    for steps in queue.values():
        for step in steps:
            step()

    for n in range(len(UNITS)):
        all_left(n, getattr(v, "u%d_grad" % n))
    for part in range(2):
        all_left("m%d" % part, v.mods_v.at[part])
    all_left("halo", v.lend_v)
    all_left("back", v.lend_back_v)


def copy_out(count, *refs):
    for n in range(count):
        src, dst = refs[n], refs[count + n]
        rows = src.shape[-2]
        pieces = 4 if rows % 64 == 0 else 1
        for k in range(pieces):
            at = (*[slice(None)] * (len(src.shape) - 2), slice(k * rows // pieces, (k + 1) * rows // pieces))
            pltpu.make_async_copy(src.at[at], dst.at[at], refs[-1].at[n]).start()
    for n in range(count):
        pltpu.make_async_copy(refs[n], refs[count + n], refs[-1].at[n]).wait()


def body(
    node_state,
    noise_embed,
    w_cond,
    w_qkv,
    w_out,
    w_up,
    w_down,
    neighbours,
    send_rows,
    valid,
    cotangent,
):
    nodes, width = node_state.shape[1:]
    hidden = w_up.shape[1]
    lent = send_rows.shape[0]
    table = nodes + lent
    patches = lax.axis_size("patch")
    fold = patches // GROUP
    rows_each = width // patches
    block = width // GROUP
    half = width // 2

    hbm = pl.BlockSpec(memory_space=pl.ANY)
    vmem = pl.BlockSpec(memory_space=pltpu.VMEM)
    inputs = [
        ("states_hbm", node_state, hbm),
        ("noise_hbm", noise_embed, hbm),
        ("w_cond_hbm", w_cond, hbm),
        ("w_qkv_hbm", w_qkv, hbm),
        ("w_out_hbm", w_out, hbm),
        ("w_up_hbm", w_up, hbm),
        ("w_down_hbm", w_down, hbm),
        ("neighbours_hbm", neighbours.T, hbm),
        ("send_hbm", send_rows[None, :], hbm),
        ("valid_hbm", valid[None, :], hbm),
        ("cot_hbm", cotangent, hbm),
    ]
    outputs = [
        ("out_v", node_state.shape, vmem),
        ("d_states_v", node_state.shape, vmem),
        ("down_v", (hidden // GROUP, width), vmem),
        ("up_v", (block, hidden), vmem),
        ("o_v", (block, width), vmem),
        ("qkv_v", (block, 3 * width), vmem),
    ]
    if fold == 1:
        outputs += [("d_noise_v", noise_embed.shape, vmem), ("d_cond_v", (rows_each, 4 * width), vmem)]
    else:
        outputs += [("d_noise_v", (noise_embed.shape[0], 4 * width), vmem)]
    tiles = hidden // width
    receivers = receive_plan()[1]
    scratch = [
        ("noise_v", noise_embed.shape, F32),
        ("neighbours_v", neighbours.shape[::-1], jnp.int32),
        ("pick_v", (1, lent), jnp.int32),
        ("valid_v", (1, nodes), jnp.int32),
        ("states_v", (nodes, width), F32),
        ("cot_v", (nodes, width), F32),
        ("w_cond_v", (2, width, 2 * width), BF16),
        ("w_qkv_v", w_qkv.shape, BF16),
        ("w_out_v", (width, width), BF16),
        ("w_up_v", w_up.shape, BF16),
        ("w_down_v", w_down.shape, BF16),
        ("normed1_v", (nodes, width), F32),
        ("table_v", (table, width), BF16),
        ("lend_v", (lent, width), BF16),
        ("halo_v", (lent, width), BF16),
        ("returned_v", (lent, width), BF16),
        ("q_v", (nodes, width), BF16),
        ("k_v", (table, width), BF16),
        ("v_v", (table, width), BF16),
        ("count_v", (table, nodes), F32),
        ("attn_v", (HEADS, table, nodes), F32),
        ("mix_v", (nodes, width), BF16),
        ("middle_v", (nodes, width), F32),
        ("normed2_v", (nodes, width), F32),
        ("hidden2_v", (nodes, width), BF16),
        ("d_branch_v", (nodes, width), BF16),
        ("d_mix_v", (nodes, width), BF16),
        ("d_q_v", (nodes, width), BF16),
        ("d_k_v", (table, width), BF16),
        ("d_v_v", (table, width), BF16),
        ("mod_v", (2, 1, 2 * width), F32),
        ("mod_core_v", (2, 1, 2 * width), F32),
        ("mods_v", (2, 9, 1, 2 * width), F32),
        ("rows_v", (2, 2, 1, 2 * width), F32),
        ("noise_part_v", noise_embed.shape, F32),
        ("up_proj_v", (nodes, hidden), F32),
        ("activation_v", (nodes, hidden), BF16),
        ("d_up_v", (nodes, hidden), BF16),
        ("d_middle_v", (nodes, width), F32),
        ("d_attended_v", (nodes, width), BF16),
        ("d_hidden1_v", (nodes, width), F32),
        ("lend_back_v", (lent, width), BF16),
    ]
    for n, (_, _, _, wide, flow) in enumerate(UNITS):
        name = "u%d" % n
        rows = 16 if flow[0] == "C" else 32
        part = (2, 32, wide) if flow[0] == "B" else (rows, wide)
        buffers = [("_grad", (4, 2, 2, 32, wide)), ("_core", (4, 2, 32, wide))]
        buffers += [("_mine", (4, 2, 2, 16, wide) if flow[0] == "C" else (4, 2, 32, wide))]
        buffers += [("_result", (rows, wide)), ("_received", (rows, wide))]
        if flow[0] == "G":
            buffers += [("_plane", (7, rows, wide))]
        else:
            buffers += [("_x", (rows, wide) if flow[0] == "B" else (4, rows, wide))]
            if flow[0] == "C":
                buffers += [("_y", (4, 2, 16, wide))]
            if flow[0] == "B":
                buffers += [("_pair", part)]
            if flow[1:] == "d":
                buffers += [("_landing", (3, *part))]
            else:
                buffers += [("_triple", (3, *part)), ("_single", part), ("_middle", part), ("_comb", (2, *part))]
        scratch += [(name + suffix, shape, BF16) for suffix, shape in buffers]
    semaphores = [
        ("load_sem", pltpu.SemaphoreType.DMA((12,))),
        ("send_sem", pltpu.SemaphoreType.DMA((len(UNITS) + 4,))),
        ("recv_sem", pltpu.SemaphoreType.DMA((receivers,))),
    ]
    names = [n for group in (inputs, outputs, scratch, semaphores) for n in [e[0] for e in group]]
    results = pl.pallas_call(
        functools.partial(kernel, fold, patches, names),
        out_shape=[pltpu.VMEM(shape, F32) for _, shape, _ in outputs],
        in_specs=[spec for _, _, spec in inputs],
        out_specs=[spec for _, _, spec in outputs],
        scratch_shapes=[pltpu.VMEM(shape, dtype) for _, shape, dtype in scratch]
        + [sem for _, sem in semaphores],
        compiler_params=pltpu.CompilerParams(
            collective_id=0, has_side_effects=True, vmem_limit_bytes=44 * 1024 * 1024
        ),
    )(
        *[pltpu.with_memory_space_constraint(array, pltpu.HBM) for _, array, _ in inputs]
    )
    if fold == 1:
        results = pl.pallas_call(
            functools.partial(copy_out, len(results)),
            out_shape=[jax.ShapeDtypeStruct(a.shape, a.dtype) for a in results],
            in_specs=[hbm] * len(results),
            out_specs=[hbm] * len(results),
            scratch_shapes=[pltpu.SemaphoreType.DMA((len(results),))],
            compiler_params=pltpu.CompilerParams(vmem_limit_bytes=1024 * 1024),
        )(*results)
    output, d_state, g_down, g_up, g_out, g_qkv = results[:6]
    if fold == 1:
        grad_noise, grad_cond = results[6:]
    else:
        groups = [[m * fold + i for i in range(fold)] for m in range(GROUP)]

        def rest(array):
            return lax.psum_scatter(
                array, "patch", scatter_dimension=0, axis_index_groups=groups, tiled=True
            )

        g_down, g_up, g_out, g_qkv = rest(g_down), rest(g_up), rest(g_out), rest(g_qkv)
        mods = lax.psum(results[6], "patch") / GROUP
        highest = lax.Precision.HIGHEST
        grad_noise = jnp.dot(mods, w_cond.astype(F32).T, precision=highest)
        first_row = lax.axis_index("patch") * rows_each
        cond_cols = lax.dynamic_slice_in_dim(noise_embed, first_row, rows_each, 1)
        grad_cond = jnp.dot(cond_cols.T, mods, precision=highest)
    return output, d_state, grad_noise, grad_cond, g_qkv, g_out, g_up, g_down


def solution(mesh):
    in_specs = (
        P("rep", "patch", None),
        P(),
        P(),
        P(),
        P(),
        P(),
        P(),
        P("patch", None),
        P("patch"),
        P("patch"),
        P("rep", "patch", None),
    )
    out_specs = (
        P("rep", "patch", None),
        P("rep", "patch", None),
        P(),
        P("patch", None),
        P("patch", None),
        P("patch", None),
        P("patch", None),
        P("patch", None),
    )
    return jax.shard_map(body, mesh=mesh, in_specs=in_specs, out_specs=out_specs, check_vma=False)
```

```python
import functools

import jax
import jax.numpy as jnp
from jax import lax
from jax.experimental import pallas as pl
from jax.experimental.pallas import tpu as pltpu
from jax.sharding import PartitionSpec as P

HEADS = 4
GROUP = 16
UNITS = (
    ("d", 0, 0, 512, "C"), ("d", 1, 0, 256, "B"), ("d", 1, 256, 256, "Ad"), ("d", 2, 0, 256, "C"),
    ("d", 2, 256, 256, "A"), ("d", 3, 0, 256, "B"), ("d", 3, 256, 256, "A"), ("u", 0, 0, 512, "A"),
    ("u", 1, 0, 512, "Cd"), ("u", 2, 0, 256, "B"), ("u", 2, 256, 256, "A"), ("u", 3, 0, 512, "Cd"),
    ("o", 0, 0, 256, "Cd"), ("o", 0, 256, 256, "A"), ("h", 0, 0, 128, "C"),
    ("h", 0, 128, 256, "Cd"), ("h", 1, 0, 384, "Cd"), ("h", 2, 0, 128, "Cd"),
    ("h", 2, 128, 256, "C"), ("h", 3, 0, 128, "C"), ("h", 3, 128, 256, "B"),
)
ORDER = (
    "mask", ("up", 2), ("dup", 2), ("gu", 2), ("up", 3), ("up", 0), ("up", 1), ("gd", 1),
    ("dup", 0), 9, 10, ("dup", 1), ("gu", 1), ("gu", 0), 3, ("dup", 3), 4, 5, "mid", 8, 6,
    ("gd", 0), 7, ("gu", 3), ("attn", 0), "m1", 10, ("attn", 1), 9, ("attn", 2), 3, 1, 0, 4, 2,
    ("gq", 1), 11, ("attn", 3), 5, ("gq", 2), 6, ("gq", 3), "table", 16, 8, ("gq", 0), 10, 18, 19,
    20, "go", 9, "m0", 7, 14, 15, 1, 0, 12, 13, 3, 5, "m1", 4, 2, 17, 10, 6, 11, 8, "state", 1,
    "out", 20, 4, 9, 16, 0, "m0", 18, 6, 7, 13, 19, 5, 14, 3, 11, 15, 1, 20, 2, 16, 12, "m1", 8, 7,
    0, 18, 17, 19, 3, 14, 10, 13, 4, 15, 9, "m0", 20, 6, 5, 12, 1, 2, 11, 17, 8, 18, 0, 19, 7, 16,
    14, 3, 13, 20, 15, 11, 0, 12, 18, 16, 19, 17, 14, 13, 15, 12, 18, 19, 17, 14,
)
MESH = pl.DeviceIdType.MESH
F32 = jnp.float32
BF16 = jnp.bfloat16


def dot(a, b):
    return lax.dot_general(a, b, (((1,), (0,)), ((), ())), preferred_element_type=F32)


def dot_nt(a, b):
    return lax.dot_general(a, b, (((1,), (1,)), ((), ())), preferred_element_type=F32)


def dot_tn(a, b):
    return lax.dot_general(a, b, (((0,), (0,)), ((), ())), preferred_element_type=F32)


def split3(v):
    high = v.astype(BF16)
    rest = v - high.astype(F32)
    mid = rest.astype(BF16)
    low = (rest - mid.astype(F32)).astype(BF16)
    return high.astype(F32), mid.astype(F32), low.astype(F32)


def layer_norm(values):
    centred = values - jnp.mean(values, axis=-1, keepdims=True)
    inv_std = lax.rsqrt(jnp.mean(centred * centred, axis=-1, keepdims=True) + 1e-05)
    return centred * inv_std, inv_std


def norm_back(gradient, normed, inv_std):
    first = jnp.mean(gradient, axis=-1, keepdims=True)
    second = jnp.mean(gradient * normed, axis=-1, keepdims=True)
    return (gradient - first - normed * second) * inv_std


ROUTES = {
    "A": (("core", -1, 0), ("x", 0, 1), ("first", 1, 3), ("middle", 2, 3), ("y", 3, 4)),
    "Ad": (("core", -1, 0), ("x", 0, 1), ("z", 1, 2), ("y", 2, 3)),
    "B": (("core", -1, 0), ("first", 0, 2), ("middle", 1, 2), ("x", 2, 3), ("y", 3, 4)),
    "Bd": (("core", -1, 0), ("z", 0, 1), ("x", 1, 2), ("y", 2, 3)),
    "C": (("core", -1, 0), ("early y", 0, 1), ("x", 1, 2), ("first", 2, 4), ("middle", 3, 4), ("y", 4, 5)),
    "Cd": (("core", -1, 0), ("early y", 0, 1), ("x", 1, 2), ("z", 2, 3), ("y", 3, 4)),
    "G": (("core", -1, 0), ("plane", 0, 1), ("y", 1, 2)),
    "M": (("core", -1, 0), ("plane", 0, 1), ("y", 1, 2)),
}
SOURCE = {"d": lambda w: ("gd", w // 2), "u": lambda w: ("gu", w), "o": lambda w: "go", "h": lambda w: ("gq", w)}


def receive_plan():
    steps = {}
    for position, entry in enumerate(ORDER):
        steps.setdefault(entry, []).append(position)
    copies = []
    for n, (kind, where, _, _, route) in enumerate(UNITS):
        copies += [(n, steps[SOURCE[kind](where)][0], *copy) for copy in ROUTES[route]]
    for name, source in (("m1", "mid"), ("m0", "table")):
        copies += [(name, steps[source][0], *copy) for copy in ROUTES["M"]]
    timed = []
    for n, start, what, sender, waiter in copies:
        timed.append((start if sender < 0 else steps[n][sender], steps[n][waiter], what, n))
    timed.sort(key=lambda copy: copy[0])
    kinds = {"early y": "y", "middle": "first"}

    def answered(send, kind, waited):
        return any(
            kinds.get(what, what) == kind and what != "middle" and waited <= sent and got <= send
            for sent, got, what, _ in timed
        )

    numbers, free = {}, [(-1, 0), (-1, 1)]
    count = 4
    for send, got, what, n in timed:
        kind = kinds.get(what, what)
        fit = [entry for entry in free if answered(send, kind, entry[0])]
        if fit:
            entry = max(fit)
            free.remove(entry)
            number = entry[1]
        else:
            number, count = count, count + 1
        numbers[n, what] = number
        free.append((got, number))
    return numbers, count


class Names:
    pass


class Message:
    def __init__(self, v, outgoing, receive, src, dst, target):
        self.parts = dict(
            src_ref=src,
            dst_ref=dst,
            send_sem=v.send_sem.at[outgoing],
            recv_sem=v.recv_sem.at[receive],
            device_id=target,
            device_id_type=MESH,
        )

    def start(self):
        pltpu.make_async_remote_copy(**self.parts).start()

    def arrive(self):
        pltpu.make_async_remote_copy(**self.parts).wait_recv()

    def leave(self):
        pltpu.make_async_remote_copy(**self.parts).wait_send()


def kernel(fold, patches, names, *refs):
    v = Names()
    for name, ref in zip(names, refs):
        setattr(v, name, ref)
    p = lax.axis_index("patch")
    r = lax.axis_index("rep")
    member = p // fold
    lane = lax.rem(p, fold)
    c = lax.rem(member, 2)
    x = lax.rem(member // 2, 2)
    z = member // 4
    finish = fold == 1

    def device(index, rep=r):
        return (index * fold + lane, rep)

    before = (lax.rem(p + patches - 1, patches), r)
    after = (lax.rem(p + 1, patches), r)
    core_peer = device(member + 1 - 2 * c)
    x_peer = device(member + 2 - 4 * x)
    y_peer = (p, 1 - r)

    def z_peer(there):
        return device(there * 4 + x * 2 + c)

    def z_x_peer(there):
        return device(there * 4 + (1 - x) * 2 + c)

    nodes, width = v.states_hbm.shape[1:]
    tiles = v.w_up_hbm.shape[1] // width
    head = width // HEADS
    factor = head ** (-0.5)
    table = v.k_v.shape[0]
    lent = table - nodes
    half = lent // 2

    loads = {}
    loaded = [0]

    def load(key, *pairs):
        copies = []
        for src, dst in pairs:
            copy = pltpu.make_async_copy(src, dst, v.load_sem.at[loaded[0]])
            loaded[0] += 1
            copy.start()
            copies.append(copy)
        loads[key] = copies

    def arrive(key):
        for copy in loads.pop(key, ()):
            copy.wait()

    load("states", (v.states_hbm.at[0], v.states_v), (v.send_hbm, v.pick_v))

    barrier = pltpu.get_barrier_semaphore()
    others = [before, after, core_peer, x_peer, y_peer] + [z_peer(lax.rem(z + d, 4)) for d in range(1, 4)]
    others += [z_x_peer(lax.rem(z + d, 4)) for d in range(1, 4)]
    for other in others:
        pl.semaphore_signal(barrier, inc=1, device_id=other, device_id_type=MESH)

    load("cond1", (v.noise_hbm, v.noise_v), (v.w_cond_hbm.at[:, 0 : 2 * width], v.w_cond_v.at[0]))
    load("index", (v.neighbours_hbm, v.neighbours_v), (v.valid_hbm, v.valid_v))
    load("qkv", (v.w_qkv_hbm, v.w_qkv_v))
    load("cond2", (v.w_cond_hbm.at[:, 2 * width : 4 * width], v.w_cond_v.at[1]))

    def tile(ref, t):
        return ref[:, t * width : (t + 1) * width]

    numbers, _ = receive_plan()
    outgoing = {n: n for n in range(len(UNITS))}
    for name in ("m0", "m1", "halo", "back"):
        outgoing[name] = len(outgoing)

    def message(n, src, dst, target, receive):
        return Message(v, outgoing[n], numbers.get((n, receive), receive), src, dst, target)

    def send(n, src, dst, target, receive):
        copy = message(n, src, dst, target, receive)
        copy.start()
        return copy

    def all_left(n, ref):
        message(n, ref, ref, x_peer, 0).leave()

    arrive("states")
    normed1, inv1 = layer_norm(v.states_v[...])
    v.normed1_v[...] = normed1
    pick = (v.pick_v[...] == lax.broadcasted_iota(jnp.int32, (nodes, lent), 0)).astype(BF16)
    v.lend_v[...] = dot_tn(pick, normed1.astype(BF16)).astype(BF16)
    pl.semaphore_wait(barrier, len(others))
    halo = [
        send("halo", v.lend_v.at[0:half], v.halo_v.at[half:lent], before, 0),
        send("halo", v.lend_v.at[half:lent], v.halo_v.at[0:half], after, 1),
    ]

    load("out", (v.w_out_hbm, v.w_out_v))
    load("up", (v.w_up_hbm, v.w_up_v))
    load("down", (v.cot_hbm.at[0], v.cot_v), (v.w_down_hbm, v.w_down_v))

    for key in ("cond1", "index", "qkv", "cond2"):
        arrive(key)
    condition = v.noise_v[pl.ds(r, 1), :]
    row = lax.broadcasted_iota(jnp.int32, (16, width), 0)
    high, mid, low = split3(condition)
    stacked = jnp.where(row == 0, high, jnp.where(row == 1, mid, jnp.where(row == 2, low, 0.0))).astype(BF16)
    mod1 = jnp.sum(dot(stacked, v.w_cond_v[0]), axis=0, keepdims=True)
    scale1, shift1 = mod1[:, :width], mod1[:, width:]
    hidden1 = (v.normed1_v[...] * (1.0 + scale1) + shift1).astype(BF16)
    v.table_v[0:nodes, :] = hidden1

    v.k_v[0:nodes, :] = dot(hidden1, tile(v.w_qkv_v, 1)).astype(BF16)
    v.v_v[0:nodes, :] = dot(hidden1, tile(v.w_qkv_v, 2)).astype(BF16)
    v.q_v[...] = dot(hidden1, tile(v.w_qkv_v, 0)).astype(BF16)

    entry = lax.broadcasted_iota(jnp.int32, (table, nodes), 0)
    count = jnp.zeros((table, nodes), F32)
    for j in range(v.neighbours_v.shape[0]):
        count = count + (v.neighbours_v[j : j + 1, :] == entry).astype(F32)
    v.count_v[...] = count

    mod2 = jnp.sum(dot(stacked, v.w_cond_v[1]), axis=0, keepdims=True)
    scale2, shift2 = mod2[:, :width], mod2[:, width:]
    real = jnp.sum(v.valid_v[...], axis=1, keepdims=True)
    mask = (lax.broadcasted_iota(jnp.int32, (nodes, 1), 0) < real).astype(F32)

    for copy in halo:
        copy.arrive()
    rows = (v.halo_v[...].astype(F32) * (1.0 + scale1) + shift1).astype(BF16)
    v.table_v[nodes:table, :] = rows
    v.k_v[nodes:table, :] = dot(rows, tile(v.w_qkv_v, 1)).astype(BF16)
    v.v_v[nodes:table, :] = dot(rows, tile(v.w_qkv_v, 2)).astype(BF16)

    for h in range(HEADS):
        cols = slice(h * head, (h + 1) * head)
        scores = dot_nt(v.k_v[:, cols], v.q_v[:, cols]) * factor
        times = v.count_v[...]
        scores = jnp.where(times > 0.0, scores, -1e30)
        exponent = times * jnp.exp(scores - jnp.max(scores, axis=0, keepdims=True))
        attn = exponent * (1.0 / jnp.sum(exponent, axis=0, keepdims=True))
        v.attn_v[h] = attn
        v.mix_v[:, cols] = dot_tn(attn.astype(BF16), v.v_v[:, cols]).astype(BF16)

    arrive("out")
    middle = v.states_v[...] + mask * dot(v.mix_v[...], v.w_out_v[...])
    v.middle_v[...] = middle
    normed2, inv2 = layer_norm(middle)
    v.normed2_v[...] = normed2
    v.hidden2_v[...] = (normed2 * (1.0 + scale2) + shift2).astype(BF16)

    def exchange_z(own, name, n):
        triple, single, middle_in, comb = (
            getattr(v, name + "_triple"),
            getattr(v, name + "_single"),
            getattr(v, name + "_middle"),
            getattr(v, name + "_comb"),
        )
        outer = (z == 0) | (z == 3)
        outer_z = jnp.where(z < 2, 0, 3)
        other_inner = jnp.where(z < 2, 2, 1)
        other_outer = 3 - outer_z
        near_inner = jnp.where(z < 2, 1, 2)
        first = jnp.where(z == 0, 1, 0)
        offset = jnp.where(z == 1, 1, 0)
        to_inner = message(n, own.at[pl.ds(first, 3)], triple, z_peer(near_inner), "first")
        to_outer = message(n, own.at[outer_z], single, z_peer(outer_z), "first")
        across = message(n, comb.at[0], middle_in, z_peer(other_inner), "middle")
        beyond = message(n, comb.at[1], middle_in, z_peer(other_outer), "middle")

        def begin():
            @pl.when(outer)
            def _():
                to_inner.start()

            @pl.when(jnp.logical_not(outer))
            def _():
                to_outer.start()

        def combine():
            @pl.when(jnp.logical_not(outer))
            def _():
                to_inner.arrive()
                comb[1] = own[other_outer] + triple[other_outer - offset]
                beyond.start()
                comb[0] = own[other_inner] + triple[other_inner - offset]
                across.start()

        def finish_sum(result):
            across.arrive()

            @pl.when(outer)
            def _():
                to_outer.arrive()
                total = own[z].astype(F32) + single[...].astype(F32) + middle_in[...].astype(F32)
                result[...] = total.astype(BF16)

            @pl.when(jnp.logical_not(outer))
            def _():
                total = own[z].astype(F32) + triple[z - offset].astype(F32) + middle_in[...].astype(F32)
                result[...] = total.astype(BF16)

        return begin, combine, finish_sum

    def direct_z(own, name, n):
        landing = getattr(v, name + "_landing")

        def begin():
            for d in range(1, 4):
                there = lax.rem(z + d, 4)
                send(n, own.at[there], landing.at[d - 1], z_peer(there), "z")

        def finish_sum(result):
            message(n, landing, landing, x_peer, "z").arrive()
            total = own[z].astype(F32)
            for d in range(3):
                total = total + landing[d].astype(F32)
            result[...] = total.astype(BF16)

        return begin, finish_sum

    queue = {}
    core_copies = {}

    def place(n, value, part=None):
        kind, where, start, wide, _ = UNITS[n]
        rows = value.shape[0]

        def at(first):
            return pl.ds(first if part is None else pl.multiple_of(first + part * rows, rows), rows)

        if kind == "d":
            for b in range(wide // 128):
                block = value[:, b * 128 : (b + 1) * 128]
                v.down_v[at((start // 128 + b) * 32), where * 128 : (where + 1) * 128] = block
        elif kind == "u":
            first = where * width + start
            v.up_v[at(0), first : first + wide] = value
        elif kind == "o":
            v.o_v[at(0), start : start + wide] = value
        else:
            for b in range(wide // 128):
                first = (start // 128 + b) * width + where * 128
                v.qkv_v[at(0), first : first + 128] = value[:, b * 128 : (b + 1) * 128]

    def unit_steps(n):
        name, flow = "u%d" % n, UNITS[n][4]
        grad, landed, mine = (getattr(v, name + suffix) for suffix in ("_grad", "_core", "_mine"))
        result, received = getattr(v, name + "_result"), getattr(v, name + "_received")
        direct = flow[1:] == "d"
        copies = {}

        def core_sum():
            core_copies[n].arrive()
            total = grad[:, :, c] + landed[...]
            mine[...] = total.reshape(mine.shape)

        def y_exchange():
            copies["last"] = send(n, result, received, y_peer, "y")

        def ending():
            copies["last"].arrive()
            if flow[0] == "C":
                place(n, result[...].astype(F32), r)
                place(n, received[...].astype(F32), 1 - r)
            else:
                place(n, result[...].astype(F32) + received[...].astype(F32))

        def reduce_z(own, then):
            if direct:
                begin, finish_sum = direct_z(own, name, n)
                middle_steps = []
            else:
                begin, combine, finish_sum = exchange_z(own, name, n)
                middle_steps = [combine]

            def last():
                finish_sum(then[0])
                then[1]()

            return begin, middle_steps + [last]

        if flow[0] == "G":
            plane = getattr(v, name + "_plane")

            def start():
                core_sum()
                for d in range(1, 8):
                    there = lax.rem(z + d // 2, 4)
                    target = z_peer(there) if d % 2 == 0 else z_x_peer(there)
                    send(n, mine.at[there, x if d % 2 == 0 else 1 - x], plane.at[d - 1], target, "plane")
                copies["plane"] = message(n, plane, plane, x_peer, "plane")

            def second():
                copies["plane"].arrive()
                total = mine[z, x].astype(F32)
                for d in range(7):
                    total = total + plane[d].astype(F32)
                result[...] = total.astype(BF16)
                y_exchange()

            return [start, second, ending]
        if flow[0] == "A":
            from_x = getattr(v, name + "_x")
            begin, rest = reduce_z(from_x, (result, y_exchange))

            def start():
                core_sum()
                copies["x"] = send(n, mine.at[:, 1 - x], from_x, x_peer, "x")

            def second():
                copies["x"].arrive()
                from_x[...] = mine[:, x] + from_x[...]
                begin()

            return [start, second] + rest + [ending]
        if flow[0] == "C":
            from_y, from_x = getattr(v, name + "_y"), getattr(v, name + "_x")
            begin, rest = reduce_z(from_x, (result, y_exchange))

            def start():
                core_sum()
                copies["y"] = send(n, mine.at[:, :, 1 - r], from_y, y_peer, "early y")

            def second():
                copies["y"].arrive()
                from_y[...] = mine[:, :, r] + from_y[...]
                copies["x"] = send(n, from_y.at[:, 1 - x], from_x, x_peer, "x")

            def third():
                copies["x"].arrive()
                from_x[...] = from_y[:, x] + from_x[...]
                begin()

            return [start, second, third] + rest + [ending]
        pair, from_x = getattr(v, name + "_pair"), getattr(v, name + "_x")

        def x_exchange():
            copies["x"] = send(n, pair.at[1 - x], from_x, x_peer, "x")

        begin, rest = reduce_z(mine, (pair, x_exchange))

        def start():
            core_sum()
            begin()

        def after_x():
            copies["x"].arrive()
            result[...] = pair[x] + from_x[...]
            y_exchange()

        return [start] + rest + [after_x, ending]

    def produce(kind, where, piece):
        for n, (its_kind, its_where, start, wide, _) in enumerate(UNITS):
            if (its_kind, its_where) == (kind, where):
                grad = getattr(v, "u%d_grad" % n)
                for b in range(0, wide, 128):
                    grad[..., b : b + 128] = piece(start + b).reshape(4, 2, 2, 32, 128)
                landed = getattr(v, "u%d_core" % n)
                core_copies[n] = send(n, grad.at[:, :, 1 - c], landed, core_peer, "core")
                queue[n] = unit_steps(n)

    def section_up(t):
        arrive("up")
        cols = slice(t * width, (t + 1) * width)
        up = dot(v.hidden2_v[...], v.w_up_v[:, cols])
        v.up_proj_v[:, cols] = up
        v.activation_v[:, cols] = (up * (1.0 / (1.0 + jnp.exp(-up)))).astype(BF16)

    def section_mask():
        arrive("down")
        v.d_branch_v[...] = (mask * v.cot_v[...]).astype(BF16)

    def section_dup(t):
        cols = slice(t * width, (t + 1) * width)
        up = v.up_proj_v[:, cols]
        sigmoid = 1.0 / (1.0 + jnp.exp(-up))
        d_act = dot_nt(v.d_branch_v[...], v.w_down_v[t * width : (t + 1) * width, :])
        v.d_up_v[:, cols] = (d_act * sigmoid * (1.0 + up * (1.0 - sigmoid))).astype(BF16)

    def section_gd(h):
        value = dot_tn(v.activation_v[...], v.d_branch_v[:, h * 256 : (h + 1) * 256]).astype(BF16)
        value = value.reshape(GROUP, 4, 32, 256)
        for k in range(2):
            produce("d", 2 * h + k, lambda start: value[:, start // 128, :, k * 128 : (k + 1) * 128])

    def section_gu(t):
        value = dot_tn(v.hidden2_v[...], v.d_up_v[:, t * width : (t + 1) * width]).astype(BF16)
        produce("u", t, lambda start: value[:, start : start + 128])

    def section_out():
        branch = dot(v.activation_v[:, 0:width], v.w_down_v[0:width, :])
        for t in range(1, tiles):
            branch = branch + dot(v.activation_v[:, t * width : (t + 1) * width], v.w_down_v[t * width : (t + 1) * width, :])
        v.out_v[0] = v.middle_v[...] + mask * branch

    def section_mid():
        d_hidden2 = dot_nt(v.d_up_v[:, 0:width], tile(v.w_up_v, 0))
        for t in range(1, tiles):
            d_hidden2 = d_hidden2 + dot_nt(v.d_up_v[:, t * width : (t + 1) * width], tile(v.w_up_v, t))
        normed2 = v.normed2_v[...]
        v.mod_v[1, :, 0:width] = jnp.sum(d_hidden2 * normed2, axis=0, keepdims=True)
        v.mod_v[1, :, width : 2 * width] = jnp.sum(d_hidden2, axis=0, keepdims=True)
        queue["m1"] = mod_steps(1)
        d_middle = v.cot_v[...] + norm_back(d_hidden2 * (1.0 + scale2), normed2, inv2)
        v.d_middle_v[...] = d_middle
        v.d_attended_v[...] = (mask * d_middle).astype(BF16)
        v.d_mix_v[...] = dot_nt(v.d_attended_v[...], v.w_out_v[...]).astype(BF16)

    def section_go():
        value = dot_tn(v.mix_v[...], v.d_attended_v[...]).astype(BF16)
        produce("o", 0, lambda start: value[:, start : start + 128])

    def section_attn(h):
        cols = slice(h * head, (h + 1) * head)
        attn = v.attn_v[h]
        d_attn = dot_nt(v.v_v[:, cols], v.d_mix_v[:, cols])
        inner = jnp.sum(attn * d_attn, axis=0, keepdims=True)
        d_scores = (attn * (d_attn - inner)).astype(BF16)
        v.d_q_v[:, cols] = (dot_tn(d_scores, v.k_v[:, cols]) * factor).astype(BF16)
        v.d_k_v[:, cols] = (dot(d_scores, v.q_v[:, cols]) * factor).astype(BF16)
        v.d_v_v[:, cols] = dot(attn.astype(BF16), v.d_mix_v[:, cols]).astype(BF16)

    def section_gq(h):
        cols = slice(h * head, (h + 1) * head)
        values = [
            dot_tn(v.table_v[0:nodes, :], v.d_q_v[:, cols]).astype(BF16),
            dot_tn(v.table_v[...], v.d_k_v[:, cols]).astype(BF16),
            dot_tn(v.table_v[...], v.d_v_v[:, cols]).astype(BF16),
        ]
        produce("h", h, lambda start: values[start // 128])

    back = []

    def section_table():
        d_table = dot_nt(v.d_k_v[...], tile(v.w_qkv_v, 1)) + dot_nt(v.d_v_v[...], tile(v.w_qkv_v, 2))
        v.lend_back_v[...] = d_table[nodes:table, :].astype(BF16)
        back.append(send("back", v.lend_back_v.at[0:half], v.returned_v.at[half:lent], before, 2))
        back.append(send("back", v.lend_back_v.at[half:lent], v.returned_v.at[0:half], after, 3))
        d_hidden1 = d_table[0:nodes, :] + dot_nt(v.d_q_v[...], tile(v.w_qkv_v, 0))
        v.d_hidden1_v[...] = d_hidden1
        d_lent = d_table[nodes:table, :]
        v.mod_v[0, :, 0:width] = jnp.sum(d_hidden1 * v.normed1_v[...], axis=0, keepdims=True) + jnp.sum(
            d_lent * v.halo_v[...].astype(F32), axis=0, keepdims=True
        )
        v.mod_v[0, :, width : 2 * width] = jnp.sum(d_hidden1, axis=0, keepdims=True) + jnp.sum(
            d_lent, axis=0, keepdims=True
        )
        queue["m0"] = mod_steps(0)

    def section_state():
        for copy in back:
            copy.arrive()
        d_hidden1 = v.d_hidden1_v[...] + dot(pick, v.returned_v[...])
        normed1 = v.normed1_v[...]
        v.d_states_v[0] = v.d_middle_v[...] + norm_back(d_hidden1 * (1.0 + scale1), normed1, inv1)

    def mod_steps(part):
        own, from_core, plane, rows = v.mod_v.at[part], v.mod_core_v.at[part], v.mods_v.at[part], v.rows_v.at[part]
        name = "m%d" % part
        copies = [send(name, own, from_core, core_peer, "core")]

        def spread():
            copies.pop().arrive()
            plane[0] = own[...] + from_core[...]
            for d in range(1, 8):
                there = lax.rem(z + d // 2, 4)
                target = z_peer(there) if d % 2 == 0 else z_x_peer(there)
                send(name, plane.at[0], plane.at[d], target, "plane")
            copies.append(message(name, plane.at[pl.ds(1, 7)], plane.at[pl.ds(1, 7)], x_peer, "plane"))

        def swap():
            copies.pop().arrive()
            total = jnp.zeros(own.shape, F32)
            for there in range(4):
                for side in range(2):
                    total = total + plane[lax.rem(z + 4 - there, 4) * 2 + lax.rem(x + side, 2)]
            rows[r] = total
            copies.append(send(name, rows.at[r], rows.at[r], y_peer, "y"))

        def spend():
            copies.pop().arrive()
            first_row, second_row = rows[0], rows[1]
            here = slice(part * 2 * width, (part + 1) * 2 * width)
            if not finish:
                v.d_noise_v[0:1, here] = first_row
                v.d_noise_v[1:2, here] = second_row
                return
            row = lax.broadcasted_iota(jnp.int32, (16, 2 * width), 0)
            stacked = jnp.zeros((16, 2 * width), F32)
            for number, piece in enumerate(split3(first_row) + split3(second_row)):
                stacked = jnp.where(row == number, piece, stacked)
            noise = dot_nt(stacked.astype(BF16), v.w_cond_v[part])
            first_noise = jnp.sum(noise[0:3], axis=0, keepdims=True)
            second_noise = jnp.sum(noise[3:6], axis=0, keepdims=True)
            if part == 1:
                v.noise_part_v[0:1, :] = first_noise
                v.noise_part_v[1:2, :] = second_noise
            else:
                v.d_noise_v[0:1, :] = first_noise + v.noise_part_v[0:1, :]
                v.d_noise_v[1:2, :] = second_noise + v.noise_part_v[1:2, :]
            shape = (v.d_cond_v.shape[0], width)
            mine = lax.broadcasted_iota(jnp.int32, shape, 1) == (
                lax.broadcasted_iota(jnp.int32, shape, 0) + p * shape[0]
            )
            picked = [
                jnp.sum(jnp.where(mine, v.noise_v[b : b + 1, :], 0.0), axis=1, keepdims=True)
                for b in range(2)
            ]
            v.d_cond_v[:, here] = picked[0] * first_row + picked[1] * second_row

        return [spread, swap, spend]

    sections = {
        "up": section_up,
        "mask": section_mask,
        "dup": section_dup,
        "gd": section_gd,
        "gu": section_gu,
        "out": section_out,
        "mid": section_mid,
        "go": section_go,
        "attn": section_attn,
        "gq": section_gq,
        "table": section_table,
        "state": section_state,
    }
    for entry in ORDER:
        if entry in queue:
            queue[entry].pop(0)()
        elif isinstance(entry, tuple):
            sections[entry[0]](entry[1])
        else:
            sections[entry]()
    for steps in queue.values():
        for step in steps:
            step()

    for n in range(len(UNITS)):
        all_left(n, getattr(v, "u%d_grad" % n))
    for part in range(2):
        all_left("m%d" % part, v.mods_v.at[part])
    all_left("halo", v.lend_v)
    all_left("back", v.lend_back_v)


def copy_out(count, *refs):
    for n in range(count):
        src, dst = refs[n], refs[count + n]
        rows = src.shape[-2]
        pieces = 4 if rows % 64 == 0 else 1
        for k in range(pieces):
            at = (*[slice(None)] * (len(src.shape) - 2), slice(k * rows // pieces, (k + 1) * rows // pieces))
            pltpu.make_async_copy(src.at[at], dst.at[at], refs[-1].at[n]).start()
    for n in range(count):
        pltpu.make_async_copy(refs[n], refs[count + n], refs[-1].at[n]).wait()


def body(
    node_state,
    noise_embed,
    w_cond,
    w_qkv,
    w_out,
    w_up,
    w_down,
    neighbours,
    send_rows,
    valid,
    cotangent,
):
    nodes, width = node_state.shape[1:]
    hidden = w_up.shape[1]
    lent = send_rows.shape[0]
    table = nodes + lent
    patches = lax.axis_size("patch")
    fold = patches // GROUP
    rows_each = width // patches
    block = width // GROUP
    half = width // 2

    hbm = pl.BlockSpec(memory_space=pl.ANY)
    vmem = pl.BlockSpec(memory_space=pltpu.VMEM)
    inputs = [
        ("states_hbm", node_state, hbm),
        ("noise_hbm", noise_embed, hbm),
        ("w_cond_hbm", w_cond, hbm),
        ("w_qkv_hbm", w_qkv, hbm),
        ("w_out_hbm", w_out, hbm),
        ("w_up_hbm", w_up, hbm),
        ("w_down_hbm", w_down, hbm),
        ("neighbours_hbm", neighbours.T, hbm),
        ("send_hbm", send_rows[None, :], hbm),
        ("valid_hbm", valid[None, :], hbm),
        ("cot_hbm", cotangent, hbm),
    ]
    outputs = [
        ("out_v", node_state.shape, vmem),
        ("d_states_v", node_state.shape, vmem),
        ("down_v", (hidden // GROUP, width), vmem),
        ("up_v", (block, hidden), vmem),
        ("o_v", (block, width), vmem),
        ("qkv_v", (block, 3 * width), vmem),
    ]
    if fold == 1:
        outputs += [("d_noise_v", noise_embed.shape, vmem), ("d_cond_v", (rows_each, 4 * width), vmem)]
    else:
        outputs += [("d_noise_v", (noise_embed.shape[0], 4 * width), vmem)]
    tiles = hidden // width
    receivers = receive_plan()[1]
    scratch = [
        ("noise_v", noise_embed.shape, F32),
        ("neighbours_v", neighbours.shape[::-1], jnp.int32),
        ("pick_v", (1, lent), jnp.int32),
        ("valid_v", (1, nodes), jnp.int32),
        ("states_v", (nodes, width), F32),
        ("cot_v", (nodes, width), F32),
        ("w_cond_v", (2, width, 2 * width), BF16),
        ("w_qkv_v", w_qkv.shape, BF16),
        ("w_out_v", (width, width), BF16),
        ("w_up_v", w_up.shape, BF16),
        ("w_down_v", w_down.shape, BF16),
        ("normed1_v", (nodes, width), F32),
        ("table_v", (table, width), BF16),
        ("lend_v", (lent, width), BF16),
        ("halo_v", (lent, width), BF16),
        ("returned_v", (lent, width), BF16),
        ("q_v", (nodes, width), BF16),
        ("k_v", (table, width), BF16),
        ("v_v", (table, width), BF16),
        ("count_v", (table, nodes), F32),
        ("attn_v", (HEADS, table, nodes), F32),
        ("mix_v", (nodes, width), BF16),
        ("middle_v", (nodes, width), F32),
        ("normed2_v", (nodes, width), F32),
        ("hidden2_v", (nodes, width), BF16),
        ("d_branch_v", (nodes, width), BF16),
        ("d_mix_v", (nodes, width), BF16),
        ("d_q_v", (nodes, width), BF16),
        ("d_k_v", (table, width), BF16),
        ("d_v_v", (table, width), BF16),
        ("mod_v", (2, 1, 2 * width), F32),
        ("mod_core_v", (2, 1, 2 * width), F32),
        ("mods_v", (2, 9, 1, 2 * width), F32),
        ("rows_v", (2, 2, 1, 2 * width), F32),
        ("noise_part_v", noise_embed.shape, F32),
        ("up_proj_v", (nodes, hidden), F32),
        ("activation_v", (nodes, hidden), BF16),
        ("d_up_v", (nodes, hidden), BF16),
        ("d_middle_v", (nodes, width), F32),
        ("d_attended_v", (nodes, width), BF16),
        ("d_hidden1_v", (nodes, width), F32),
        ("lend_back_v", (lent, width), BF16),
    ]
    for n, (_, _, _, wide, flow) in enumerate(UNITS):
        name = "u%d" % n
        rows = 16 if flow[0] == "C" else 32
        part = (2, 32, wide) if flow[0] == "B" else (rows, wide)
        buffers = [("_grad", (4, 2, 2, 32, wide)), ("_core", (4, 2, 32, wide))]
        buffers += [("_mine", (4, 2, 2, 16, wide) if flow[0] == "C" else (4, 2, 32, wide))]
        buffers += [("_result", (rows, wide)), ("_received", (rows, wide))]
        if flow[0] == "G":
            buffers += [("_plane", (7, rows, wide))]
        else:
            buffers += [("_x", (rows, wide) if flow[0] == "B" else (4, rows, wide))]
            if flow[0] == "C":
                buffers += [("_y", (4, 2, 16, wide))]
            if flow[0] == "B":
                buffers += [("_pair", part)]
            if flow[1:] == "d":
                buffers += [("_landing", (3, *part))]
            else:
                buffers += [("_triple", (3, *part)), ("_single", part), ("_middle", part), ("_comb", (2, *part))]
        scratch += [(name + suffix, shape, BF16) for suffix, shape in buffers]
    semaphores = [
        ("load_sem", pltpu.SemaphoreType.DMA((12,))),
        ("send_sem", pltpu.SemaphoreType.DMA((len(UNITS) + 4,))),
        ("recv_sem", pltpu.SemaphoreType.DMA((receivers,))),
    ]
    names = [n for group in (inputs, outputs, scratch, semaphores) for n in [e[0] for e in group]]
    results = pl.pallas_call(
        functools.partial(kernel, fold, patches, names),
        out_shape=[pltpu.VMEM(shape, F32) for _, shape, _ in outputs],
        in_specs=[spec for _, _, spec in inputs],
        out_specs=[spec for _, _, spec in outputs],
        scratch_shapes=[pltpu.VMEM(shape, dtype) for _, shape, dtype in scratch]
        + [sem for _, sem in semaphores],
        compiler_params=pltpu.CompilerParams(
            collective_id=0, has_side_effects=True, vmem_limit_bytes=44 * 1024 * 1024
        ),
    )(
        *[pltpu.with_memory_space_constraint(array, pltpu.HBM) for _, array, _ in inputs]
    )
    if fold == 1:
        results = pl.pallas_call(
            functools.partial(copy_out, len(results)),
            out_shape=[jax.ShapeDtypeStruct(a.shape, a.dtype) for a in results],
            in_specs=[hbm] * len(results),
            out_specs=[hbm] * len(results),
            scratch_shapes=[pltpu.SemaphoreType.DMA((len(results),))],
            compiler_params=pltpu.CompilerParams(vmem_limit_bytes=1024 * 1024),
        )(*results)
    output, d_state, g_down, g_up, g_out, g_qkv = results[:6]
    if fold == 1:
        grad_noise, grad_cond = results[6:]
    else:
        groups = [[m * fold + i for i in range(fold)] for m in range(GROUP)]

        def rest(array):
            return lax.psum_scatter(
                array, "patch", scatter_dimension=0, axis_index_groups=groups, tiled=True
            )

        g_down, g_up, g_out, g_qkv = rest(g_down), rest(g_up), rest(g_out), rest(g_qkv)
        mods = lax.psum(results[6], "patch") / GROUP
        highest = lax.Precision.HIGHEST
        grad_noise = jnp.dot(mods, w_cond.astype(F32).T, precision=highest)
        first_row = lax.axis_index("patch") * rows_each
        cond_cols = lax.dynamic_slice_in_dim(noise_embed, first_row, rows_each, 1)
        grad_cond = jnp.dot(cond_cols.T, mods, precision=highest)
    return output, d_state, grad_noise, grad_cond, g_qkv, g_out, g_up, g_down


def solution(mesh):
    in_specs = (
        P("rep", "patch", None),
        P(),
        P(),
        P(),
        P(),
        P(),
        P(),
        P("patch", None),
        P("patch"),
        P("patch"),
        P("rep", "patch", None),
    )
    out_specs = (
        P("rep", "patch", None),
        P("rep", "patch", None),
        P(),
        P("patch", None),
        P("patch", None),
        P("patch", None),
        P("patch", None),
        P("patch", None),
    )
    return jax.shard_map(body, mesh=mesh, in_specs=in_specs, out_specs=out_specs, check_vma=False)
```

```python
import functools

import jax
import jax.numpy as jnp
from jax import lax
from jax.experimental import pallas as pl
from jax.experimental.pallas import tpu as pltpu
from jax.sharding import PartitionSpec as P

HEADS = 4
GROUP = 16
UNITS = (
    ("d", 0, 0, 512, "Cd"), ("d", 1, 0, 512, "Ad"), ("d", 2, 0, 256, "Bd"), ("d", 2, 256, 256, "C"),
    ("d", 3, 0, 256, "Ad"), ("d", 3, 256, 256, "B"), ("u", 0, 0, 256, "Cd"),
    ("u", 0, 256, 256, "C"), ("u", 1, 0, 512, "A"), ("u", 2, 0, 512, "C"), ("u", 3, 0, 256, "B"),
    ("u", 3, 256, 256, "Bd"), ("o", 0, 0, 512, "C"), ("h", 0, 0, 384, "Cd"), ("h", 1, 0, 128, "Ad"),
    ("h", 1, 128, 256, "Cd"), ("h", 2, 0, 128, "Cd"), ("h", 2, 128, 256, "Ad"),
    ("h", 3, 0, 128, "A"), ("h", 3, 128, 256, "Cd"),
)
ORDER = (
    ("up", 2), "mask", ("up", 0), ("up", 3), ("up", 1), ("gd", 1), ("dup", 3), ("gd", 0), 2, 3,
    ("dup", 1), 4, ("gu", 3), ("dup", 0), 0, 5, ("gu", 0), 1, ("dup", 2), ("gu", 1), 11, "mid", 7,
    ("gu", 2), 10, 8, 6, "go", 4, ("attn", 1), ("attn", 2), ("gq", 1), 12, 1, 9, 14, ("attn", 3),
    ("gq", 3), 5, 3, 7, "m1", 18, 6, 0, ("gq", 2), 16, 8, 3, 10, 14, 15, ("attn", 0), 17, 12, 19,
    ("gq", 0), 18, 7, "table", 6, 9, 13, 0, 8, "m1", 15, 12, 3, 17, 19, 5, 18, 16, 7, 10, 4, 1, 13,
    9, "m0", 14, 11, 2, 15, 19, 8, 18, 16, 5, 6, 12, 13, 17, 9, 10, "out", 7, 14, 3, 0, 11, "state",
    "m0", 18, 5, 12, 2, 15, 4, 16, 19, 8, 6, 9, 17, 1, 7, 13, 10, 3, "m1", 15, 16, "m0", 2, 0, 19,
    12, 9, 11, 13,
)
MESH = pl.DeviceIdType.MESH
F32 = jnp.float32
BF16 = jnp.bfloat16


def dot(a, b):
    return lax.dot_general(a, b, (((1,), (0,)), ((), ())), preferred_element_type=F32)


def dot_nt(a, b):
    return lax.dot_general(a, b, (((1,), (1,)), ((), ())), preferred_element_type=F32)


def dot_tn(a, b):
    return lax.dot_general(a, b, (((0,), (0,)), ((), ())), preferred_element_type=F32)


def split3(v):
    high = v.astype(BF16)
    rest = v - high.astype(F32)
    mid = rest.astype(BF16)
    low = (rest - mid.astype(F32)).astype(BF16)
    return high.astype(F32), mid.astype(F32), low.astype(F32)


def layer_norm(values):
    centred = values - jnp.mean(values, axis=-1, keepdims=True)
    inv_std = lax.rsqrt(jnp.mean(centred * centred, axis=-1, keepdims=True) + 1e-05)
    return centred * inv_std, inv_std


def norm_back(gradient, normed, inv_std):
    first = jnp.mean(gradient, axis=-1, keepdims=True)
    second = jnp.mean(gradient * normed, axis=-1, keepdims=True)
    return (gradient - first - normed * second) * inv_std


ROUTES = {
    "A": (("core", -1, 0), ("x", 0, 1), ("first", 1, 3), ("middle", 2, 3), ("y", 3, 4)),
    "Ad": (("core", -1, 0), ("x", 0, 1), ("z", 1, 2), ("y", 2, 3)),
    "B": (("core", -1, 0), ("first", 0, 2), ("middle", 1, 2), ("x", 2, 3), ("y", 3, 4)),
    "Bd": (("core", -1, 0), ("z", 0, 1), ("x", 1, 2), ("y", 2, 3)),
    "C": (("core", -1, 0), ("early y", 0, 1), ("x", 1, 2), ("first", 2, 4), ("middle", 3, 4), ("y", 4, 5)),
    "Cd": (("core", -1, 0), ("early y", 0, 1), ("x", 1, 2), ("z", 2, 3), ("y", 3, 4)),
    "G": (("core", -1, 0), ("plane", 0, 1), ("y", 1, 2)),
    "M": (("core", -1, 0), ("plane", 0, 1), ("y", 1, 2)),
}
SOURCE = {"d": lambda w: ("gd", w // 2), "u": lambda w: ("gu", w), "o": lambda w: "go", "h": lambda w: ("gq", w)}


def receive_plan():
    steps = {}
    for position, entry in enumerate(ORDER):
        steps.setdefault(entry, []).append(position)
    copies = []
    for n, (kind, where, _, _, route) in enumerate(UNITS):
        copies += [(n, steps[SOURCE[kind](where)][0], *copy) for copy in ROUTES[route]]
    for name, source in (("m1", "mid"), ("m0", "table")):
        copies += [(name, steps[source][0], *copy) for copy in ROUTES["M"]]
    timed = []
    for n, start, what, sender, waiter in copies:
        timed.append((start if sender < 0 else steps[n][sender], steps[n][waiter], what, n))
    timed.sort(key=lambda copy: copy[0])
    kinds = {"early y": "y", "middle": "first"}

    def answered(send, kind, waited):
        return any(
            kinds.get(what, what) == kind and what != "middle" and waited <= sent and got <= send
            for sent, got, what, _ in timed
        )

    numbers, free = {}, [(-1, 0), (-1, 1)]
    count = 4
    for send, got, what, n in timed:
        kind = kinds.get(what, what)
        fit = [entry for entry in free if answered(send, kind, entry[0])]
        if fit:
            entry = max(fit)
            free.remove(entry)
            number = entry[1]
        else:
            number, count = count, count + 1
        numbers[n, what] = number
        free.append((got, number))
    return numbers, count


class Names:
    pass


class Message:
    def __init__(self, v, outgoing, receive, src, dst, target):
        self.parts = dict(
            src_ref=src,
            dst_ref=dst,
            send_sem=v.send_sem.at[outgoing],
            recv_sem=v.recv_sem.at[receive],
            device_id=target,
            device_id_type=MESH,
        )

    def start(self):
        pltpu.make_async_remote_copy(**self.parts).start()

    def arrive(self):
        pltpu.make_async_remote_copy(**self.parts).wait_recv()

    def leave(self):
        pltpu.make_async_remote_copy(**self.parts).wait_send()


def kernel(fold, patches, names, *refs):
    v = Names()
    for name, ref in zip(names, refs):
        setattr(v, name, ref)
    p = lax.axis_index("patch")
    r = lax.axis_index("rep")
    member = p // fold
    lane = lax.rem(p, fold)
    c = lax.rem(member, 2)
    x = lax.rem(member // 2, 2)
    z = member // 4
    finish = fold == 1

    def device(index, rep=r):
        return (index * fold + lane, rep)

    before = (lax.rem(p + patches - 1, patches), r)
    after = (lax.rem(p + 1, patches), r)
    core_peer = device(member + 1 - 2 * c)
    x_peer = device(member + 2 - 4 * x)
    y_peer = (p, 1 - r)

    def z_peer(there):
        return device(there * 4 + x * 2 + c)

    def z_x_peer(there):
        return device(there * 4 + (1 - x) * 2 + c)

    nodes, width = v.states_hbm.shape[1:]
    tiles = v.w_up_hbm.shape[1] // width
    head = width // HEADS
    factor = head ** (-0.5)
    table = v.k_v.shape[0]
    lent = table - nodes
    half = lent // 2

    loads = {}
    loaded = [0]

    def load(key, *pairs):
        copies = []
        for src, dst in pairs:
            copy = pltpu.make_async_copy(src, dst, v.load_sem.at[loaded[0]])
            loaded[0] += 1
            copy.start()
            copies.append(copy)
        loads[key] = copies

    def arrive(key):
        for copy in loads.pop(key, ()):
            copy.wait()

    load("states", (v.states_hbm.at[0], v.states_v), (v.send_hbm, v.pick_v))

    barrier = pltpu.get_barrier_semaphore()
    others = [before, after, core_peer, x_peer, y_peer] + [z_peer(lax.rem(z + d, 4)) for d in range(1, 4)]
    others += [z_x_peer(lax.rem(z + d, 4)) for d in range(1, 4)]
    for other in others:
        pl.semaphore_signal(barrier, inc=1, device_id=other, device_id_type=MESH)

    load("cond1", (v.noise_hbm, v.noise_v), (v.w_cond_hbm.at[:, 0 : 2 * width], v.w_cond_v.at[0]))
    load("index", (v.neighbours_hbm, v.neighbours_v), (v.valid_hbm, v.valid_v))
    load("qkv", (v.w_qkv_hbm, v.w_qkv_v))
    load("cond2", (v.w_cond_hbm.at[:, 2 * width : 4 * width], v.w_cond_v.at[1]))

    def tile(ref, t):
        return ref[:, t * width : (t + 1) * width]

    numbers, _ = receive_plan()
    outgoing = {n: n for n in range(len(UNITS))}
    for name in ("m0", "m1", "halo", "back"):
        outgoing[name] = len(outgoing)

    def message(n, src, dst, target, receive):
        return Message(v, outgoing[n], numbers.get((n, receive), receive), src, dst, target)

    def send(n, src, dst, target, receive):
        copy = message(n, src, dst, target, receive)
        copy.start()
        return copy

    def all_left(n, ref):
        message(n, ref, ref, x_peer, 0).leave()

    arrive("states")
    normed1, inv1 = layer_norm(v.states_v[...])
    v.normed1_v[...] = normed1
    pick = (v.pick_v[...] == lax.broadcasted_iota(jnp.int32, (nodes, lent), 0)).astype(BF16)
    v.lend_v[...] = dot_tn(pick, normed1.astype(BF16)).astype(BF16)
    pl.semaphore_wait(barrier, len(others))
    halo = [
        send("halo", v.lend_v.at[0:half], v.halo_v.at[half:lent], before, 0),
        send("halo", v.lend_v.at[half:lent], v.halo_v.at[0:half], after, 1),
    ]

    load("out", (v.w_out_hbm, v.w_out_v))
    load("up", (v.w_up_hbm, v.w_up_v))
    load("down", (v.cot_hbm.at[0], v.cot_v), (v.w_down_hbm, v.w_down_v))

    for key in ("cond1", "index", "qkv", "cond2"):
        arrive(key)
    condition = v.noise_v[pl.ds(r, 1), :]
    row = lax.broadcasted_iota(jnp.int32, (16, width), 0)
    high, mid, low = split3(condition)
    stacked = jnp.where(row == 0, high, jnp.where(row == 1, mid, jnp.where(row == 2, low, 0.0))).astype(BF16)
    mod1 = jnp.sum(dot(stacked, v.w_cond_v[0]), axis=0, keepdims=True)
    scale1, shift1 = mod1[:, :width], mod1[:, width:]
    hidden1 = (v.normed1_v[...] * (1.0 + scale1) + shift1).astype(BF16)
    v.table_v[0:nodes, :] = hidden1

    v.k_v[0:nodes, :] = dot(hidden1, tile(v.w_qkv_v, 1)).astype(BF16)
    v.v_v[0:nodes, :] = dot(hidden1, tile(v.w_qkv_v, 2)).astype(BF16)
    v.q_v[...] = dot(hidden1, tile(v.w_qkv_v, 0)).astype(BF16)

    ids = v.neighbours_v[...].astype(jnp.int16)
    entry = lax.broadcasted_iota(jnp.int32, (table, nodes), 0).astype(jnp.int16)
    count = jnp.zeros((table, nodes), BF16)
    for j in range(ids.shape[0]):
        count = jnp.where(ids[j : j + 1, :] == entry, count + jnp.ones_like(count), count)
    v.count_v[...] = count

    mod2 = jnp.sum(dot(stacked, v.w_cond_v[1]), axis=0, keepdims=True)
    scale2, shift2 = mod2[:, :width], mod2[:, width:]
    real = jnp.sum(v.valid_v[...], axis=1, keepdims=True)
    mask = (lax.broadcasted_iota(jnp.int32, (nodes, 1), 0) < real).astype(F32)

    for copy in halo:
        copy.arrive()
    rows = (v.halo_v[...].astype(F32) * (1.0 + scale1) + shift1).astype(BF16)
    v.table_v[nodes:table, :] = rows
    v.k_v[nodes:table, :] = dot(rows, tile(v.w_qkv_v, 1)).astype(BF16)
    v.v_v[nodes:table, :] = dot(rows, tile(v.w_qkv_v, 2)).astype(BF16)

    for h in range(HEADS):
        cols = slice(h * head, (h + 1) * head)
        scores = dot_nt(v.k_v[:, cols], v.q_v[:, cols]) * factor
        times = v.count_v[...].astype(F32)
        scores = jnp.where(times > 0.0, scores, -1e30)
        exponent = times * jnp.exp(scores - jnp.max(scores, axis=0, keepdims=True))
        attn = exponent * (1.0 / jnp.sum(exponent, axis=0, keepdims=True))
        v.attn_v[h] = attn
        v.mix_v[:, cols] = dot_tn(attn.astype(BF16), v.v_v[:, cols]).astype(BF16)

    arrive("out")
    middle = v.states_v[...] + mask * dot(v.mix_v[...], v.w_out_v[...])
    v.middle_v[...] = middle
    normed2, inv2 = layer_norm(middle)
    v.normed2_v[...] = normed2
    v.hidden2_v[...] = (normed2 * (1.0 + scale2) + shift2).astype(BF16)

    def exchange_z(own, name, n):
        triple, single, middle_in, comb = (
            getattr(v, name + "_triple"),
            getattr(v, name + "_single"),
            getattr(v, name + "_middle"),
            getattr(v, name + "_comb"),
        )
        outer = (z == 0) | (z == 3)
        outer_z = jnp.where(z < 2, 0, 3)
        other_inner = jnp.where(z < 2, 2, 1)
        other_outer = 3 - outer_z
        near_inner = jnp.where(z < 2, 1, 2)
        first = jnp.where(z == 0, 1, 0)
        offset = jnp.where(z == 1, 1, 0)
        to_inner = message(n, own.at[pl.ds(first, 3)], triple, z_peer(near_inner), "first")
        to_outer = message(n, own.at[outer_z], single, z_peer(outer_z), "first")
        across = message(n, comb.at[0], middle_in, z_peer(other_inner), "middle")
        beyond = message(n, comb.at[1], middle_in, z_peer(other_outer), "middle")

        def begin():
            @pl.when(outer)
            def _():
                to_inner.start()

            @pl.when(jnp.logical_not(outer))
            def _():
                to_outer.start()

        def combine():
            @pl.when(jnp.logical_not(outer))
            def _():
                to_inner.arrive()
                comb[1] = own[other_outer] + triple[other_outer - offset]
                beyond.start()
                comb[0] = own[other_inner] + triple[other_inner - offset]
                across.start()

        def finish_sum(result):
            across.arrive()

            @pl.when(outer)
            def _():
                to_outer.arrive()
                total = own[z].astype(F32) + single[...].astype(F32) + middle_in[...].astype(F32)
                result[...] = total.astype(BF16)

            @pl.when(jnp.logical_not(outer))
            def _():
                total = own[z].astype(F32) + triple[z - offset].astype(F32) + middle_in[...].astype(F32)
                result[...] = total.astype(BF16)

        return begin, combine, finish_sum

    def direct_z(own, name, n):
        landing = getattr(v, name + "_landing")

        def begin():
            for d in range(1, 4):
                there = lax.rem(z + d, 4)
                send(n, own.at[there], landing.at[d - 1], z_peer(there), "z")

        def finish_sum(result):
            message(n, landing, landing, x_peer, "z").arrive()
            total = own[z].astype(F32)
            for d in range(3):
                total = total + landing[d].astype(F32)
            result[...] = total.astype(BF16)

        return begin, finish_sum

    queue = {}
    core_copies = {}

    def place(n, value, part=None):
        kind, where, start, wide, _ = UNITS[n]
        rows = value.shape[0]

        def at(first):
            return pl.ds(first if part is None else pl.multiple_of(first + part * rows, rows), rows)

        if kind == "d":
            for b in range(wide // 128):
                block = value[:, b * 128 : (b + 1) * 128]
                v.down_v[at((start // 128 + b) * 32), where * 128 : (where + 1) * 128] = block
        elif kind == "u":
            first = where * width + start
            v.up_v[at(0), first : first + wide] = value
        elif kind == "o":
            v.o_v[at(0), start : start + wide] = value
        else:
            for b in range(wide // 128):
                first = (start // 128 + b) * width + where * 128
                v.qkv_v[at(0), first : first + 128] = value[:, b * 128 : (b + 1) * 128]

    def unit_steps(n):
        name, flow = "u%d" % n, UNITS[n][4]
        grad, landed, mine = (getattr(v, name + suffix) for suffix in ("_grad", "_core", "_mine"))
        result, received = getattr(v, name + "_result"), getattr(v, name + "_received")
        direct = flow[1:] == "d"
        copies = {}

        def core_sum():
            core_copies[n].arrive()
            total = grad[:, :, c] + landed[...]
            mine[...] = total.reshape(mine.shape)

        def y_exchange():
            copies["last"] = send(n, result, received, y_peer, "y")

        def ending():
            copies["last"].arrive()
            if flow[0] == "C":
                place(n, result[...].astype(F32), r)
                place(n, received[...].astype(F32), 1 - r)
            else:
                place(n, result[...].astype(F32) + received[...].astype(F32))

        def reduce_z(own, then):
            if direct:
                begin, finish_sum = direct_z(own, name, n)
                middle_steps = []
            else:
                begin, combine, finish_sum = exchange_z(own, name, n)
                middle_steps = [combine]

            def last():
                finish_sum(then[0])
                then[1]()

            return begin, middle_steps + [last]

        if flow[0] == "G":
            plane = getattr(v, name + "_plane")

            def start():
                core_sum()
                for d in range(1, 8):
                    there = lax.rem(z + d // 2, 4)
                    target = z_peer(there) if d % 2 == 0 else z_x_peer(there)
                    send(n, mine.at[there, x if d % 2 == 0 else 1 - x], plane.at[d - 1], target, "plane")
                copies["plane"] = message(n, plane, plane, x_peer, "plane")

            def second():
                copies["plane"].arrive()
                total = mine[z, x].astype(F32)
                for d in range(7):
                    total = total + plane[d].astype(F32)
                result[...] = total.astype(BF16)
                y_exchange()

            return [start, second, ending]
        if flow[0] == "A":
            from_x = getattr(v, name + "_x")
            begin, rest = reduce_z(from_x, (result, y_exchange))

            def start():
                core_sum()
                copies["x"] = send(n, mine.at[:, 1 - x], from_x, x_peer, "x")

            def second():
                copies["x"].arrive()
                from_x[...] = mine[:, x] + from_x[...]
                begin()

            return [start, second] + rest + [ending]
        if flow[0] == "C":
            from_y, from_x = getattr(v, name + "_y"), getattr(v, name + "_x")
            begin, rest = reduce_z(from_x, (result, y_exchange))

            def start():
                core_sum()
                copies["y"] = send(n, mine.at[:, :, 1 - r], from_y, y_peer, "early y")

            def second():
                copies["y"].arrive()
                from_y[...] = mine[:, :, r] + from_y[...]
                copies["x"] = send(n, from_y.at[:, 1 - x], from_x, x_peer, "x")

            def third():
                copies["x"].arrive()
                from_x[...] = from_y[:, x] + from_x[...]
                begin()

            return [start, second, third] + rest + [ending]
        pair, from_x = getattr(v, name + "_pair"), getattr(v, name + "_x")

        def x_exchange():
            copies["x"] = send(n, pair.at[1 - x], from_x, x_peer, "x")

        begin, rest = reduce_z(mine, (pair, x_exchange))

        def start():
            core_sum()
            begin()

        def after_x():
            copies["x"].arrive()
            result[...] = pair[x] + from_x[...]
            y_exchange()

        return [start] + rest + [after_x, ending]

    def produce(kind, where, piece):
        for n, (its_kind, its_where, start, wide, _) in enumerate(UNITS):
            if (its_kind, its_where) == (kind, where):
                grad = getattr(v, "u%d_grad" % n)
                for b in range(0, wide, 128):
                    grad[..., b : b + 128] = piece(start + b).reshape(4, 2, 2, 32, 128)
                landed = getattr(v, "u%d_core" % n)
                core_copies[n] = send(n, grad.at[:, :, 1 - c], landed, core_peer, "core")
                queue[n] = unit_steps(n)

    def section_up(t):
        arrive("up")
        cols = slice(t * width, (t + 1) * width)
        up = dot(v.hidden2_v[...], v.w_up_v[:, cols])
        v.up_proj_v[:, cols] = up
        v.activation_v[:, cols] = (up * (1.0 / (1.0 + jnp.exp(-up)))).astype(BF16)

    def section_mask():
        arrive("down")
        v.d_branch_v[...] = (mask * v.cot_v[...]).astype(BF16)

    def section_dup(t):
        cols = slice(t * width, (t + 1) * width)
        up = v.up_proj_v[:, cols]
        sigmoid = 1.0 / (1.0 + jnp.exp(-up))
        d_act = dot_nt(v.d_branch_v[...], v.w_down_v[t * width : (t + 1) * width, :])
        v.d_up_v[:, cols] = (d_act * sigmoid * (1.0 + up * (1.0 - sigmoid))).astype(BF16)

    def section_gd(h):
        value = dot_tn(v.activation_v[...], v.d_branch_v[:, h * 256 : (h + 1) * 256]).astype(BF16)
        value = value.reshape(GROUP, 4, 32, 256)
        for k in range(2):
            produce("d", 2 * h + k, lambda start: value[:, start // 128, :, k * 128 : (k + 1) * 128])

    def section_gu(t):
        value = dot_tn(v.hidden2_v[...], v.d_up_v[:, t * width : (t + 1) * width]).astype(BF16)
        produce("u", t, lambda start: value[:, start : start + 128])

    def section_out():
        branch = dot(v.activation_v[:, 0:width], v.w_down_v[0:width, :])
        for t in range(1, tiles):
            branch = branch + dot(v.activation_v[:, t * width : (t + 1) * width], v.w_down_v[t * width : (t + 1) * width, :])
        v.out_v[0] = v.middle_v[...] + mask * branch

    def section_mid():
        d_hidden2 = dot_nt(v.d_up_v[:, 0:width], tile(v.w_up_v, 0))
        for t in range(1, tiles):
            d_hidden2 = d_hidden2 + dot_nt(v.d_up_v[:, t * width : (t + 1) * width], tile(v.w_up_v, t))
        normed2 = v.normed2_v[...]
        v.mod_v[1, :, 0:width] = jnp.sum(d_hidden2 * normed2, axis=0, keepdims=True)
        v.mod_v[1, :, width : 2 * width] = jnp.sum(d_hidden2, axis=0, keepdims=True)
        queue["m1"] = mod_steps(1)
        d_middle = v.cot_v[...] + norm_back(d_hidden2 * (1.0 + scale2), normed2, inv2)
        v.d_middle_v[...] = d_middle
        v.d_attended_v[...] = (mask * d_middle).astype(BF16)
        v.d_mix_v[...] = dot_nt(v.d_attended_v[...], v.w_out_v[...]).astype(BF16)

    def section_go():
        value = dot_tn(v.mix_v[...], v.d_attended_v[...]).astype(BF16)
        produce("o", 0, lambda start: value[:, start : start + 128])

    def section_attn(h):
        cols = slice(h * head, (h + 1) * head)
        attn = v.attn_v[h]
        d_attn = dot_nt(v.v_v[:, cols], v.d_mix_v[:, cols])
        inner = jnp.sum(attn * d_attn, axis=0, keepdims=True)
        d_scores = (attn * (d_attn - inner)).astype(BF16)
        v.d_q_v[:, cols] = (dot_tn(d_scores, v.k_v[:, cols]) * factor).astype(BF16)
        v.d_k_v[:, cols] = (dot(d_scores, v.q_v[:, cols]) * factor).astype(BF16)
        v.d_v_v[:, cols] = dot(attn.astype(BF16), v.d_mix_v[:, cols]).astype(BF16)

    def section_gq(h):
        cols = slice(h * head, (h + 1) * head)
        values = [
            dot_tn(v.table_v[0:nodes, :], v.d_q_v[:, cols]).astype(BF16),
            dot_tn(v.table_v[...], v.d_k_v[:, cols]).astype(BF16),
            dot_tn(v.table_v[...], v.d_v_v[:, cols]).astype(BF16),
        ]
        produce("h", h, lambda start: values[start // 128])

    back = []

    def section_table():
        d_table = dot_nt(v.d_k_v[...], tile(v.w_qkv_v, 1)) + dot_nt(v.d_v_v[...], tile(v.w_qkv_v, 2))
        v.lend_back_v[...] = d_table[nodes:table, :].astype(BF16)
        back.append(send("back", v.lend_back_v.at[0:half], v.returned_v.at[half:lent], before, 2))
        back.append(send("back", v.lend_back_v.at[half:lent], v.returned_v.at[0:half], after, 3))
        d_hidden1 = d_table[0:nodes, :] + dot_nt(v.d_q_v[...], tile(v.w_qkv_v, 0))
        v.d_hidden1_v[...] = d_hidden1
        d_lent = d_table[nodes:table, :]
        v.mod_v[0, :, 0:width] = jnp.sum(d_hidden1 * v.normed1_v[...], axis=0, keepdims=True) + jnp.sum(
            d_lent * v.halo_v[...].astype(F32), axis=0, keepdims=True
        )
        v.mod_v[0, :, width : 2 * width] = jnp.sum(d_hidden1, axis=0, keepdims=True) + jnp.sum(
            d_lent, axis=0, keepdims=True
        )
        queue["m0"] = mod_steps(0)

    def section_state():
        for copy in back:
            copy.arrive()
        d_hidden1 = v.d_hidden1_v[...] + dot(pick, v.returned_v[...])
        normed1 = v.normed1_v[...]
        v.d_states_v[0] = v.d_middle_v[...] + norm_back(d_hidden1 * (1.0 + scale1), normed1, inv1)

    def mod_steps(part):
        own, from_core, plane, rows = v.mod_v.at[part], v.mod_core_v.at[part], v.mods_v.at[part], v.rows_v.at[part]
        name = "m%d" % part
        copies = [send(name, own, from_core, core_peer, "core")]

        def spread():
            copies.pop().arrive()
            plane[0] = own[...] + from_core[...]
            for d in range(1, 8):
                there = lax.rem(z + d // 2, 4)
                target = z_peer(there) if d % 2 == 0 else z_x_peer(there)
                send(name, plane.at[0], plane.at[d], target, "plane")
            copies.append(message(name, plane.at[pl.ds(1, 7)], plane.at[pl.ds(1, 7)], x_peer, "plane"))

        def swap():
            copies.pop().arrive()
            total = jnp.zeros(own.shape, F32)
            for there in range(4):
                for side in range(2):
                    total = total + plane[lax.rem(z + 4 - there, 4) * 2 + lax.rem(x + side, 2)]
            rows[r] = total
            copies.append(send(name, rows.at[r], rows.at[r], y_peer, "y"))

        def spend():
            copies.pop().arrive()
            first_row, second_row = rows[0], rows[1]
            here = slice(part * 2 * width, (part + 1) * 2 * width)
            if not finish:
                v.d_noise_v[0:1, here] = first_row
                v.d_noise_v[1:2, here] = second_row
                return
            row = lax.broadcasted_iota(jnp.int32, (16, 2 * width), 0)
            stacked = jnp.zeros((16, 2 * width), F32)
            for number, piece in enumerate(split3(first_row) + split3(second_row)):
                stacked = jnp.where(row == number, piece, stacked)
            noise = dot_nt(stacked.astype(BF16), v.w_cond_v[part])
            first_noise = jnp.sum(noise[0:3], axis=0, keepdims=True)
            second_noise = jnp.sum(noise[3:6], axis=0, keepdims=True)
            if part == 1:
                v.noise_part_v[0:1, :] = first_noise
                v.noise_part_v[1:2, :] = second_noise
            else:
                v.d_noise_v[0:1, :] = first_noise + v.noise_part_v[0:1, :]
                v.d_noise_v[1:2, :] = second_noise + v.noise_part_v[1:2, :]
            shape = (v.d_cond_v.shape[0], width)
            mine = lax.broadcasted_iota(jnp.int32, shape, 1) == (
                lax.broadcasted_iota(jnp.int32, shape, 0) + p * shape[0]
            )
            picked = [
                jnp.sum(jnp.where(mine, v.noise_v[b : b + 1, :], 0.0), axis=1, keepdims=True)
                for b in range(2)
            ]
            v.d_cond_v[:, here] = picked[0] * first_row + picked[1] * second_row

        return [spread, swap, spend]

    sections = {
        "up": section_up,
        "mask": section_mask,
        "dup": section_dup,
        "gd": section_gd,
        "gu": section_gu,
        "out": section_out,
        "mid": section_mid,
        "go": section_go,
        "attn": section_attn,
        "gq": section_gq,
        "table": section_table,
        "state": section_state,
    }
    for entry in ORDER:
        if entry in queue:
            queue[entry].pop(0)()
        elif isinstance(entry, tuple):
            sections[entry[0]](entry[1])
        else:
            sections[entry]()
    for steps in queue.values():
        for step in steps:
            step()

    for n in range(len(UNITS)):
        all_left(n, getattr(v, "u%d_grad" % n))
    for part in range(2):
        all_left("m%d" % part, v.mods_v.at[part])
    all_left("halo", v.lend_v)
    all_left("back", v.lend_back_v)


def copy_out(count, *refs):
    for n in range(count):
        src, dst = refs[n], refs[count + n]
        rows = src.shape[-2]
        pieces = 4 if rows % 64 == 0 else 1
        for k in range(pieces):
            at = (*[slice(None)] * (len(src.shape) - 2), slice(k * rows // pieces, (k + 1) * rows // pieces))
            pltpu.make_async_copy(src.at[at], dst.at[at], refs[-1].at[n]).start()
    for n in range(count):
        pltpu.make_async_copy(refs[n], refs[count + n], refs[-1].at[n]).wait()


def body(
    node_state,
    noise_embed,
    w_cond,
    w_qkv,
    w_out,
    w_up,
    w_down,
    neighbours,
    send_rows,
    valid,
    cotangent,
):
    nodes, width = node_state.shape[1:]
    hidden = w_up.shape[1]
    lent = send_rows.shape[0]
    table = nodes + lent
    patches = lax.axis_size("patch")
    fold = patches // GROUP
    rows_each = width // patches
    block = width // GROUP
    half = width // 2

    hbm = pl.BlockSpec(memory_space=pl.ANY)
    vmem = pl.BlockSpec(memory_space=pltpu.VMEM)
    inputs = [
        ("states_hbm", node_state, hbm),
        ("noise_hbm", noise_embed, hbm),
        ("w_cond_hbm", w_cond, hbm),
        ("w_qkv_hbm", w_qkv, hbm),
        ("w_out_hbm", w_out, hbm),
        ("w_up_hbm", w_up, hbm),
        ("w_down_hbm", w_down, hbm),
        ("neighbours_hbm", neighbours.T, hbm),
        ("send_hbm", send_rows[None, :], hbm),
        ("valid_hbm", valid[None, :], hbm),
        ("cot_hbm", cotangent, hbm),
    ]
    outputs = [
        ("out_v", node_state.shape, vmem),
        ("d_states_v", node_state.shape, vmem),
        ("down_v", (hidden // GROUP, width), vmem),
        ("up_v", (block, hidden), vmem),
        ("o_v", (block, width), vmem),
        ("qkv_v", (block, 3 * width), vmem),
    ]
    if fold == 1:
        outputs += [("d_noise_v", noise_embed.shape, vmem), ("d_cond_v", (rows_each, 4 * width), vmem)]
    else:
        outputs += [("d_noise_v", (noise_embed.shape[0], 4 * width), vmem)]
    tiles = hidden // width
    receivers = receive_plan()[1]
    scratch = [
        ("noise_v", noise_embed.shape, F32),
        ("neighbours_v", neighbours.shape[::-1], jnp.int32),
        ("pick_v", (1, lent), jnp.int32),
        ("valid_v", (1, nodes), jnp.int32),
        ("states_v", (nodes, width), F32),
        ("cot_v", (nodes, width), F32),
        ("w_cond_v", (2, width, 2 * width), BF16),
        ("w_qkv_v", w_qkv.shape, BF16),
        ("w_out_v", (width, width), BF16),
        ("w_up_v", w_up.shape, BF16),
        ("w_down_v", w_down.shape, BF16),
        ("normed1_v", (nodes, width), F32),
        ("table_v", (table, width), BF16),
        ("lend_v", (lent, width), BF16),
        ("halo_v", (lent, width), BF16),
        ("returned_v", (lent, width), BF16),
        ("q_v", (nodes, width), BF16),
        ("k_v", (table, width), BF16),
        ("v_v", (table, width), BF16),
        ("count_v", (table, nodes), BF16),
        ("attn_v", (HEADS, table, nodes), F32),
        ("mix_v", (nodes, width), BF16),
        ("middle_v", (nodes, width), F32),
        ("normed2_v", (nodes, width), F32),
        ("hidden2_v", (nodes, width), BF16),
        ("d_branch_v", (nodes, width), BF16),
        ("d_mix_v", (nodes, width), BF16),
        ("d_q_v", (nodes, width), BF16),
        ("d_k_v", (table, width), BF16),
        ("d_v_v", (table, width), BF16),
        ("mod_v", (2, 1, 2 * width), F32),
        ("mod_core_v", (2, 1, 2 * width), F32),
        ("mods_v", (2, 9, 1, 2 * width), F32),
        ("rows_v", (2, 2, 1, 2 * width), F32),
        ("noise_part_v", noise_embed.shape, F32),
        ("up_proj_v", (nodes, hidden), F32),
        ("activation_v", (nodes, hidden), BF16),
        ("d_up_v", (nodes, hidden), BF16),
        ("d_middle_v", (nodes, width), F32),
        ("d_attended_v", (nodes, width), BF16),
        ("d_hidden1_v", (nodes, width), F32),
        ("lend_back_v", (lent, width), BF16),
    ]
    for n, (_, _, _, wide, flow) in enumerate(UNITS):
        name = "u%d" % n
        rows = 16 if flow[0] == "C" else 32
        part = (2, 32, wide) if flow[0] == "B" else (rows, wide)
        buffers = [("_grad", (4, 2, 2, 32, wide)), ("_core", (4, 2, 32, wide))]
        buffers += [("_mine", (4, 2, 2, 16, wide) if flow[0] == "C" else (4, 2, 32, wide))]
        buffers += [("_result", (rows, wide)), ("_received", (rows, wide))]
        if flow[0] == "G":
            buffers += [("_plane", (7, rows, wide))]
        else:
            buffers += [("_x", (rows, wide) if flow[0] == "B" else (4, rows, wide))]
            if flow[0] == "C":
                buffers += [("_y", (4, 2, 16, wide))]
            if flow[0] == "B":
                buffers += [("_pair", part)]
            if flow[1:] == "d":
                buffers += [("_landing", (3, *part))]
            else:
                buffers += [("_triple", (3, *part)), ("_single", part), ("_middle", part), ("_comb", (2, *part))]
        scratch += [(name + suffix, shape, BF16) for suffix, shape in buffers]
    semaphores = [
        ("load_sem", pltpu.SemaphoreType.DMA((12,))),
        ("send_sem", pltpu.SemaphoreType.DMA((len(UNITS) + 4,))),
        ("recv_sem", pltpu.SemaphoreType.DMA((receivers,))),
    ]
    names = [n for group in (inputs, outputs, scratch, semaphores) for n in [e[0] for e in group]]
    results = pl.pallas_call(
        functools.partial(kernel, fold, patches, names),
        out_shape=[pltpu.VMEM(shape, F32) for _, shape, _ in outputs],
        in_specs=[spec for _, _, spec in inputs],
        out_specs=[spec for _, _, spec in outputs],
        scratch_shapes=[pltpu.VMEM(shape, dtype) for _, shape, dtype in scratch]
        + [sem for _, sem in semaphores],
        compiler_params=pltpu.CompilerParams(
            collective_id=0, has_side_effects=True, vmem_limit_bytes=44 * 1024 * 1024
        ),
    )(
        *[pltpu.with_memory_space_constraint(array, pltpu.HBM) for _, array, _ in inputs]
    )
    if fold == 1:
        results = pl.pallas_call(
            functools.partial(copy_out, len(results)),
            out_shape=[jax.ShapeDtypeStruct(a.shape, a.dtype) for a in results],
            in_specs=[hbm] * len(results),
            out_specs=[hbm] * len(results),
            scratch_shapes=[pltpu.SemaphoreType.DMA((len(results),))],
            compiler_params=pltpu.CompilerParams(vmem_limit_bytes=1024 * 1024),
        )(*results)
    output, d_state, g_down, g_up, g_out, g_qkv = results[:6]
    if fold == 1:
        grad_noise, grad_cond = results[6:]
    else:
        groups = [[m * fold + i for i in range(fold)] for m in range(GROUP)]

        def rest(array):
            return lax.psum_scatter(
                array, "patch", scatter_dimension=0, axis_index_groups=groups, tiled=True
            )

        g_down, g_up, g_out, g_qkv = rest(g_down), rest(g_up), rest(g_out), rest(g_qkv)
        mods = lax.psum(results[6], "patch") / GROUP
        highest = lax.Precision.HIGHEST
        grad_noise = jnp.dot(mods, w_cond.astype(F32).T, precision=highest)
        first_row = lax.axis_index("patch") * rows_each
        cond_cols = lax.dynamic_slice_in_dim(noise_embed, first_row, rows_each, 1)
        grad_cond = jnp.dot(cond_cols.T, mods, precision=highest)
    return output, d_state, grad_noise, grad_cond, g_qkv, g_out, g_up, g_down


def solution(mesh):
    in_specs = (
        P("rep", "patch", None),
        P(),
        P(),
        P(),
        P(),
        P(),
        P(),
        P("patch", None),
        P("patch"),
        P("patch"),
        P("rep", "patch", None),
    )
    out_specs = (
        P("rep", "patch", None),
        P("rep", "patch", None),
        P(),
        P("patch", None),
        P("patch", None),
        P("patch", None),
        P("patch", None),
        P("patch", None),
    )
    return jax.shard_map(body, mesh=mesh, in_specs=in_specs, out_specs=out_specs, check_vma=False)
```

```python
import functools

import jax
import jax.numpy as jnp
from jax import lax
from jax.experimental import pallas as pl
from jax.experimental.pallas import tpu as pltpu
from jax.sharding import PartitionSpec as P

HEADS = 4
GROUP = 16
UNITS = (
    ("d", 0, 0, 512, "Cd"), ("d", 1, 0, 512, "Ad"), ("d", 2, 0, 256, "Bd"), ("d", 2, 256, 256, "C"),
    ("d", 3, 0, 256, "Ad"), ("d", 3, 256, 256, "B"), ("u", 0, 0, 256, "Cd"),
    ("u", 0, 256, 256, "C"), ("u", 1, 0, 512, "A"), ("u", 2, 0, 512, "C"), ("u", 3, 0, 256, "B"),
    ("u", 3, 256, 256, "Bd"), ("o", 0, 0, 512, "C"), ("h", 0, 0, 384, "Cd"), ("h", 1, 0, 128, "Ad"),
    ("h", 1, 128, 256, "Cd"), ("h", 2, 0, 128, "Cd"), ("h", 2, 128, 256, "Ad"),
    ("h", 3, 0, 128, "A"), ("h", 3, 128, 256, "Cd"),
)
ORDER = (
    ("up", 2), "mask", ("up", 0), ("up", 3), ("up", 1), ("gd", 1), ("dup", 3), ("gd", 0), 2, 3,
    ("dup", 1), 4, ("gu", 3), ("dup", 0), 0, 5, ("gu", 0), 1, ("dup", 2), ("gu", 1), 11, "mid", 7,
    ("gu", 2), 10, 8, 6, "go", 4, ("attn", 1), ("attn", 2), ("gq", 1), 12, 1, 9, 14, ("attn", 3),
    ("gq", 3), 5, 3, 7, "m1", 18, 6, 0, ("gq", 2), 16, 8, 3, 10, 14, 15, ("attn", 0), 17, 12, 19,
    ("gq", 0), 18, 7, "table", 6, 9, 13, 0, 8, "m1", 15, 12, 3, 17, 19, 5, 18, 16, 7, 10, 4, 1, 13,
    9, "m0", 14, 11, 2, 15, 19, 8, 18, 16, 5, 6, 12, 13, 17, 9, 10, "out", 7, 14, 3, 0, 11, "state",
    18, 5, 12, 2, 15, "m0", 4, 16, 19, 8, 6, 9, 17, 1, 7, 13, 10, 3, "m1", 15, 16, 2, 0, 19, 12, 9,
    "m0", 11, 13,
)
MESH = pl.DeviceIdType.MESH
F32 = jnp.float32
BF16 = jnp.bfloat16


def dot(a, b):
    return lax.dot_general(a, b, (((1,), (0,)), ((), ())), preferred_element_type=F32)


def dot_nt(a, b):
    return lax.dot_general(a, b, (((1,), (1,)), ((), ())), preferred_element_type=F32)


def dot_tn(a, b):
    return lax.dot_general(a, b, (((0,), (0,)), ((), ())), preferred_element_type=F32)


def split3(v):
    high = v.astype(BF16)
    rest = v - high.astype(F32)
    mid = rest.astype(BF16)
    low = (rest - mid.astype(F32)).astype(BF16)
    return high.astype(F32), mid.astype(F32), low.astype(F32)


def layer_norm(values):
    centred = values - jnp.mean(values, axis=-1, keepdims=True)
    inv_std = lax.rsqrt(jnp.mean(centred * centred, axis=-1, keepdims=True) + 1e-05)
    return centred * inv_std, inv_std


def norm_back(gradient, normed, inv_std):
    first = jnp.mean(gradient, axis=-1, keepdims=True)
    second = jnp.mean(gradient * normed, axis=-1, keepdims=True)
    return (gradient - first - normed * second) * inv_std


ROUTES = {
    "A": (("core", -1, 0), ("x", 0, 1), ("first", 1, 3), ("middle", 2, 3), ("y", 3, 4)),
    "Ad": (("core", -1, 0), ("x", 0, 1), ("z", 1, 2), ("y", 2, 3)),
    "B": (("core", -1, 0), ("first", 0, 2), ("middle", 1, 2), ("x", 2, 3), ("y", 3, 4)),
    "Bd": (("core", -1, 0), ("z", 0, 1), ("x", 1, 2), ("y", 2, 3)),
    "C": (("core", -1, 0), ("early y", 0, 1), ("x", 1, 2), ("first", 2, 4), ("middle", 3, 4), ("y", 4, 5)),
    "Cd": (("core", -1, 0), ("early y", 0, 1), ("x", 1, 2), ("z", 2, 3), ("y", 3, 4)),
    "G": (("core", -1, 0), ("plane", 0, 1), ("y", 1, 2)),
    "M": (("core", -1, 0), ("plane", 0, 1), ("y", 1, 2)),
}
SOURCE = {"d": lambda w: ("gd", w // 2), "u": lambda w: ("gu", w), "o": lambda w: "go", "h": lambda w: ("gq", w)}


def receive_plan():
    steps = {}
    for position, entry in enumerate(ORDER):
        steps.setdefault(entry, []).append(position)
    copies = []
    for n, (kind, where, _, _, route) in enumerate(UNITS):
        copies += [(n, steps[SOURCE[kind](where)][0], *copy) for copy in ROUTES[route]]
    for name, source in (("m1", "mid"), ("m0", "table")):
        copies += [(name, steps[source][0], *copy) for copy in ROUTES["M"]]
    timed = []
    for n, start, what, sender, waiter in copies:
        timed.append((start if sender < 0 else steps[n][sender], steps[n][waiter], what, n))
    timed.sort(key=lambda copy: copy[0])
    kinds = {"early y": "y", "middle": "first"}

    def answered(send, kind, waited):
        return any(
            kinds.get(what, what) == kind and what != "middle" and waited <= sent and got <= send
            for sent, got, what, _ in timed
        )

    numbers, free = {}, [(-1, 0), (-1, 1)]
    count = 4
    for send, got, what, n in timed:
        kind = kinds.get(what, what)
        fit = [entry for entry in free if answered(send, kind, entry[0])]
        if fit:
            entry = max(fit)
            free.remove(entry)
            number = entry[1]
        else:
            number, count = count, count + 1
        numbers[n, what] = number
        free.append((got, number))
    return numbers, count


class Names:
    pass


class Message:
    def __init__(self, v, outgoing, receive, src, dst, target):
        self.parts = dict(
            src_ref=src,
            dst_ref=dst,
            send_sem=v.send_sem.at[outgoing],
            recv_sem=v.recv_sem.at[receive],
            device_id=target,
            device_id_type=MESH,
        )

    def start(self):
        pltpu.make_async_remote_copy(**self.parts).start()

    def arrive(self):
        pltpu.make_async_remote_copy(**self.parts).wait_recv()

    def leave(self):
        pltpu.make_async_remote_copy(**self.parts).wait_send()


def kernel(fold, patches, names, *refs):
    v = Names()
    for name, ref in zip(names, refs):
        setattr(v, name, ref)
    p = lax.axis_index("patch")
    r = lax.axis_index("rep")
    member = p // fold
    lane = lax.rem(p, fold)
    c = lax.rem(member, 2)
    x = lax.rem(member // 2, 2)
    z = member // 4
    finish = fold == 1

    def device(index, rep=r):
        return (index * fold + lane, rep)

    before = (lax.rem(p + patches - 1, patches), r)
    after = (lax.rem(p + 1, patches), r)
    core_peer = device(member + 1 - 2 * c)
    x_peer = device(member + 2 - 4 * x)
    y_peer = (p, 1 - r)

    def z_peer(there):
        return device(there * 4 + x * 2 + c)

    def z_x_peer(there):
        return device(there * 4 + (1 - x) * 2 + c)

    nodes, width = v.states_hbm.shape[1:]
    tiles = v.w_up_hbm.shape[1] // width
    head = width // HEADS
    factor = head ** (-0.5)
    table = v.k_v.shape[0]
    lent = table - nodes
    half = lent // 2

    loads = {}
    loaded = [0]

    def load(key, *pairs):
        copies = []
        for src, dst in pairs:
            copy = pltpu.make_async_copy(src, dst, v.load_sem.at[loaded[0]])
            loaded[0] += 1
            copy.start()
            copies.append(copy)
        loads[key] = copies

    def arrive(key):
        for copy in loads.pop(key, ()):
            copy.wait()

    load("states", (v.states_hbm.at[0], v.states_v), (v.send_hbm, v.pick_v))

    barrier = pltpu.get_barrier_semaphore()
    others = [before, after, core_peer, x_peer, y_peer] + [z_peer(lax.rem(z + d, 4)) for d in range(1, 4)]
    others += [z_x_peer(lax.rem(z + d, 4)) for d in range(1, 4)]
    for other in others:
        pl.semaphore_signal(barrier, inc=1, device_id=other, device_id_type=MESH)

    load("cond1", (v.noise_hbm, v.noise_v), (v.w_cond_hbm.at[:, 0 : 2 * width], v.w_cond_v.at[0]))
    load("index", (v.neighbours_hbm, v.neighbours_v), (v.valid_hbm, v.valid_v))
    load("qkv", (v.w_qkv_hbm, v.w_qkv_v))
    load("cond2", (v.w_cond_hbm.at[:, 2 * width : 4 * width], v.w_cond_v.at[1]))

    def tile(ref, t):
        return ref[:, t * width : (t + 1) * width]

    numbers, _ = receive_plan()
    outgoing = {n: n for n in range(len(UNITS))}
    for name in ("m0", "m1", "halo", "back"):
        outgoing[name] = len(outgoing)

    def message(n, src, dst, target, receive):
        return Message(v, outgoing[n], numbers.get((n, receive), receive), src, dst, target)

    def send(n, src, dst, target, receive):
        copy = message(n, src, dst, target, receive)
        copy.start()
        return copy

    def all_left(n, ref):
        message(n, ref, ref, x_peer, 0).leave()

    arrive("states")
    normed1, inv1 = layer_norm(v.states_v[...])
    v.normed1_v[...] = normed1
    pick = (v.pick_v[...] == lax.broadcasted_iota(jnp.int32, (nodes, lent), 0)).astype(BF16)
    v.lend_v[...] = dot_tn(pick, normed1.astype(BF16)).astype(BF16)
    pl.semaphore_wait(barrier, len(others))
    halo = [
        send("halo", v.lend_v.at[0:half], v.halo_v.at[half:lent], before, 0),
        send("halo", v.lend_v.at[half:lent], v.halo_v.at[0:half], after, 1),
    ]

    load("out", (v.w_out_hbm, v.w_out_v))
    load("up", (v.w_up_hbm, v.w_up_v))
    load("down", (v.cot_hbm.at[0], v.cot_v), (v.w_down_hbm, v.w_down_v))

    for key in ("cond1", "index", "qkv", "cond2"):
        arrive(key)
    condition = v.noise_v[pl.ds(r, 1), :]
    row = lax.broadcasted_iota(jnp.int32, (16, width), 0)
    high, mid, low = split3(condition)
    stacked = jnp.where(row == 0, high, jnp.where(row == 1, mid, jnp.where(row == 2, low, 0.0))).astype(BF16)
    mod1 = jnp.sum(dot(stacked, v.w_cond_v[0]), axis=0, keepdims=True)
    scale1, shift1 = mod1[:, :width], mod1[:, width:]
    hidden1 = (v.normed1_v[...] * (1.0 + scale1) + shift1).astype(BF16)
    v.table_v[0:nodes, :] = hidden1

    v.k_v[0:nodes, :] = dot(hidden1, tile(v.w_qkv_v, 1)).astype(BF16)
    v.v_v[0:nodes, :] = dot(hidden1, tile(v.w_qkv_v, 2)).astype(BF16)
    v.q_v[...] = dot(hidden1, tile(v.w_qkv_v, 0)).astype(BF16)

    ids = v.neighbours_v[...].astype(jnp.int16)
    entry = lax.broadcasted_iota(jnp.int32, (table, nodes), 0).astype(jnp.int16)
    count = jnp.zeros((table, nodes), BF16)
    for j in range(ids.shape[0]):
        count = jnp.where(ids[j : j + 1, :] == entry, count + jnp.ones_like(count), count)
    v.count_v[...] = count

    mod2 = jnp.sum(dot(stacked, v.w_cond_v[1]), axis=0, keepdims=True)
    scale2, shift2 = mod2[:, :width], mod2[:, width:]
    real = jnp.sum(v.valid_v[...], axis=1, keepdims=True)
    mask = (lax.broadcasted_iota(jnp.int32, (nodes, 1), 0) < real).astype(F32)

    for copy in halo:
        copy.arrive()
    rows = (v.halo_v[...].astype(F32) * (1.0 + scale1) + shift1).astype(BF16)
    v.table_v[nodes:table, :] = rows
    v.k_v[nodes:table, :] = dot(rows, tile(v.w_qkv_v, 1)).astype(BF16)
    v.v_v[nodes:table, :] = dot(rows, tile(v.w_qkv_v, 2)).astype(BF16)

    for h in range(HEADS):
        cols = slice(h * head, (h + 1) * head)
        scores = dot_nt(v.k_v[:, cols], v.q_v[:, cols]) * factor
        times = v.count_v[...].astype(F32)
        scores = jnp.where(times > 0.0, scores, -1e30)
        exponent = times * jnp.exp(scores - jnp.max(scores, axis=0, keepdims=True))
        attn = exponent * (1.0 / jnp.sum(exponent, axis=0, keepdims=True))
        v.attn_v[h] = attn
        v.mix_v[:, cols] = dot_tn(attn.astype(BF16), v.v_v[:, cols]).astype(BF16)

    arrive("out")
    middle = v.states_v[...] + mask * dot(v.mix_v[...], v.w_out_v[...])
    v.middle_v[...] = middle
    normed2, inv2 = layer_norm(middle)
    v.normed2_v[...] = normed2
    v.hidden2_v[...] = (normed2 * (1.0 + scale2) + shift2).astype(BF16)

    def exchange_z(own, name, n):
        triple, single, middle_in, comb = (
            getattr(v, name + "_triple"),
            getattr(v, name + "_single"),
            getattr(v, name + "_middle"),
            getattr(v, name + "_comb"),
        )
        outer = (z == 0) | (z == 3)
        outer_z = jnp.where(z < 2, 0, 3)
        other_inner = jnp.where(z < 2, 2, 1)
        other_outer = 3 - outer_z
        near_inner = jnp.where(z < 2, 1, 2)
        first = jnp.where(z == 0, 1, 0)
        offset = jnp.where(z == 1, 1, 0)
        to_inner = message(n, own.at[pl.ds(first, 3)], triple, z_peer(near_inner), "first")
        to_outer = message(n, own.at[outer_z], single, z_peer(outer_z), "first")
        across = message(n, comb.at[0], middle_in, z_peer(other_inner), "middle")
        beyond = message(n, comb.at[1], middle_in, z_peer(other_outer), "middle")

        def begin():
            @pl.when(outer)
            def _():
                to_inner.start()

            @pl.when(jnp.logical_not(outer))
            def _():
                to_outer.start()

        def combine():
            @pl.when(jnp.logical_not(outer))
            def _():
                to_inner.arrive()
                comb[1] = own[other_outer] + triple[other_outer - offset]
                beyond.start()
                comb[0] = own[other_inner] + triple[other_inner - offset]
                across.start()

        def finish_sum(result):
            across.arrive()

            @pl.when(outer)
            def _():
                to_outer.arrive()
                total = own[z].astype(F32) + single[...].astype(F32) + middle_in[...].astype(F32)
                result[...] = total.astype(BF16)

            @pl.when(jnp.logical_not(outer))
            def _():
                total = own[z].astype(F32) + triple[z - offset].astype(F32) + middle_in[...].astype(F32)
                result[...] = total.astype(BF16)

        return begin, combine, finish_sum

    def direct_z(own, name, n):
        landing = getattr(v, name + "_landing")

        def begin():
            for d in range(1, 4):
                there = lax.rem(z + d, 4)
                send(n, own.at[there], landing.at[d - 1], z_peer(there), "z")

        def finish_sum(result):
            message(n, landing, landing, x_peer, "z").arrive()
            total = own[z].astype(F32)
            for d in range(3):
                total = total + landing[d].astype(F32)
            result[...] = total.astype(BF16)

        return begin, finish_sum

    queue = {}
    core_copies = {}

    def place(n, value, part=None):
        kind, where, start, wide, _ = UNITS[n]
        rows = value.shape[0]

        def at(first):
            return pl.ds(first if part is None else pl.multiple_of(first + part * rows, rows), rows)

        if kind == "d":
            for b in range(wide // 128):
                block = value[:, b * 128 : (b + 1) * 128]
                v.down_v[at((start // 128 + b) * 32), where * 128 : (where + 1) * 128] = block
        elif kind == "u":
            first = where * width + start
            v.up_v[at(0), first : first + wide] = value
        elif kind == "o":
            v.o_v[at(0), start : start + wide] = value
        else:
            for b in range(wide // 128):
                first = (start // 128 + b) * width + where * 128
                v.qkv_v[at(0), first : first + 128] = value[:, b * 128 : (b + 1) * 128]

    def unit_steps(n):
        name, flow = "u%d" % n, UNITS[n][4]
        grad, landed, mine = (getattr(v, name + suffix) for suffix in ("_grad", "_core", "_mine"))
        result, received = getattr(v, name + "_result"), getattr(v, name + "_received")
        direct = flow[1:] == "d"
        copies = {}

        def core_sum():
            core_copies[n].arrive()
            total = grad[:, :, c] + landed[...]
            mine[...] = total.reshape(mine.shape)

        def y_exchange():
            copies["last"] = send(n, result, received, y_peer, "y")

        def ending():
            copies["last"].arrive()
            if flow[0] == "C":
                place(n, result[...].astype(F32), r)
                place(n, received[...].astype(F32), 1 - r)
            else:
                place(n, result[...].astype(F32) + received[...].astype(F32))

        def reduce_z(own, then):
            if direct:
                begin, finish_sum = direct_z(own, name, n)
                middle_steps = []
            else:
                begin, combine, finish_sum = exchange_z(own, name, n)
                middle_steps = [combine]

            def last():
                finish_sum(then[0])
                then[1]()

            return begin, middle_steps + [last]

        if flow[0] == "G":
            plane = getattr(v, name + "_plane")

            def start():
                core_sum()
                for d in range(1, 8):
                    there = lax.rem(z + d // 2, 4)
                    target = z_peer(there) if d % 2 == 0 else z_x_peer(there)
                    send(n, mine.at[there, x if d % 2 == 0 else 1 - x], plane.at[d - 1], target, "plane")
                copies["plane"] = message(n, plane, plane, x_peer, "plane")

            def second():
                copies["plane"].arrive()
                total = mine[z, x].astype(F32)
                for d in range(7):
                    total = total + plane[d].astype(F32)
                result[...] = total.astype(BF16)
                y_exchange()

            return [start, second, ending]
        if flow[0] == "A":
            from_x = getattr(v, name + "_x")
            begin, rest = reduce_z(from_x, (result, y_exchange))

            def start():
                core_sum()
                copies["x"] = send(n, mine.at[:, 1 - x], from_x, x_peer, "x")

            def second():
                copies["x"].arrive()
                from_x[...] = mine[:, x] + from_x[...]
                begin()

            return [start, second] + rest + [ending]
        if flow[0] == "C":
            from_y, from_x = getattr(v, name + "_y"), getattr(v, name + "_x")
            begin, rest = reduce_z(from_x, (result, y_exchange))

            def start():
                core_sum()
                copies["y"] = send(n, mine.at[:, :, 1 - r], from_y, y_peer, "early y")

            def second():
                copies["y"].arrive()
                from_y[...] = mine[:, :, r] + from_y[...]
                copies["x"] = send(n, from_y.at[:, 1 - x], from_x, x_peer, "x")

            def third():
                copies["x"].arrive()
                from_x[...] = from_y[:, x] + from_x[...]
                begin()

            return [start, second, third] + rest + [ending]
        pair, from_x = getattr(v, name + "_pair"), getattr(v, name + "_x")

        def x_exchange():
            copies["x"] = send(n, pair.at[1 - x], from_x, x_peer, "x")

        begin, rest = reduce_z(mine, (pair, x_exchange))

        def start():
            core_sum()
            begin()

        def after_x():
            copies["x"].arrive()
            result[...] = pair[x] + from_x[...]
            y_exchange()

        return [start] + rest + [after_x, ending]

    def produce(kind, where, piece):
        for n, (its_kind, its_where, start, wide, _) in enumerate(UNITS):
            if (its_kind, its_where) == (kind, where):
                grad = getattr(v, "u%d_grad" % n)
                for b in range(0, wide, 128):
                    grad[..., b : b + 128] = piece(start + b).reshape(4, 2, 2, 32, 128)
                landed = getattr(v, "u%d_core" % n)
                core_copies[n] = send(n, grad.at[:, :, 1 - c], landed, core_peer, "core")
                queue[n] = unit_steps(n)

    def section_up(t):
        arrive("up")
        cols = slice(t * width, (t + 1) * width)
        up = dot(v.hidden2_v[...], v.w_up_v[:, cols])
        v.up_proj_v[:, cols] = up
        v.activation_v[:, cols] = (up * (1.0 / (1.0 + jnp.exp(-up)))).astype(BF16)

    def section_mask():
        arrive("down")
        v.d_branch_v[...] = (mask * v.cot_v[...]).astype(BF16)

    def section_dup(t):
        cols = slice(t * width, (t + 1) * width)
        up = v.up_proj_v[:, cols]
        sigmoid = 1.0 / (1.0 + jnp.exp(-up))
        d_act = dot_nt(v.d_branch_v[...], v.w_down_v[t * width : (t + 1) * width, :])
        v.d_up_v[:, cols] = (d_act * sigmoid * (1.0 + up * (1.0 - sigmoid))).astype(BF16)

    def section_gd(h):
        value = dot_tn(v.activation_v[...], v.d_branch_v[:, h * 256 : (h + 1) * 256]).astype(BF16)
        value = value.reshape(GROUP, 4, 32, 256)
        for k in range(2):
            produce("d", 2 * h + k, lambda start: value[:, start // 128, :, k * 128 : (k + 1) * 128])

    def section_gu(t):
        value = dot_tn(v.hidden2_v[...], v.d_up_v[:, t * width : (t + 1) * width]).astype(BF16)
        produce("u", t, lambda start: value[:, start : start + 128])

    def section_out():
        branch = dot(v.activation_v[:, 0:width], v.w_down_v[0:width, :])
        for t in range(1, tiles):
            branch = branch + dot(v.activation_v[:, t * width : (t + 1) * width], v.w_down_v[t * width : (t + 1) * width, :])
        v.out_v[0] = v.middle_v[...] + mask * branch

    def section_mid():
        d_hidden2 = dot_nt(v.d_up_v[:, 0:width], tile(v.w_up_v, 0))
        for t in range(1, tiles):
            d_hidden2 = d_hidden2 + dot_nt(v.d_up_v[:, t * width : (t + 1) * width], tile(v.w_up_v, t))
        normed2 = v.normed2_v[...]
        v.mod_v[1, :, 0:width] = jnp.sum(d_hidden2 * normed2, axis=0, keepdims=True)
        v.mod_v[1, :, width : 2 * width] = jnp.sum(d_hidden2, axis=0, keepdims=True)
        queue["m1"] = mod_steps(1)
        d_middle = v.cot_v[...] + norm_back(d_hidden2 * (1.0 + scale2), normed2, inv2)
        v.d_middle_v[...] = d_middle
        v.d_attended_v[...] = (mask * d_middle).astype(BF16)
        v.d_mix_v[...] = dot_nt(v.d_attended_v[...], v.w_out_v[...]).astype(BF16)

    def section_go():
        value = dot_tn(v.mix_v[...], v.d_attended_v[...]).astype(BF16)
        produce("o", 0, lambda start: value[:, start : start + 128])

    def section_attn(h):
        cols = slice(h * head, (h + 1) * head)
        attn = v.attn_v[h]
        d_attn = dot_nt(v.v_v[:, cols], v.d_mix_v[:, cols])
        inner = jnp.sum(attn * d_attn, axis=0, keepdims=True)
        d_scores = (attn * (d_attn - inner)).astype(BF16)
        v.d_q_v[:, cols] = (dot_tn(d_scores, v.k_v[:, cols]) * factor).astype(BF16)
        v.d_k_v[:, cols] = (dot(d_scores, v.q_v[:, cols]) * factor).astype(BF16)
        v.d_v_v[:, cols] = dot(attn.astype(BF16), v.d_mix_v[:, cols]).astype(BF16)

    def section_gq(h):
        cols = slice(h * head, (h + 1) * head)
        values = [
            dot_tn(v.table_v[0:nodes, :], v.d_q_v[:, cols]).astype(BF16),
            dot_tn(v.table_v[...], v.d_k_v[:, cols]).astype(BF16),
            dot_tn(v.table_v[...], v.d_v_v[:, cols]).astype(BF16),
        ]
        produce("h", h, lambda start: values[start // 128])

    back = []

    def section_table():
        d_table = dot_nt(v.d_k_v[...], tile(v.w_qkv_v, 1)) + dot_nt(v.d_v_v[...], tile(v.w_qkv_v, 2))
        v.lend_back_v[...] = d_table[nodes:table, :].astype(BF16)
        back.append(send("back", v.lend_back_v.at[0:half], v.returned_v.at[half:lent], before, 2))
        back.append(send("back", v.lend_back_v.at[half:lent], v.returned_v.at[0:half], after, 3))
        d_hidden1 = d_table[0:nodes, :] + dot_nt(v.d_q_v[...], tile(v.w_qkv_v, 0))
        v.d_hidden1_v[...] = d_hidden1
        d_lent = d_table[nodes:table, :]
        v.mod_v[0, :, 0:width] = jnp.sum(d_hidden1 * v.normed1_v[...], axis=0, keepdims=True) + jnp.sum(
            d_lent * v.halo_v[...].astype(F32), axis=0, keepdims=True
        )
        v.mod_v[0, :, width : 2 * width] = jnp.sum(d_hidden1, axis=0, keepdims=True) + jnp.sum(
            d_lent, axis=0, keepdims=True
        )
        queue["m0"] = mod_steps(0)

    def section_state():
        for copy in back:
            copy.arrive()
        d_hidden1 = v.d_hidden1_v[...] + dot(pick, v.returned_v[...])
        normed1 = v.normed1_v[...]
        v.d_states_v[0] = v.d_middle_v[...] + norm_back(d_hidden1 * (1.0 + scale1), normed1, inv1)

    def mod_steps(part):
        own, from_core, plane, rows = v.mod_v.at[part], v.mod_core_v.at[part], v.mods_v.at[part], v.rows_v.at[part]
        name = "m%d" % part
        copies = [send(name, own, from_core, core_peer, "core")]

        def spread():
            copies.pop().arrive()
            plane[0] = own[...] + from_core[...]
            for d in range(1, 8):
                there = lax.rem(z + d // 2, 4)
                target = z_peer(there) if d % 2 == 0 else z_x_peer(there)
                send(name, plane.at[0], plane.at[d], target, "plane")
            copies.append(message(name, plane.at[pl.ds(1, 7)], plane.at[pl.ds(1, 7)], x_peer, "plane"))

        def swap():
            copies.pop().arrive()
            total = jnp.zeros(own.shape, F32)
            for there in range(4):
                for side in range(2):
                    total = total + plane[lax.rem(z + 4 - there, 4) * 2 + lax.rem(x + side, 2)]
            rows[r] = total
            copies.append(send(name, rows.at[r], rows.at[r], y_peer, "y"))

        def spend():
            copies.pop().arrive()
            first_row, second_row = rows[0], rows[1]
            here = slice(part * 2 * width, (part + 1) * 2 * width)
            if not finish:
                v.d_noise_v[0:1, here] = first_row
                v.d_noise_v[1:2, here] = second_row
                return
            row = lax.broadcasted_iota(jnp.int32, (16, 2 * width), 0)
            stacked = jnp.zeros((16, 2 * width), F32)
            for number, piece in enumerate(split3(first_row) + split3(second_row)):
                stacked = jnp.where(row == number, piece, stacked)
            noise = dot_nt(stacked.astype(BF16), v.w_cond_v[part])
            first_noise = jnp.sum(noise[0:3], axis=0, keepdims=True)
            second_noise = jnp.sum(noise[3:6], axis=0, keepdims=True)
            if part == 1:
                v.noise_part_v[0:1, :] = first_noise
                v.noise_part_v[1:2, :] = second_noise
            else:
                v.d_noise_v[0:1, :] = first_noise + v.noise_part_v[0:1, :]
                v.d_noise_v[1:2, :] = second_noise + v.noise_part_v[1:2, :]
            shape = (v.d_cond_v.shape[0], width)
            mine = lax.broadcasted_iota(jnp.int32, shape, 1) == (
                lax.broadcasted_iota(jnp.int32, shape, 0) + p * shape[0]
            )
            picked = [
                jnp.sum(jnp.where(mine, v.noise_v[b : b + 1, :], 0.0), axis=1, keepdims=True)
                for b in range(2)
            ]
            v.d_cond_v[:, here] = picked[0] * first_row + picked[1] * second_row

        return [spread, swap, spend]

    sections = {
        "up": section_up,
        "mask": section_mask,
        "dup": section_dup,
        "gd": section_gd,
        "gu": section_gu,
        "out": section_out,
        "mid": section_mid,
        "go": section_go,
        "attn": section_attn,
        "gq": section_gq,
        "table": section_table,
        "state": section_state,
    }
    for entry in ORDER:
        if entry in queue:
            queue[entry].pop(0)()
        elif isinstance(entry, tuple):
            sections[entry[0]](entry[1])
        else:
            sections[entry]()
    for steps in queue.values():
        for step in steps:
            step()

    for n in range(len(UNITS)):
        all_left(n, getattr(v, "u%d_grad" % n))
    for part in range(2):
        all_left("m%d" % part, v.mods_v.at[part])
    all_left("halo", v.lend_v)
    all_left("back", v.lend_back_v)


def copy_out(count, *refs):
    for n in range(count):
        src, dst = refs[n], refs[count + n]
        rows = src.shape[-2]
        pieces = 4 if rows % 64 == 0 else 1
        for k in range(pieces):
            at = (*[slice(None)] * (len(src.shape) - 2), slice(k * rows // pieces, (k + 1) * rows // pieces))
            pltpu.make_async_copy(src.at[at], dst.at[at], refs[-1].at[n]).start()
    for n in range(count):
        pltpu.make_async_copy(refs[n], refs[count + n], refs[-1].at[n]).wait()


def body(
    node_state,
    noise_embed,
    w_cond,
    w_qkv,
    w_out,
    w_up,
    w_down,
    neighbours,
    send_rows,
    valid,
    cotangent,
):
    nodes, width = node_state.shape[1:]
    hidden = w_up.shape[1]
    lent = send_rows.shape[0]
    table = nodes + lent
    patches = lax.axis_size("patch")
    fold = patches // GROUP
    rows_each = width // patches
    block = width // GROUP
    half = width // 2

    hbm = pl.BlockSpec(memory_space=pl.ANY)
    vmem = pl.BlockSpec(memory_space=pltpu.VMEM)
    inputs = [
        ("states_hbm", node_state, hbm),
        ("noise_hbm", noise_embed, hbm),
        ("w_cond_hbm", w_cond, hbm),
        ("w_qkv_hbm", w_qkv, hbm),
        ("w_out_hbm", w_out, hbm),
        ("w_up_hbm", w_up, hbm),
        ("w_down_hbm", w_down, hbm),
        ("neighbours_hbm", neighbours.T, hbm),
        ("send_hbm", send_rows[None, :], hbm),
        ("valid_hbm", valid[None, :], hbm),
        ("cot_hbm", cotangent, hbm),
    ]
    outputs = [
        ("out_v", node_state.shape, vmem),
        ("d_states_v", node_state.shape, vmem),
        ("down_v", (hidden // GROUP, width), vmem),
        ("up_v", (block, hidden), vmem),
        ("o_v", (block, width), vmem),
        ("qkv_v", (block, 3 * width), vmem),
    ]
    if fold == 1:
        outputs += [("d_noise_v", noise_embed.shape, vmem), ("d_cond_v", (rows_each, 4 * width), vmem)]
    else:
        outputs += [("d_noise_v", (noise_embed.shape[0], 4 * width), vmem)]
    tiles = hidden // width
    receivers = receive_plan()[1]
    scratch = [
        ("noise_v", noise_embed.shape, F32),
        ("neighbours_v", neighbours.shape[::-1], jnp.int32),
        ("pick_v", (1, lent), jnp.int32),
        ("valid_v", (1, nodes), jnp.int32),
        ("states_v", (nodes, width), F32),
        ("cot_v", (nodes, width), F32),
        ("w_cond_v", (2, width, 2 * width), BF16),
        ("w_qkv_v", w_qkv.shape, BF16),
        ("w_out_v", (width, width), BF16),
        ("w_up_v", w_up.shape, BF16),
        ("w_down_v", w_down.shape, BF16),
        ("normed1_v", (nodes, width), F32),
        ("table_v", (table, width), BF16),
        ("lend_v", (lent, width), BF16),
        ("halo_v", (lent, width), BF16),
        ("returned_v", (lent, width), BF16),
        ("q_v", (nodes, width), BF16),
        ("k_v", (table, width), BF16),
        ("v_v", (table, width), BF16),
        ("count_v", (table, nodes), BF16),
        ("attn_v", (HEADS, table, nodes), F32),
        ("mix_v", (nodes, width), BF16),
        ("middle_v", (nodes, width), F32),
        ("normed2_v", (nodes, width), F32),
        ("hidden2_v", (nodes, width), BF16),
        ("d_branch_v", (nodes, width), BF16),
        ("d_mix_v", (nodes, width), BF16),
        ("d_q_v", (nodes, width), BF16),
        ("d_k_v", (table, width), BF16),
        ("d_v_v", (table, width), BF16),
        ("mod_v", (2, 1, 2 * width), F32),
        ("mod_core_v", (2, 1, 2 * width), F32),
        ("mods_v", (2, 9, 1, 2 * width), F32),
        ("rows_v", (2, 2, 1, 2 * width), F32),
        ("noise_part_v", noise_embed.shape, F32),
        ("up_proj_v", (nodes, hidden), F32),
        ("activation_v", (nodes, hidden), BF16),
        ("d_up_v", (nodes, hidden), BF16),
        ("d_middle_v", (nodes, width), F32),
        ("d_attended_v", (nodes, width), BF16),
        ("d_hidden1_v", (nodes, width), F32),
        ("lend_back_v", (lent, width), BF16),
    ]
    for n, (_, _, _, wide, flow) in enumerate(UNITS):
        name = "u%d" % n
        rows = 16 if flow[0] == "C" else 32
        part = (2, 32, wide) if flow[0] == "B" else (rows, wide)
        buffers = [("_grad", (4, 2, 2, 32, wide)), ("_core", (4, 2, 32, wide))]
        buffers += [("_mine", (4, 2, 2, 16, wide) if flow[0] == "C" else (4, 2, 32, wide))]
        buffers += [("_result", (rows, wide)), ("_received", (rows, wide))]
        if flow[0] == "G":
            buffers += [("_plane", (7, rows, wide))]
        else:
            buffers += [("_x", (rows, wide) if flow[0] == "B" else (4, rows, wide))]
            if flow[0] == "C":
                buffers += [("_y", (4, 2, 16, wide))]
            if flow[0] == "B":
                buffers += [("_pair", part)]
            if flow[1:] == "d":
                buffers += [("_landing", (3, *part))]
            else:
                buffers += [("_triple", (3, *part)), ("_single", part), ("_middle", part), ("_comb", (2, *part))]
        scratch += [(name + suffix, shape, BF16) for suffix, shape in buffers]
    semaphores = [
        ("load_sem", pltpu.SemaphoreType.DMA((12,))),
        ("send_sem", pltpu.SemaphoreType.DMA((len(UNITS) + 4,))),
        ("recv_sem", pltpu.SemaphoreType.DMA((receivers,))),
    ]
    names = [n for group in (inputs, outputs, scratch, semaphores) for n in [e[0] for e in group]]
    results = pl.pallas_call(
        functools.partial(kernel, fold, patches, names),
        out_shape=[pltpu.VMEM(shape, F32) for _, shape, _ in outputs],
        in_specs=[spec for _, _, spec in inputs],
        out_specs=[spec for _, _, spec in outputs],
        scratch_shapes=[pltpu.VMEM(shape, dtype) for _, shape, dtype in scratch]
        + [sem for _, sem in semaphores],
        compiler_params=pltpu.CompilerParams(
            collective_id=0, has_side_effects=True, vmem_limit_bytes=44 * 1024 * 1024
        ),
    )(
        *[pltpu.with_memory_space_constraint(array, pltpu.HBM) for _, array, _ in inputs]
    )
    if fold == 1:
        results = pl.pallas_call(
            functools.partial(copy_out, len(results)),
            out_shape=[jax.ShapeDtypeStruct(a.shape, a.dtype) for a in results],
            in_specs=[hbm] * len(results),
            out_specs=[hbm] * len(results),
            scratch_shapes=[pltpu.SemaphoreType.DMA((len(results),))],
            compiler_params=pltpu.CompilerParams(vmem_limit_bytes=1024 * 1024),
        )(*results)
    output, d_state, g_down, g_up, g_out, g_qkv = results[:6]
    if fold == 1:
        grad_noise, grad_cond = results[6:]
    else:
        groups = [[m * fold + i for i in range(fold)] for m in range(GROUP)]

        def rest(array):
            return lax.psum_scatter(
                array, "patch", scatter_dimension=0, axis_index_groups=groups, tiled=True
            )

        g_down, g_up, g_out, g_qkv = rest(g_down), rest(g_up), rest(g_out), rest(g_qkv)
        mods = lax.psum(results[6], "patch") / GROUP
        highest = lax.Precision.HIGHEST
        grad_noise = jnp.dot(mods, w_cond.astype(F32).T, precision=highest)
        first_row = lax.axis_index("patch") * rows_each
        cond_cols = lax.dynamic_slice_in_dim(noise_embed, first_row, rows_each, 1)
        grad_cond = jnp.dot(cond_cols.T, mods, precision=highest)
    return output, d_state, grad_noise, grad_cond, g_qkv, g_out, g_up, g_down


def solution(mesh):
    in_specs = (
        P("rep", "patch", None),
        P(),
        P(),
        P(),
        P(),
        P(),
        P(),
        P("patch", None),
        P("patch"),
        P("patch"),
        P("rep", "patch", None),
    )
    out_specs = (
        P("rep", "patch", None),
        P("rep", "patch", None),
        P(),
        P("patch", None),
        P("patch", None),
        P("patch", None),
        P("patch", None),
        P("patch", None),
    )
    return jax.shard_map(body, mesh=mesh, in_specs=in_specs, out_specs=out_specs, check_vma=False)
```
